32 devices in a mesh: seq: 16 (over z, y, x), col: 2 (over core).
Axes of the slice: x: 2, y: 2, z: 4, core: 2. Of those that a mesh axis runs over, the one named last changes fastest.
Arguments:
- hidden: bfloat16 [4, 96, 2304], P(None, None, 'seq'), may hold values from -6 to 6
- key_cache: bfloat16 [1152, 128, 2048], P('seq', None, 'col'), may hold values from -300 to 300
- value_cache: bfloat16 [1152, 128, 2048], P('seq', None, 'col'), may hold values from -6 to 6
- page_table: int32 [96, 128], replicated, may hold values from 0 to 1151, as said below
- cache_len: int32 [96], replicated, may hold values from 1 to 16380, as said below
- order: int32 [96], replicated, may hold values from 0 to 95, each once
- route_ids: int32 [4, 96, 2], replicated, may hold values from 0 to 7, all different within a row; in each aligned block of 96 rows (0 to 95, 96 to 191, ..., all dimensions but the last counted through in order) at most 48 rows name the same one
- w_qkv: bfloat16 [2304, 3, 2048], P('seq', None, 'col'), may hold values from -0.125 to 0.125
- w_out: bfloat16 [2048, 2304], P('col', 'seq'), may hold values from -0.125 to 0.125
- w_router: bfloat16 [2304, 8], replicated, may hold values from -0.125 to 0.125
- w_gate_up: bfloat16 [8, 2304, 2, 5760], P('col', None, None, 'seq'), may hold values from -0.125 to 0.125
- w_down: bfloat16 [8, 5760, 2304], P('col', 'seq'), may hold values from -0.109375 to 0.109375
Outputs:
- layer_out: bfloat16 [4, 96, 2304], P(None, None, 'seq')
- new_keys: bfloat16 [4, 96, 2048], P(None, None, 'col')
- new_values: bfloat16 [4, 96, 2048], P(None, None, 'col')
The draws below stay inside these ranges and needn't reach their ends.
Inputs may be any that keep to these rules, and one draw needn't show every extreme that they name: `cache_len`: one request's cache holds exactly 16380 tokens; 4 requests hold more than 640 tokens, the others at most 640. `page_table`: for request r the entries 0 to ceil((cache_len[r] + 4) / 128) - 1 name pages that no other such entry names; later entries are never read. `order`: each request sits in exactly one batch slot. `route_ids`: the two experts of a row differ; in each step no expert is named by more than 48 requests.
All inputs are finite; a program needn't handle non-finite values.
Results may differ from the reference program's by a relative error of at most 0.011.
Values may be sent and summed in bfloat16 or wider, within the bound.
A program may use at most 256 MiB of HBM per device.

```python
import math
import jax
import jax.numpy as jnp
import numpy as np
from jax import lax

D = 2304
HEADS = 32
HEAD_DIM = 64
EXPERTS = 8
FF = 5760
PAGE = 128
MAXP = 128
STEPS = 4
REQS = 96
PAGES = 1152
CAP = 48


def layout(key):
    base_key = jax.random.fold_in(key, 7)
    key_long, key_short, key_rank, key_pool, key_filler = jax.random.split(base_key, 5)
    longest = MAXP * PAGE - STEPS
    long_count = max(1, REQS // 24)
    short_len = jax.random.randint(key_short, (REQS,), 1, 5 * PAGE + 1)
    long_len = jax.random.randint(key_long, (REQS,), 5 * PAGE + 1, longest + 1)
    ranking = jax.random.permutation(key_rank, REQS)
    lengths = jnp.where(ranking < long_count, long_len, short_len)
    lengths = jnp.where(ranking == 0, longest, lengths)
    needed = (lengths + STEPS + PAGE - 1) // PAGE
    offsets = jnp.cumsum(needed) - needed
    page_pool = jax.random.permutation(key_pool, PAGES)
    columns = jnp.arange(MAXP)
    spots = jnp.minimum(offsets[:, None] + columns[None, :], PAGES - 1)
    filler = jax.random.randint(key_filler, (REQS, MAXP), 0, PAGES)
    table = jnp.where(columns[None, :] < needed[:, None], page_pool[spots], filler)
    return (lengths.astype(jnp.int32), table.astype(jnp.int32))


def draw_cache_len(key, part):
    return layout(key)[0]


def draw_page_table(key, part):
    return layout(key)[1]


def draw_key_cache(key, part):
    key_base = jax.random.fold_in(jax.random.fold_in(key, 11), 0)
    shape = (PAGES, PAGE, HEADS * HEAD_DIM)
    return jax.random.normal(key_base, shape, jnp.float32).astype(jnp.bfloat16)


def spiked(entries, key, source, target, shards_of, factor):
    owner, partner = [(jnp.arange(entries.shape[dim]) // (entries.shape[dim] // shards_of)).reshape([-1 if axis == dim else 1 for axis in range(entries.ndim)]) for dim in (source, target)]
    chosen = jax.random.permutation(key, shards_of)[partner]
    strong = (owner == chosen) | (owner == (partner + shards_of // 2) % shards_of)
    return jnp.where(strong, factor * entries, entries)


def level_of(key, dims, cuts, least, top_value):
    def one(axis_at, shards_of):
        heights = jax.random.uniform(jax.random.fold_in(jax.random.fold_in(key, 6), axis_at), (shards_of,), jnp.float32, least / len(cuts), top_value / len(cuts))
        return jnp.repeat(jnp.exp(heights), dims[axis_at] // shards_of).reshape((-1,) + (1,) * (len(dims) - axis_at - 1))

    factor_of = one(*cuts[0])
    for cut in cuts[1:]:
        factor_of = factor_of * one(*cut)
    return factor_of


def shared_out(stream_key, own, number, rows, amount, top, reach, skew):
    order = jax.random.permutation(stream_key, amount)
    crowded, usual = shares(amount, rows * top, reach, skew, True), shares(amount, rows * top, reach, skew, False)
    places = jnp.arange(amount)

    def named(tallies, turn):
        used = int((tallies > 0).sum())
        fixed = max(1, used // 4)
        passed = fixed + (places - fixed + turn * (used - fixed)) % max(1, amount - fixed)
        return jnp.zeros((amount,), jnp.int32).at[order[jnp.where(places < fixed, places, passed)]].set(jnp.asarray(tallies, jnp.int32))

    tallies = jnp.where(number % 4 == 0, named(crowded, number // 4), named(usual, number - number // 4 - 1))
    mixed = jax.random.permutation(jax.random.fold_in(own, 3), amount)
    giver, taker = mixed[0:amount // 2 * 2:2], mixed[1:amount // 2 * 2:2]
    slack = jnp.minimum(tallies[giver] - 1, reach - tallies[taker]) // 2
    slack = jnp.where((giver == order[0]) | (taker == order[0]) | (tallies[taker] == 0), 0, jnp.maximum(slack, 0))
    passed = jax.random.randint(jax.random.fold_in(own, 4), (amount // 2,), 0, 1 << 20) % (slack + 1)
    tallies = tallies.at[giver].add(-passed).at[taker].add(passed)
    labels = jnp.searchsorted(jnp.cumsum(tallies), jnp.arange(rows * top), side="right").astype(jnp.int32)
    grid = labels.reshape(top, rows).T
    grid = grid[jax.random.permutation(jax.random.fold_in(own, 1), rows)]
    turn = jax.random.randint(jax.random.fold_in(own, 2), (rows, 1), 0, top)
    return jnp.take_along_axis(grid, (jnp.arange(top)[None, :] + turn) % top, axis=1)


def shares(number_of, total, limit, slope, full):
    weights = [(1 << 20) // math.isqrt(grade ** slope) + 1 for grade in range(1, number_of + 1)]
    largest = limit if full else min(limit, max(-(-total // number_of), total * weights[0] // sum(weights)))
    least = 1 if total - largest >= number_of - 1 else 0
    given, spare = [largest] + [least] * (number_of - 1), total - largest - least * (number_of - 1)
    while spare > 0:
        movable = [i for i in range(1, number_of) if given[i] < largest] or [i for i in range(1, number_of) if given[i] < limit]
        pool, left = sum([weights[i] for i in movable]), spare
        for i in movable:
            more = min(limit - given[i], max(1, left * weights[i] // pool), spare)
            given[i] = given[i] + more
            spare = spare - more
    return np.array(given)


def noise(key, dims, deviation, bound, shards=(), kind=jnp.bfloat16):
    loudness = level_of(key, dims, shards, -0.22, 0.18) if shards else 1.0
    result = jax.random.normal(key, dims, jnp.float32) * deviation * loudness
    return jnp.minimum(jnp.maximum(result, -bound), bound).astype(kind)


def heavy_noise(rng, dims, width, limit, pieces, heavy, kind=jnp.bfloat16):
    result = width * jax.random.normal(rng, dims, jnp.float32)
    if pieces:
        result = result * level_of(rng, dims, pieces, -0.22, 0.18)
    return jnp.clip(spiked(result, jax.random.fold_in(rng, 3), *heavy), -limit, limit).astype(kind)


def setup_inputs(seed: int = 0) -> dict:
    splits = jax.random.split(jax.random.key(seed), 13)
    hidden = noise(splits[0], (STEPS, REQS, D), 1.0, 6.0, ((2, 16),))
    key_cache = draw_key_cache(jax.random.fold_in(splits[12], 71), 0)
    value_cache = noise(splits[2], (PAGES, PAGE, HEADS * HEAD_DIM), 1.0, 6.0, ((0, 16), (2, 2)))
    page_table = draw_page_table(jax.random.fold_in(splits[12], 71), 0)
    cache_len = draw_cache_len(jax.random.fold_in(splits[12], 71), 0)
    order = jax.random.permutation(splits[5], REQS).astype(jnp.int32)
    route_ids_keys = jax.random.split(jax.random.fold_in(splits[6], 1), STEPS * REQS // REQS)
    route_ids_turns = jax.random.permutation(jax.random.fold_in(splits[6], 3), STEPS * REQS // REQS)
    route_ids = jax.vmap(lambda own, number: shared_out(jax.random.fold_in(splits[6], 2), own, number, REQS, EXPERTS, 2, CAP, 2))(route_ids_keys, route_ids_turns).reshape((STEPS, REQS, 2))
    w_qkv = noise(splits[7], (D, 3, HEADS * HEAD_DIM), D ** -0.5, 0.125, ((0, 16), (2, 2)))
    w_out = noise(splits[8], (HEADS * HEAD_DIM, D), (HEADS * HEAD_DIM) ** -0.5, 0.125, ((0, 2), (1, 16)))
    w_router = noise(splits[9], (D, EXPERTS), D ** -0.5, 0.125)
    w_gate_up = noise(splits[10], (EXPERTS, D, 2, FF), D ** -0.5, 0.125, ((0, 2), (3, 16)))
    w_down = heavy_noise(splits[11], (EXPERTS, FF, D), FF ** -0.5, 0.109375, ((0, 2), (1, 16)), (1, 2, 16, 2.0))
    return dict(hidden=hidden, key_cache=key_cache, value_cache=value_cache, page_table=page_table, cache_len=cache_len, order=order, route_ids=route_ids, w_qkv=w_qkv, w_out=w_out, w_router=w_router, w_gate_up=w_gate_up, w_down=w_down)


EPSILON = 1e-05

def rotate(row_data, positions, head_dim):
    head_count = row_data.shape[1] // head_dim
    half_dim = head_dim // 2
    frequency = jnp.exp(-jnp.log(10000.0) * 2.0 * jnp.arange(half_dim, dtype=jnp.float32) / head_dim)
    angles = positions.astype(jnp.float32)[:, None] * frequency[None, :]
    cosine = jnp.cos(angles)[:, None, :]
    sines = jnp.sin(angles)[:, None, :]
    by_head = row_data.reshape(row_data.shape[0], head_count, head_dim)
    front_half = by_head[:, :, :half_dim]
    back_half = by_head[:, :, half_dim:]
    turned = jnp.concatenate([front_half * cosine - back_half * sines, back_half * cosine + front_half * sines], axis=2)
    return turned.reshape(row_data.shape)

def reference(hidden, key_cache, value_cache, page_table, cache_len, order, route_ids, w_qkv, w_out, w_router, w_gate_up, w_down):
    columns = HEADS * HEAD_DIM
    span = MAXP * PAGE
    w_proj = w_qkv.reshape(D, 3 * columns)
    new_keys = jnp.zeros((STEPS, REQS, columns), jnp.bfloat16)
    new_values = jnp.zeros((STEPS, REQS, columns), jnp.bfloat16)
    expert_ids = jnp.arange(EXPERTS)
    layers = []
    for moment in range(STEPS):
        inputs = jnp.zeros((REQS, D), jnp.bfloat16).at[order].set(hidden[moment])
        wide_in = inputs.astype(jnp.float32)
        inv_one = lax.rsqrt(lax.optimization_barrier(jnp.mean(wide_in * wide_in, axis=1)) + EPSILON)
        proj = jnp.dot(inputs, w_proj, preferred_element_type=jnp.float32) * inv_one[:, None]
        positions = cache_len + moment
        query = rotate(proj[:, :columns], positions, HEAD_DIM).astype(jnp.bfloat16)
        new_keys = new_keys.at[moment].set(rotate(proj[:, columns:2 * columns], positions, HEAD_DIM).astype(jnp.bfloat16))
        new_values = new_values.at[moment].set(proj[:, 2 * columns:].astype(jnp.bfloat16))
        fresh_keys = jnp.transpose(new_keys, (1, 0, 2))
        fresh_values = jnp.transpose(new_values, (1, 0, 2))

        def attend_one(request_args):
            query_row, table_row, length, key_new, value_new = request_args
            key_rows = jnp.concatenate([key_cache[table_row].reshape(span, columns), key_new], axis=0)
            value_rows = jnp.concatenate([value_cache[table_row].reshape(span, columns), value_new], axis=0)
            position_ids = jnp.arange(span + STEPS)
            visible = jnp.where(position_ids < span, position_ids < length, position_ids - span <= moment)
            scores = jnp.einsum('hd,khd->hk', query_row.reshape(HEADS, HEAD_DIM).astype(jnp.float32), key_rows.reshape(span + STEPS, HEADS, HEAD_DIM).astype(jnp.float32), precision=lax.Precision.HIGHEST) * HEAD_DIM ** (-0.5)
            scores = jnp.where(visible[None, :], scores, -jnp.inf)
            top_score = lax.optimization_barrier(jnp.max(scores, axis=1, keepdims=True))
            weight = jnp.where(visible[None, :], jnp.exp(scores - top_score), 0.0)
            lowered = lax.optimization_barrier(weight.astype(jnp.bfloat16)).astype(jnp.float32)
            summed = jnp.einsum('hk,khd->hd', lowered, value_rows.reshape(span + STEPS, HEADS, HEAD_DIM).astype(jnp.float32), precision=lax.Precision.HIGHEST)
            return (summed / lax.optimization_barrier(jnp.sum(weight, axis=1, keepdims=True))).reshape(columns).astype(jnp.bfloat16)
        attention = lax.map(attend_one, (query, page_table, cache_len, fresh_keys, fresh_values))
        mid = (wide_in + jnp.dot(attention, w_out, preferred_element_type=jnp.float32)).astype(jnp.bfloat16)
        wide_mid = mid.astype(jnp.float32)
        inv_two = lax.rsqrt(lax.optimization_barrier(jnp.mean(wide_mid * wide_mid, axis=1)) + EPSILON)
        logits = jnp.dot(mid, w_router, preferred_element_type=jnp.float32) * inv_two[:, None]
        chosen = route_ids[moment]
        first_pick = chosen[:, 0:1] == expert_ids[None, :]
        second_pick = chosen[:, 1:2] == expert_ids[None, :]
        first_share = jax.nn.sigmoid(lax.optimization_barrier(jnp.sum(jnp.where(first_pick, logits, 0.0), axis=1)) - lax.optimization_barrier(jnp.sum(jnp.where(second_pick, logits, 0.0), axis=1)))
        gate_rows = jnp.where(first_pick, first_share[:, None], 0.0) + jnp.where(second_pick, 1.0 - first_share[:, None], 0.0)
        mixture = wide_mid
        for expert in range(EXPERTS):
            pair_sum = jnp.dot(mid, w_gate_up[expert].reshape(D, 2 * FF), preferred_element_type=jnp.float32) * inv_two[:, None]
            active = (jax.nn.silu(pair_sum[:, :FF]) * pair_sum[:, FF:]).astype(jnp.bfloat16)
            mixture = mixture + gate_rows[:, expert:expert + 1] * jnp.dot(active, w_down[expert], preferred_element_type=jnp.float32)
        layers.append(mixture.astype(jnp.bfloat16))
    return (jnp.stack(layers), new_keys, new_values)
```

```python
import functools

import jax
import jax.numpy as jnp
from jax import lax
from jax.experimental import pallas as pl
from jax.experimental.pallas import tpu as pltpu
from jax.sharding import PartitionSpec as P

HEAD_DIM = 64
EPSILON = 1e-05
LOWEST = -1e30
GROUP = 4
MIB = 1024 * 1024


def rotate(row_data, positions, head_dim):
    head_count = row_data.shape[1] // head_dim
    half_dim = head_dim // 2
    frequency = jnp.exp(
        -jnp.log(10000.0) * 2.0 * jnp.arange(half_dim, dtype=jnp.float32) / head_dim
    )
    angles = positions.astype(jnp.float32)[:, None] * frequency[None, :]
    cosine = jnp.cos(angles)[:, None, :]
    sines = jnp.sin(angles)[:, None, :]
    by_head = row_data.reshape(row_data.shape[0], head_count, head_dim)
    front_half = by_head[:, :, :half_dim]
    back_half = by_head[:, :, half_dim:]
    turned = jnp.concatenate(
        [front_half * cosine - back_half * sines, back_half * cosine + front_half * sines], axis=2
    )
    return turned.reshape(row_data.shape)


def page_kernel(owner_ref, count_ref, q_ref, k_ref, v_ref, sum_ref, peak_ref, total_ref):
    page = pl.program_id(0)
    steps, cols = q_ref.shape[1], q_ref.shape[2]
    size = k_ref.shape[1]
    padded = peak_ref.shape[2] // steps
    count = count_ref[page]
    wide = q_ref[0].astype(jnp.float32)
    own = lax.broadcasted_iota(jnp.int32, (padded, cols), 1) // HEAD_DIM == lax.broadcasted_iota(
        jnp.int32, (padded, cols), 0
    )
    spread = jnp.concatenate(
        [jnp.where(own, wide[n : n + 1, :], 0.0) for n in range(steps)], axis=0
    ).astype(jnp.bfloat16)
    scores = lax.dot_general(
        k_ref[0], spread, (((1,), (1,)), ((), ())), preferred_element_type=jnp.float32
    ) * (HEAD_DIM ** (-0.5))
    live = lax.broadcasted_iota(jnp.int32, (size, steps * padded), 0) < count
    scores = jnp.where(live, scores, LOWEST)
    peak = jnp.max(scores, axis=0, keepdims=True)
    weights = jnp.where(live, jnp.exp(scores - peak), 0.0)
    peak_ref[0] = peak
    total_ref[0] = jnp.sum(weights, axis=0, keepdims=True)
    mixed = lax.dot_general(
        weights.astype(jnp.bfloat16),
        v_ref[0],
        (((0,), (0,)), ((), ())),
        preferred_element_type=jnp.float32,
    )
    for n in range(steps):
        part = jnp.where(own, mixed[n * padded : (n + 1) * padded, :], 0.0)
        sum_ref[0, n : n + 1, :] = jnp.sum(part, axis=0, keepdims=True)


def page_parts(owner, count, query, keys, values):
    pages, size, cols = keys.shape
    steps = query.shape[1]
    heads = cols // HEAD_DIM
    padded = -(-heads // 8) * 8
    sums, peak, total = pl.pallas_call(
        page_kernel,
        grid_spec=pltpu.PrefetchScalarGridSpec(
            num_scalar_prefetch=2,
            grid=(pages,),
            in_specs=[
                pl.BlockSpec((1, steps, cols), lambda p, o, c: (o[p], 0, 0)),
                pl.BlockSpec((1, size, cols), lambda p, o, c: (p, 0, 0)),
                pl.BlockSpec((1, size, cols), lambda p, o, c: (p, 0, 0)),
            ],
            out_specs=[
                pl.BlockSpec((1, steps, cols), lambda p, o, c: (p, 0, 0)),
                pl.BlockSpec((1, 1, steps * padded), lambda p, o, c: (p, 0, 0)),
                pl.BlockSpec((1, 1, steps * padded), lambda p, o, c: (p, 0, 0)),
            ],
        ),
        out_shape=(
            jax.ShapeDtypeStruct((pages, steps, cols), jnp.float32),
            jax.ShapeDtypeStruct((pages, 1, steps * padded), jnp.float32),
            jax.ShapeDtypeStruct((pages, 1, steps * padded), jnp.float32),
        ),
        cost_estimate=pl.CostEstimate(
            flops=4 * pages * steps * padded * size * cols,
            bytes_accessed=4 * pages * size * cols,
            transcendentals=pages * steps * padded * size,
        ),
    )(owner, count, query, keys, values)
    peak = peak.reshape(pages, steps, padded)[:, :, :heads]
    total = total.reshape(pages, steps, padded)[:, :, :heads]
    return sums, peak, total


def pieces(value, count):
    out = []
    for _ in range(count):
        part = lax.reduce_precision(value, 8, 7)
        out.append(part.astype(jnp.bfloat16))
        value = value - part
    return out


def exchange(blocks):
    return lax.all_to_all(blocks, "seq", split_axis=0, concat_axis=0, tiled=True)


def col_scatter(rows):
    if lax.axis_size("col") == 2:
        half = rows.shape[0] // 2
        me = lax.axis_index("col")
        mine = lax.dynamic_slice_in_dim(rows, me * half, half, 0)
        theirs = lax.dynamic_slice_in_dim(rows, (1 - me) * half, half, 0)
        return mine + lax.ppermute(theirs, "col", [(0, 1), (1, 0)])
    return lax.psum_scatter(rows, "col", scatter_dimension=0, tiled=True)


def col_gather(rows):
    if lax.axis_size("col") == 2:
        me = lax.axis_index("col")
        other = lax.ppermute(rows, "col", [(0, 1), (1, 0)])
        first = jnp.where(me == 0, rows, other)
        second = jnp.where(me == 0, other, rows)
        return jnp.concatenate([first, second], axis=0)
    return lax.all_gather(rows, "col", axis=0, tiled=True)


def local(
    hidden,
    key_cache,
    value_cache,
    page_table,
    cache_len,
    order,
    route_ids,
    w_qkv,
    w_out,
    w_router,
    w_gate_up,
    w_down,
):
    steps, requests, width_loc = hidden.shape
    pages_loc, page_size, cols = key_cache.shape
    heads = cols // HEAD_DIM
    shards = lax.axis_size("seq")
    width_all = width_loc * shards
    experts_loc = w_gate_up.shape[0]
    ff_loc = w_gate_up.shape[3]
    expert_count = w_router.shape[1]
    expert_base = lax.axis_index("col") * experts_loc
    seq_index = lax.axis_index("seq")
    share = -(-requests // shards)
    filler = share * shards - requests
    row_count = steps * requests
    own_rows = share * steps

    placing = (order[:, None] == jnp.arange(requests)[None, :]).astype(jnp.bfloat16)
    inputs = jnp.einsum("nsc,sr->rnc", hidden, placing, preferred_element_type=jnp.float32).astype(
        jnp.bfloat16
    )
    flat_in = inputs.reshape(row_count, width_loc)
    wide_in = flat_in.astype(jnp.float32)
    squares = jnp.sum(wide_in * wide_in, axis=1, keepdims=True)
    partial = jnp.dot(
        flat_in, w_qkv.reshape(width_loc, 3 * cols), preferred_element_type=jnp.float32
    ).astype(jnp.bfloat16)
    tail = jnp.pad(jnp.concatenate(pieces(squares, 3), axis=1), ((0, 0), (0, 125)))
    sent = jnp.pad(jnp.concatenate([partial, tail], axis=1), ((0, filler * steps), (0, 0)))
    sent = sent.reshape(shards, own_rows, 3 * cols + 128)
    got = jnp.sum(exchange(sent).astype(jnp.float32), axis=0)
    inv_one = lax.rsqrt(jnp.sum(got[:, 3 * cols :], axis=1) / width_all + EPSILON)
    proj = got[:, : 3 * cols] * inv_one[:, None]
    own_len = lax.dynamic_slice_in_dim(jnp.pad(cache_len, (0, filler)), seq_index * share, share, 0)
    positions = (own_len[:, None] + jnp.arange(steps)[None, :]).reshape(own_rows)
    query = rotate(proj[:, :cols], positions, HEAD_DIM).astype(jnp.bfloat16)
    fresh_key = rotate(proj[:, cols : 2 * cols], positions, HEAD_DIM).astype(jnp.bfloat16)
    fresh_value = proj[:, 2 * cols :].astype(jnp.bfloat16)
    all_query = lax.all_gather(query, "seq", axis=0, tiled=True)[:row_count]
    all_query, fresh_pair = lax.optimization_barrier(
        (all_query, jnp.concatenate([fresh_key, fresh_value], axis=1))
    )
    all_pair = lax.all_gather(fresh_pair, "seq", axis=0, tiled=True)[:row_count]
    all_pair = all_pair.reshape(requests, steps, 2 * cols).transpose(1, 0, 2)

    needed = (cache_len + steps + page_size - 1) // page_size
    columns = jnp.arange(page_table.shape[1])
    in_use = columns[None, :] < needed[:, None]
    local_pages = page_table - seq_index * pages_loc
    page_hits = in_use[:, :, None] & (
        local_pages[:, :, None] == jnp.arange(pages_loc)[None, None, :]
    )
    owned_by = jnp.any(page_hits, axis=1)
    page_starts = jnp.sum(jnp.where(page_hits, columns[None, :, None] * page_size, 0), axis=(0, 1))
    page_len = jnp.sum(jnp.where(owned_by, cache_len[:, None], 0), axis=0)
    owner = jnp.sum(jnp.where(owned_by, jnp.arange(requests)[:, None], 0), axis=0)
    count = page_len - page_starts
    page_sums, page_peak, page_total = page_parts(
        owner.astype(jnp.int32),
        count.astype(jnp.int32),
        all_query.reshape(requests, steps, cols),
        key_cache,
        value_cache,
    )
    mask = owned_by[:, :, None, None]
    req_peak = jnp.max(jnp.where(mask, page_peak[None], LOWEST), axis=1)
    back_peak = jnp.max(jnp.where(mask, req_peak[:, None], LOWEST), axis=0)
    factor = jnp.exp(page_peak - back_peak)
    factor = jnp.where((count > 0)[:, None, None] & jnp.any(owned_by, axis=0)[:, None, None], factor, 0.0)
    owner_float = owned_by.astype(jnp.float32)
    req_total = jnp.einsum(
        "rp,pnh->rnh", owner_float, page_total * factor, precision=lax.Precision.HIGHEST
    )
    scaled = page_sums * jnp.repeat(factor, HEAD_DIM, axis=2)
    req_sums = jnp.einsum("rp,pnc->rnc", owner_float, scaled, precision=lax.Precision.HIGHEST)
    extra = jnp.concatenate(pieces(req_peak, 3) + pieces(req_total, 3), axis=2)
    spare = -extra.shape[2] % 128
    extra = jnp.pad(extra, ((0, 0), (0, 0), (0, spare)))
    sent = jnp.concatenate([req_sums.astype(jnp.bfloat16), extra], axis=2)
    sent = jnp.pad(sent, ((0, filler), (0, 0), (0, 0)))
    got = exchange(sent.reshape(shards, own_rows, sent.shape[2])).astype(jnp.float32)
    sums = got[:, :, :cols]
    bits = got[:, :, cols : cols + 6 * heads].reshape(shards, own_rows, 6, heads)
    peaks = bits[:, :, 0] + bits[:, :, 1] + bits[:, :, 2]
    totals = bits[:, :, 3] + bits[:, :, 4] + bits[:, :, 5]
    q_own = query.astype(jnp.float32).reshape(share, steps, 1, heads, HEAD_DIM)
    k_own = fresh_key.astype(jnp.float32).reshape(share, 1, steps, heads, HEAD_DIM)
    v_own = fresh_value.astype(jnp.float32).reshape(share, 1, steps, cols)
    fresh_scores = jnp.sum(q_own * k_own, axis=4) * (HEAD_DIM ** (-0.5))
    seen = (jnp.arange(steps)[None, :] <= jnp.arange(steps)[:, None])[None, :, :, None]
    fresh_scores = jnp.where(seen, fresh_scores, LOWEST)
    best = jnp.maximum(
        jnp.max(peaks, axis=0).reshape(share, steps, heads), jnp.max(fresh_scores, axis=2)
    )
    fresh_weights = jnp.where(seen, jnp.exp(fresh_scores - best[:, :, None]), 0.0)
    scale = jnp.exp(peaks - best.reshape(1, own_rows, heads))
    denominator = jnp.sum(totals * scale, axis=0) + jnp.sum(fresh_weights, axis=2).reshape(
        own_rows, heads
    )
    lowered = lax.reduce_precision(fresh_weights, 8, 7)
    numerator = jnp.sum(sums * jnp.repeat(scale, HEAD_DIM, axis=2), axis=0) + jnp.sum(
        jnp.repeat(lowered, HEAD_DIM, axis=3) * v_own, axis=2
    ).reshape(own_rows, cols)
    attended = (numerator / jnp.repeat(denominator, HEAD_DIM, axis=1)).astype(jnp.bfloat16)
    all_attended = lax.all_gather(attended, "seq", axis=0, tiled=True)[:row_count]
    projected = col_scatter(jnp.dot(all_attended, w_out, preferred_element_type=jnp.float32))
    half = projected.shape[0]
    wide_half = lax.dynamic_slice_in_dim(wide_in, lax.axis_index("col") * half, half, 0)
    residual = (wide_half + projected).astype(jnp.bfloat16)
    flat_rows = col_gather(lax.all_gather(residual, "seq", axis=1, tiled=True))

    chosen = route_ids.transpose(1, 0, 2).reshape(row_count, 2)
    expert_ids = jnp.arange(expert_count)
    w_pair = w_gate_up.reshape(experts_loc, width_all, 2 * ff_loc)
    pair_sum = jnp.einsum("rc,ecf->ref", flat_rows, w_pair, preferred_element_type=jnp.float32)
    wide_rows = flat_rows.astype(jnp.float32)
    square_sum = jnp.sum(wide_rows * wide_rows, axis=1)
    router_sum = jnp.dot(flat_rows, w_router, preferred_element_type=jnp.float32)
    inv_two = lax.rsqrt(square_sum / width_all + EPSILON)
    logits = router_sum * inv_two[:, None]
    first_pick = chosen[:, 0:1] == expert_ids[None, :]
    second_pick = chosen[:, 1:2] == expert_ids[None, :]
    first_share = jax.nn.sigmoid(
        jnp.sum(jnp.where(first_pick, logits, 0.0), axis=1)
        - jnp.sum(jnp.where(second_pick, logits, 0.0), axis=1)
    )
    gate_rows = jnp.where(first_pick, first_share[:, None], 0.0) + jnp.where(
        second_pick, 1.0 - first_share[:, None], 0.0
    )
    gate_local = lax.dynamic_slice_in_dim(gate_rows, expert_base, experts_loc, 1)
    pair_sum = pair_sum * inv_two[:, None, None]
    active = (jax.nn.silu(pair_sum[..., :ff_loc]) * pair_sum[..., ff_loc:]).astype(jnp.bfloat16)
    outputs = jnp.einsum("ref,efd->red", active, w_down, preferred_element_type=jnp.float32)
    weighted = jnp.sum(outputs * gate_local[:, :, None], axis=1)
    joined = col_scatter(weighted).astype(jnp.bfloat16)
    blocks = joined.reshape(half, shards, width_loc).transpose(1, 0, 2)
    mixture = jnp.sum(exchange(blocks).astype(jnp.float32), axis=0)
    layer_half = (residual.astype(jnp.float32) + mixture).astype(jnp.bfloat16)
    layer_rows = col_gather(layer_half).reshape(requests, steps, width_loc).transpose(1, 0, 2)
    return (layer_rows, all_pair[:, :, :cols], all_pair[:, :, cols:])


def places():
    s, c = lax.axis_index("seq"), lax.axis_index("col")
    z, y, x = s // 4, (s // 2) % 2, s % 2

    def to(dz, p):
        return ((z + dz) % 4) * 4 + ((y + p // 2) % 2) * 2 + (x + p % 2) % 2

    def source(dz, p):
        return ((z + 4 - dz) % 4) * 4 + ((y + p // 2) % 2) * 2 + (x + p % 2) % 2

    return s, c, to, source


OFFSETS = [(d, p) for p in range(4) for d in range(4)]
PEERS = OFFSETS[1:]


def send(src, dst, sems, slot, seq, col):
    return pltpu.make_async_remote_copy(
        src_ref=src,
        dst_ref=dst,
        send_sem=sems[0].at[slot],
        recv_sem=sems[1].at[slot],
        device_id=(seq, col),
        device_id_type=pl.DeviceIdType.MESH,
    )


def greet(sibling=True):
    s, c, to, _ = places()
    barrier = pltpu.get_barrier_semaphore()
    for d, p in PEERS:
        pl.semaphore_signal(
            barrier, inc=1, device_id=(to(d, p), c), device_id_type=pl.DeviceIdType.MESH
        )
    if sibling:
        pl.semaphore_signal(
            barrier, inc=1, device_id=(s, 1 - c), device_id_type=pl.DeviceIdType.MESH
        )
    pl.semaphore_wait(barrier, 16 if sibling else 15)


def gather_open(block, sems):
    s, c, to, _ = places()
    for d in range(1, 4):
        send(block(s), block(s), sems, d, to(d, 0), c).start()
    for p in range(1, 4):
        send(block(s), block(s), sems, 4 * p, to(0, p), c).start()


def gather_pass(block, sems):
    s, c, to, source = places()
    for d in range(1, 4):
        j = source(d, 0)
        send(block(j), block(j), sems, d, j, c).wait_recv()
        for p in range(1, 4):
            send(block(j), block(j), sems, 4 * p + d, to(0, p), c).start()


def gather_take(block, sems, d, p):
    _, c, _, source = places()
    j = source(d, p)
    send(block(j), block(j), sems, 4 * p + d, j, c).wait_recv()
    return j


def gather_close(block, sems):
    s, c, to, _ = places()
    for d, p in PEERS:
        send(block(s), block(s), sems, 4 * p + d, to(d, p), c).wait_send()


def share_open(block, sems, d, p):
    s, c, _, source = places()
    j = source(d, p)
    send(block(j), block(j), sems, 4 * p + d, s, 1 - c).start()


def share_take(block, other, sems, d, p):
    s, c, _, source = places()
    j = source(d, p)
    send(block(j), other(j), sems, 4 * p + d, s, 1 - c).wait_recv()
    return j


def share_close(block, sems):
    s, c, _, _ = places()
    for d, p in OFFSETS:
        send(block(s), block(s), sems, 4 * p + d, s, 1 - c).wait_send()


def halves(ref):
    c = lax.axis_index("col")
    mine, other = pl.multiple_of(c * 80, 16), pl.multiple_of((1 - c) * 80, 16)
    return (lambda j: ref.at[j, pl.ds(mine, 80), :]), (lambda j: ref.at[j, pl.ds(other, 80), :])


def dot(a, b, dims, precision=None):
    return lax.dot_general(
        a, b, (dims, ((), ())), precision=precision, preferred_element_type=jnp.float32
    )


NN = ((1,), (0,))
NT = ((1,), (1,))
TN = ((0,), (0,))


def iota(shape, axis):
    return lax.broadcasted_iota(jnp.int32, shape, axis)


def project_kernel(
    hid, order, w3, cos, sin, q_all, kv, own_in,
    hbuf, wsend, wrecv, hs, hr, ss, sr, ws, wr, qs, qr,
):
    s, c, to, source = places()
    steps, width, requests = hid.shape
    rows = steps * requests
    greet()
    mine, other = halves(hbuf)
    hsem, ssem, wsem, qsem = (hs, hr), (ss, sr), (ws, wr), (qs, qr)
    j_at = iota((rows, requests), 0)
    same = (j_at // steps) == order[...]
    placed = jnp.zeros((width, rows), jnp.float32)
    for n in range(steps):
        pick = jnp.where(same & (j_at % steps == n), 1.0, 0.0).astype(jnp.bfloat16)
        placed = placed + dot(hid[n], pick, NT)
    own = jnp.concatenate([placed, jnp.zeros((160 - width, rows), jnp.float32)], axis=0)
    own = own.astype(jnp.bfloat16)
    own_in[...] = own
    here = pl.multiple_of(c * 80, 16)
    hbuf[s, pl.ds(here, 80), :] = own_in[pl.ds(here, 80), :]
    gather_open(mine, hsem)
    share_open(mine, ssem, 0, 0)
    low = iota((width, 128), 1) < HEAD_DIM
    low_v = iota((80, 128), 1) < HEAD_DIM
    for pair in range(8):
        at = slice(128 * pair, 128 * pair + 128)
        wq, wk, wv = [w3[i, :, at].astype(jnp.float32) for i in range(3)]
        va = wv[:80]
        vb = jnp.concatenate([wv[80:], jnp.zeros((160 - width, 128), jnp.float32)], axis=0)
        turn = functools.partial(pltpu.roll, shift=64, axis=1)
        wsend[2 * pair, :width] = jnp.where(low, wq, turn(wk)).astype(jnp.bfloat16)
        wsend[2 * pair + 1, :width] = jnp.where(low, turn(wq), wk).astype(jnp.bfloat16)
        wsend[2 * pair, width:] = jnp.where(low_v, va, turn(vb)).astype(jnp.bfloat16)
        wsend[2 * pair + 1, width:] = jnp.where(low_v, turn(va), vb).astype(jnp.bfloat16)
    for d, p in PEERS:
        j = to(d, p)
        send(wsend.at[j], wrecv.at[s], wsem, 4 * p + d, j, c).start()
    gather_pass(mine, hsem)
    for d in range(1, 4):
        share_open(mine, ssem, d, 0)
    for p in range(1, 4):
        for d in range(4):
            gather_take(mine, hsem, d, p)
            share_open(mine, ssem, d, p)
    wrecv[s] = wsend[s]
    qk = jnp.zeros((128, rows), jnp.float32)
    v0 = jnp.zeros((128, rows), jnp.float32)
    v1 = jnp.zeros((128, rows), jnp.float32)
    squares = jnp.zeros((1, rows), jnp.float32)
    for d, p in OFFSETS:
        j = share_take(mine, other, ssem, d, p)
        if d or p:
            send(wrecv.at[j], wrecv.at[j], wsem, 4 * p + d, j, c).wait_recv()
        h = hbuf[j]
        w = wrecv[j]
        qk = qk + dot(w[:width], h[:width], TN)
        v0 = v0 + dot(w[width:], h[:80], TN)
        v1 = v1 + dot(w[width : width + 64], h[80:width], TN)
        wide = h.astype(jnp.float32)
        squares = squares + jnp.sum(wide * wide, axis=0, keepdims=True)
    inv = lax.rsqrt(squares / (width * 16) + EPSILON)
    half = HEAD_DIM // 2

    def turned(part):
        a, b = part[:half], part[half:]
        return jnp.concatenate([a * cos[...] - b * sin[...], b * cos[...] + a * sin[...]], axis=0)

    q_all[s] = turned(qk[:HEAD_DIM] * inv).astype(jnp.bfloat16)
    gather_open(lambda j: q_all.at[j], qsem)
    kv[:HEAD_DIM] = turned(qk[HEAD_DIM:] * inv).astype(jnp.bfloat16)
    kv[HEAD_DIM:] = ((v0[:HEAD_DIM] + v1[HEAD_DIM:]) * inv).astype(jnp.bfloat16)
    gather_pass(lambda j: q_all.at[j], qsem)
    for p in range(1, 4):
        for d in range(4):
            gather_take(lambda j: q_all.at[j], qsem, d, p)
    gather_close(mine, hsem)
    share_close(mine, ssem)
    for d, p in PEERS:
        send(wsend.at[s], wrecv.at[s], wsem, 4 * p + d, to(d, p), c).wait_send()
    gather_close(lambda j: q_all.at[j], qsem)


def vmem():
    return pl.BlockSpec(memory_space=pltpu.VMEM)


def pair_sems(count=16):
    return [pltpu.SemaphoreType.DMA((count,)), pltpu.SemaphoreType.DMA((count,))]


def project(hid, order, w3, cos, sin):
    steps, width, requests = hid.shape
    rows = steps * requests
    bf16 = jnp.bfloat16
    return pl.pallas_call(
        project_kernel,
        out_shape=(
            jax.ShapeDtypeStruct((16, HEAD_DIM, rows), bf16),
            jax.ShapeDtypeStruct((2 * HEAD_DIM, rows), bf16),
            jax.ShapeDtypeStruct((160, rows), bf16),
        ),
        in_specs=[vmem()] * 5,
        out_specs=[vmem()] * 3,
        scratch_shapes=[
            pltpu.VMEM((16, 160, rows), bf16),
            pltpu.VMEM((16, width + 80, 128), bf16),
            pltpu.VMEM((16, width + 80, 128), bf16),
            *pair_sems(), *pair_sems(), *pair_sems(), *pair_sems(),
        ],
        compiler_params=pltpu.CompilerParams(
            collective_id=0, has_side_effects=True, vmem_limit_bytes=40 * MIB
        ),
        name="project",
    )(hid, order, w3, cos, sin)


def attend_kernel(page_at, owner, count, used, q_all, *refs):
    keys, values = refs[:GROUP], refs[GROUP : 2 * GROUP]
    out, tops, flat, acc, peaks, totals, rowed = refs[2 * GROUP :]
    step = pl.program_id(0)
    rows = flat.shape[0]
    requests = rows // 4
    own = (iota((16, 1024), 1) % 256) // HEAD_DIM == iota((16, 1024), 0) // 4

    @pl.when(step == 0)
    def _():
        turned = q_all[...].reshape(16 * HEAD_DIM, rows).astype(jnp.float32)
        flat[...] = jnp.transpose(turned)

        @pl.loop(0, requests)
        def _(r):
            acc[r] = jnp.zeros((64, 256), jnp.float32)
            peaks[r] = jnp.full((64, 128), LOWEST, jnp.float32)
            totals[r] = jnp.zeros((64, 128), jnp.float32)

    @pl.when(step * GROUP < used[0])
    def _():
        token = iota((64, 128), 1)
        found = []
        for g in range(GROUP):
            at = step * GROUP + g
            r = owner[at]
            live = token < count[at]
            lines = [flat[pl.ds(4 * r + n, 1), :] for n in range(4)]
            spread = jnp.where(own, jnp.concatenate(lines * 4, axis=0), 0.0).astype(jnp.bfloat16)
            scores = jnp.concatenate(
                [
                    dot(spread[:, 256 * i : 256 * i + 256], keys[g][0, :, 256 * i : 256 * i + 256], NT)
                    for i in range(4)
                ],
                axis=0,
            )
            scores = jnp.where(live, scores * (HEAD_DIM**-0.5), LOWEST)
            top = jnp.max(scores, axis=1, keepdims=True)
            weights = jnp.where(live, jnp.exp(scores - top), 0.0)
            total = jnp.sum(weights, axis=1, keepdims=True)
            lowered = weights.astype(jnp.bfloat16)
            mixed = jnp.concatenate(
                [
                    dot(lowered[16 * i : 16 * i + 16], values[g][0, :, 256 * i : 256 * i + 256], NN)
                    for i in range(4)
                ],
                axis=0,
            )
            found.append((r, top, total, mixed))
        for r, top, total, mixed in found:
            old = peaks[r]
            new = jnp.maximum(old, top)
            keep = jnp.exp(old - new)
            add = jnp.exp(top - new)
            peaks[r] = new
            totals[r] = totals[r] * keep + total * add
            acc[r] = acc[r] * jnp.concatenate([keep, keep], axis=1) + mixed * jnp.concatenate(
                [add, add], axis=1
            )

    @pl.when(step == pl.num_programs(0) - 1)
    def _():
        diagonal = iota((64, 128), 0) == iota((64, 128), 1)
        rowed[...] = jnp.zeros_like(rowed)

        @pl.loop(0, requests // 2)
        def _(pair):
            parts = []
            for e in range(2):
                r = 2 * pair + e
                whole = acc[r]
                lines = []
                for i in range(4):
                    x = jnp.where(own[:, :256], whole[16 * i : 16 * i + 16], 0.0)
                    y = x[:8] + x[8:]
                    lines.append(y[:4] + y[4:])
                parts.append(jnp.concatenate(lines, axis=1))
                rowed[0, pl.ds(r, 1), :] = jnp.sum(
                    jnp.where(diagonal, peaks[r], 0.0), axis=0, keepdims=True
                )
                rowed[1, pl.ds(r, 1), :] = jnp.sum(
                    jnp.where(diagonal, totals[r], 0.0), axis=0, keepdims=True
                )
            flat[pl.ds(pl.multiple_of(8 * pair, 8), 8), :] = jnp.concatenate(parts, axis=0)

        out[...] = (
            jnp.transpose(flat[...]).astype(jnp.bfloat16).reshape(16, HEAD_DIM, rows)
        )
        place = (iota((128, rows), 1) // 4 == iota((128, rows), 0)).astype(jnp.float32)
        match = iota((64, rows), 0) % 4 == iota((64, rows), 1) % 4
        fold = (iota((16, 64), 1) // 4 == iota((16, 64), 0)).astype(jnp.float32)
        for k in range(2):
            spread = dot(jnp.transpose(rowed[k])[:64], place, NN, lax.Precision.HIGHEST)
            by_head = dot(fold, jnp.where(match, spread, 0.0), NN, lax.Precision.HIGHEST)
            for h in range(16):
                for t in range(3):
                    tops[h, 3 * k + t : 3 * k + t + 1, :] = by_head[
                        h : h + 1, 128 * t : 128 * t + 128
                    ]
        tops[:, 6:8, :] = jnp.zeros((16, 2, 128), jnp.float32)


def attend(page_at, owner, count, used, q_all, keys, values):
    pages, size, cols = keys.shape
    rows = q_all.shape[2]
    requests = rows // 4

    def page_spec(g):
        def index(i, page_at, owner, count, used):
            at = jnp.minimum(i * GROUP + g, jnp.maximum(used[0] - 1, 0))
            return (page_at[at], 0, 0)

        return pl.BlockSpec((1, size, cols), index)

    specs = [page_spec(g) for g in range(GROUP)]
    return pl.pallas_call(
        attend_kernel,
        grid_spec=pltpu.PrefetchScalarGridSpec(
            num_scalar_prefetch=4,
            grid=(pages // GROUP,),
            in_specs=[pl.BlockSpec((16, HEAD_DIM, rows), lambda *_: (0, 0, 0))] + specs + specs,
            out_specs=[
                pl.BlockSpec((16, HEAD_DIM, rows), lambda *_: (0, 0, 0)),
                pl.BlockSpec((16, 8, 128), lambda *_: (0, 0, 0)),
            ],
            scratch_shapes=[
                pltpu.VMEM((rows, cols), jnp.float32),
                pltpu.VMEM((requests, 64, 256), jnp.float32),
                pltpu.VMEM((requests, 64, 128), jnp.float32),
                pltpu.VMEM((requests, 64, 128), jnp.float32),
                pltpu.VMEM((2, 128, 128), jnp.float32),
            ],
        ),
        out_shape=(
            jax.ShapeDtypeStruct((16, HEAD_DIM, rows), jnp.bfloat16),
            jax.ShapeDtypeStruct((16, 8, 128), jnp.float32),
        ),
        compiler_params=pltpu.CompilerParams(vmem_limit_bytes=48 * MIB),
        cost_estimate=pl.CostEstimate(
            flops=4 * pages * 64 * size * cols,
            bytes_accessed=4 * pages * size * cols,
            transcendentals=pages * 64 * size,
        ),
        name="attend",
    )(page_at, owner, count, used, q_all, *([keys] * GROUP), *([values] * GROUP))


def combine_kernel(
    parts, tops, q_all, kv, own_in, w_out, mid_all, mid_own,
    got, got_tops, attended, partial, theirs, mbuf,
    gs, gr, ts, tr, as_, ar, ps, pr, ms, mr, ss, sr,
):
    s, c, to, source = places()
    rows = kv.shape[1]
    greet()
    gsem, tsem, asem, psem, msem, ssem = (
        (gs, gr), (ts, tr), (as_, ar), (ps, pr), (ms, mr), (ss, sr)
    )
    for d, p in PEERS:
        j = to(d, p)
        send(tops.at[j], got_tops.at[s], tsem, 4 * p + d, j, c).start()
        send(parts.at[j], got.at[s], gsem, 4 * p + d, j, c).start()
    got[s] = parts[s]
    got_tops[s] = tops[s]
    q = q_all[s].astype(jnp.float32)
    k = kv[:HEAD_DIM].astype(jnp.float32)
    v = kv[HEAD_DIM:].astype(jnp.float32)
    moment = iota((1, rows), 1) % 4
    fresh = []
    for back in range(4):
        moved = k if back == 0 else pltpu.roll(k, shift=back, axis=1)
        score = jnp.sum(q * moved, axis=0, keepdims=True) * (HEAD_DIM**-0.5)
        fresh.append(jnp.where(moment >= back, score, LOWEST))
    for d, p in PEERS:
        j = source(d, p)
        send(got_tops.at[j], got_tops.at[j], tsem, 4 * p + d, j, c).wait_recv()

    def line(j, k):
        return jnp.concatenate([got_tops[j, 3 * k + t : 3 * k + t + 1, :] for t in range(3)], axis=1)

    best = functools.reduce(jnp.maximum, fresh + [line(j, 0) for j in range(16)])
    bottom = jnp.zeros((1, rows), jnp.float32)
    top = jnp.zeros((HEAD_DIM, rows), jnp.float32)
    for back in range(4):
        weight = jnp.where(moment >= back, jnp.exp(fresh[back] - best), 0.0)
        bottom = bottom + weight
        moved = v if back == 0 else pltpu.roll(v, shift=back, axis=1)
        top = top + weight.astype(jnp.bfloat16).astype(jnp.float32) * moved
    for d, p in OFFSETS:
        j = source(d, p)
        if d or p:
            send(got.at[j], got.at[j], gsem, 4 * p + d, j, c).wait_recv()
        scale = jnp.exp(line(j, 0) - best)
        bottom = bottom + line(j, 1) * scale
        top = top + got[j].astype(jnp.float32) * scale
    attended[s] = (top / bottom).astype(jnp.bfloat16)
    whole = lambda j: attended.at[j]
    gather_open(whole, asem)
    gather_pass(whole, asem)
    for p in range(1, 4):
        for d in range(4):
            gather_take(whole, asem, d, p)
    width = w_out.shape[0]
    partial[:width] = dot(w_out[...], attended[...].reshape(16 * HEAD_DIM, rows), NN)
    partial[width:] = jnp.zeros((160 - width, rows), jnp.float32)
    here, there = pl.multiple_of(c * 80, 16), pl.multiple_of((1 - c) * 80, 16)
    swap = send(partial.at[pl.ds(there, 80), :], theirs, psem, 0, s, 1 - c)
    swap.start()
    swap.wait_recv()
    mid = own_in[pl.ds(here, 80), :].astype(jnp.float32) + partial[pl.ds(here, 80), :] + theirs[...]
    mid = mid.astype(jnp.bfloat16)
    mid_own[...] = mid
    mbuf[s, pl.ds(here, 80), :] = mid
    mine, other = halves(mbuf)
    gather_open(mine, msem)
    share_open(mine, ssem, 0, 0)
    gather_pass(mine, msem)
    for d in range(1, 4):
        share_open(mine, ssem, d, 0)
    for p in range(1, 4):
        for d in range(4):
            gather_take(mine, msem, d, p)
            share_open(mine, ssem, d, p)
    for d, p in OFFSETS:
        share_take(mine, other, ssem, d, p)
    for j in range(16):
        mid_all[width * j : width * j + width] = mbuf[j, :width]
    swap.wait_send()
    for d, p in PEERS:
        send(parts.at[s], got.at[s], gsem, 4 * p + d, to(d, p), c).wait_send()
        send(tops.at[s], got_tops.at[s], tsem, 4 * p + d, to(d, p), c).wait_send()
    gather_close(whole, asem)
    gather_close(mine, msem)
    share_close(mine, ssem)


def combine(parts, tops, q_all, kv, own_in, w_out):
    rows = kv.shape[1]
    width = w_out.shape[0]
    bf16 = jnp.bfloat16
    return pl.pallas_call(
        combine_kernel,
        out_shape=(
            jax.ShapeDtypeStruct((16 * width, rows), bf16),
            jax.ShapeDtypeStruct((80, rows), bf16),
        ),
        in_specs=[vmem()] * 6,
        out_specs=[vmem()] * 2,
        scratch_shapes=[
            pltpu.VMEM((16, HEAD_DIM, rows), bf16),
            pltpu.VMEM((16, 8, 128), jnp.float32),
            pltpu.VMEM((16, HEAD_DIM, rows), bf16),
            pltpu.VMEM((160, rows), jnp.float32),
            pltpu.VMEM((80, rows), jnp.float32),
            pltpu.VMEM((16, 160, rows), bf16),
            *pair_sems(), *pair_sems(), *pair_sems(), *pair_sems(1), *pair_sems(), *pair_sems(),
        ],
        compiler_params=pltpu.CompilerParams(
            collective_id=1, has_side_effects=True, vmem_limit_bytes=40 * MIB
        ),
        name="combine",
    )(parts, tops, q_all, kv, own_in, w_out)


def expert_kernel(mid, pair, down_hbm, router, routes, out, inv, gates, active, down, mixed, sem):
    e = pl.program_id(0)
    count = pl.num_programs(0)
    width_all, rows = mid.shape
    ff = pair.shape[2]
    fetch = pltpu.make_async_copy(down_hbm, down, sem)

    @pl.when(e == 0)
    def _():
        fetch.start()
        total = jnp.zeros((1, rows), jnp.float32)
        for i in range(16):
            at = width_all // 16
            wide = mid[at * i : at * i + at].astype(jnp.float32)
            total = total + jnp.sum(wide * wide, axis=0, keepdims=True)
        inv[...] = lax.rsqrt(total / width_all + EPSILON)
        logits = dot(router[...], mid[...], NN) * inv[...]
        which = iota(logits.shape, 0)
        first, second = which == routes[0:1], which == routes[1:2]
        share = jax.nn.sigmoid(
            jnp.sum(jnp.where(first, logits, 0.0), axis=0, keepdims=True)
            - jnp.sum(jnp.where(second, logits, 0.0), axis=0, keepdims=True)
        )
        gates[...] = jnp.where(first, share, 0.0) + jnp.where(second, 1.0 - share, 0.0)

    expert = lax.axis_index("col") * count + e
    gate = jnp.sum(jnp.where(iota(gates.shape, 0) == expert, gates[...], 0.0), axis=0, keepdims=True)
    front = dot(pair[0, 0], mid[...], NN) * inv[...]
    back = dot(pair[0, 1], mid[...], NN) * inv[...]
    value = (front / (1.0 + jnp.exp(-front))) * back
    active[e] = jnp.transpose((value * gate)).astype(jnp.bfloat16)

    @pl.when(e == count - 1)
    def _():
        fetch.wait()
        for i in range(width_all // 256):
            at = slice(256 * i, 256 * i + 256)
            part = dot(active[0], down[0, :, at], NN)
            for k in range(1, down.shape[0]):
                part = part + dot(active[k], down[k, :, at], NN)
            mixed[at] = jnp.transpose(part).astype(jnp.bfloat16)
        width = width_all // 16
        for j in range(16):
            out[j, :width] = mixed[width * j : width * j + width]
            out[j, width:] = jnp.zeros((160 - width, rows), jnp.bfloat16)


def experts(mid, pair, down, router, routes):
    width_all, rows = mid.shape
    count, _, ff, _ = pair.shape
    whole = lambda *shape: pl.BlockSpec(shape, lambda e: (0,) * len(shape))
    return pl.pallas_call(
        expert_kernel,
        grid=(count,),
        in_specs=[
            whole(width_all, rows),
            pl.BlockSpec((1, 2, ff, width_all), lambda e: (e, 0, 0, 0)),
            pl.BlockSpec(memory_space=pl.ANY),
            whole(*router.shape),
            whole(*routes.shape),
        ],
        out_specs=whole(16, 160, rows),
        out_shape=jax.ShapeDtypeStruct((16, 160, rows), jnp.bfloat16),
        scratch_shapes=[
            pltpu.VMEM((1, rows), jnp.float32),
            pltpu.VMEM((router.shape[0], rows), jnp.float32),
            pltpu.VMEM((count, rows, ff), jnp.bfloat16),
            pltpu.VMEM(down.shape, jnp.bfloat16),
            pltpu.VMEM((width_all, rows), jnp.bfloat16),
            pltpu.SemaphoreType.DMA,
        ],
        compiler_params=pltpu.CompilerParams(vmem_limit_bytes=48 * MIB),
        cost_estimate=pl.CostEstimate(
            flops=6 * count * rows * ff * width_all,
            bytes_accessed=6 * count * ff * width_all,
            transcendentals=count * rows * ff,
        ),
        name="experts",
    )(mid, pair, down, router, routes)


def close_kernel(mixed, mid_own, out, theirs, summed, got, final, cs, cr, gs, gr, fs, fr):
    s, c, to, source = places()
    rows = mid_own.shape[1]
    steps, width, requests = out.shape
    csem, gsem, fsem = (cs, cr), (gs, gr), (fs, fr)
    greet()
    here, there = pl.multiple_of(c * 80, 16), pl.multiple_of((1 - c) * 80, 16)
    swaps = []
    for d, p in PEERS + [(0, 0)]:
        j = to(d, p)
        swap = send(mixed.at[j, pl.ds(there, 80), :], theirs.at[j], csem, 4 * p + d, s, 1 - c)
        swap.start()
        swaps.append(swap)
    for (d, p), swap in zip(PEERS + [(0, 0)], swaps):
        j = to(d, p)
        swap.wait_recv()
        summed[j] = (
            mixed[j, pl.ds(here, 80), :].astype(jnp.float32) + theirs[j].astype(jnp.float32)
        ).astype(jnp.bfloat16)
        if d or p:
            send(summed.at[j], got.at[s], gsem, 4 * p + d, j, c).start()
    total = mid_own[...].astype(jnp.float32) + summed[s].astype(jnp.float32)
    for d, p in PEERS:
        j = source(d, p)
        send(got.at[j], got.at[j], gsem, 4 * p + d, j, c).wait_recv()
        total = total + got[j].astype(jnp.float32)
    final[pl.ds(here, 80), :] = total.astype(jnp.bfloat16)
    half, other = final.at[pl.ds(here, 80), :], final.at[pl.ds(there, 80), :]
    last = send(half, half, fsem, 0, s, 1 - c)
    last.start()
    send(half, other, fsem, 0, s, 1 - c).wait_recv()
    j_at = iota((rows, requests), 0)
    for n in range(steps):
        pick = jnp.where(j_at == iota((rows, requests), 1) * steps + n, 1.0, 0.0)
        out[n] = dot(final[:width], pick.astype(jnp.bfloat16), NN).astype(jnp.bfloat16)
    last.wait_send()
    for swap in swaps:
        swap.wait_send()
    for d, p in PEERS:
        send(summed.at[s], got.at[s], gsem, 4 * p + d, to(d, p), c).wait_send()


def close(mixed, mid_own, steps, width):
    rows = mid_own.shape[1]
    bf16 = jnp.bfloat16
    return pl.pallas_call(
        close_kernel,
        out_shape=jax.ShapeDtypeStruct((steps, width, rows // steps), bf16),
        in_specs=[vmem()] * 2,
        out_specs=vmem(),
        scratch_shapes=[
            pltpu.VMEM((16, 80, rows), bf16),
            pltpu.VMEM((16, 80, rows), bf16),
            pltpu.VMEM((16, 80, rows), bf16),
            pltpu.VMEM((160, rows), bf16),
            *pair_sems(), *pair_sems(), *pair_sems(1),
        ],
        compiler_params=pltpu.CompilerParams(
            collective_id=2, has_side_effects=True, vmem_limit_bytes=40 * MIB
        ),
        name="close",
    )(mixed, mid_own)


def page_lists(page_table, cache_len, pages, size, steps):
    requests = cache_len.shape[0]
    columns = jnp.arange(page_table.shape[1])
    filled = (cache_len + size - 1) // size
    in_use = columns[None, :] < filled[:, None]
    local_pages = page_table - lax.axis_index("seq") * pages
    hits = in_use[:, :, None] & (local_pages[:, :, None] == jnp.arange(pages)[None, None, :])
    left = cache_len[:, None] - columns[None, :] * size
    code = jnp.arange(requests)[:, None] * 256 + jnp.minimum(left, size)
    code = jnp.sum(jnp.where(hits, code[:, :, None], 0), axis=(0, 1))
    taken = code > 0
    index = jnp.arange(pages)
    before = jnp.sum(jnp.where(taken[:, None] & (index[:, None] < index[None, :]), 1, 0), axis=0)
    place = taken[:, None] & (before[:, None] == index[None, :])
    packed = jnp.sum(jnp.where(place, (code + index * 65536)[:, None], 0), axis=0)
    used = jnp.sum(taken.astype(jnp.int32))[None]
    return packed // 65536, (packed % 65536) // 256, packed % 256, used


def fast(
    hidden,
    key_cache,
    value_cache,
    page_table,
    cache_len,
    order,
    route_ids,
    w_qkv,
    w_out,
    w_router,
    w_gate_up,
    w_down,
):
    steps, requests, width = hidden.shape
    pages, size, cols = key_cache.shape
    rows = steps * requests
    half = HEAD_DIM // 2
    frequency = jnp.exp(
        -jnp.log(10000.0) * 2.0 * jnp.arange(half, dtype=jnp.float32) / HEAD_DIM
    )
    positions = (cache_len[:, None] + jnp.arange(steps)[None, :]).reshape(rows)
    angles = frequency[:, None] * positions.astype(jnp.float32)[None, :]
    q_all, kv, own_in = project(
        hidden.transpose(0, 2, 1),
        order[None, :],
        w_qkv.transpose(1, 0, 2),
        jnp.cos(angles),
        jnp.sin(angles),
    )
    all_kv = lax.all_gather(kv, "seq", axis=0)
    lists = page_lists(page_table, cache_len, pages, size, steps)
    parts, tops = attend(*[item.astype(jnp.int32) for item in lists], q_all, key_cache, value_cache)
    mid, mid_own = combine(parts, tops, q_all, kv, own_in, w_out.T)
    routes = route_ids.transpose(2, 1, 0).reshape(2, rows)
    mixed = experts(mid, w_gate_up.transpose(0, 2, 3, 1), w_down, w_router.T, routes)
    layer = close(mixed, mid_own, steps, width)
    pick = (
        jnp.arange(requests)[None, :, None] * steps + jnp.arange(steps)[:, None, None]
        == jnp.arange(rows)[None, None, :]
    ).astype(jnp.bfloat16)

    def by_step(block):
        return jnp.einsum(
            "nrj,cj->nrc", pick, block.reshape(cols, rows), preferred_element_type=jnp.float32
        ).astype(jnp.bfloat16)

    return (
        layer.transpose(0, 2, 1),
        by_step(all_kv[:, :HEAD_DIM]),
        by_step(all_kv[:, HEAD_DIM:]),
    )


def solution(mesh):
    placed = (
        P(None, None, "seq"),
        P("seq", None, "col"),
        P("seq", None, "col"),
        P(),
        P(),
        P(),
        P(),
        P("seq", None, "col"),
        P("col", "seq"),
        P(),
        P("col", None, None, "seq"),
        P("col", "seq", None),
    )
    small = mesh.shape["seq"] == 16 and mesh.shape["col"] == 2
    return jax.shard_map(
        fast if small else local,
        mesh=mesh,
        in_specs=placed,
        out_specs=(P(None, None, "seq"), P(None, None, "col"), P(None, None, "col")),
        check_vma=False,
    )
```

```python
import functools

import jax
import jax.numpy as jnp
from jax import lax
from jax.experimental import pallas as pl
from jax.experimental.pallas import tpu as pltpu
from jax.sharding import PartitionSpec as P

HEAD_DIM = 64
EPSILON = 1e-05
LOWEST = -1e30
GROUP = 4
MIB = 1024 * 1024


def rotate(row_data, positions, head_dim):
    head_count = row_data.shape[1] // head_dim
    half_dim = head_dim // 2
    frequency = jnp.exp(
        -jnp.log(10000.0) * 2.0 * jnp.arange(half_dim, dtype=jnp.float32) / head_dim
    )
    angles = positions.astype(jnp.float32)[:, None] * frequency[None, :]
    cosine = jnp.cos(angles)[:, None, :]
    sines = jnp.sin(angles)[:, None, :]
    by_head = row_data.reshape(row_data.shape[0], head_count, head_dim)
    front_half = by_head[:, :, :half_dim]
    back_half = by_head[:, :, half_dim:]
    turned = jnp.concatenate(
        [front_half * cosine - back_half * sines, back_half * cosine + front_half * sines], axis=2
    )
    return turned.reshape(row_data.shape)


def page_kernel(owner_ref, count_ref, q_ref, k_ref, v_ref, sum_ref, peak_ref, total_ref):
    page = pl.program_id(0)
    steps, cols = q_ref.shape[1], q_ref.shape[2]
    size = k_ref.shape[1]
    padded = peak_ref.shape[2] // steps
    count = count_ref[page]
    wide = q_ref[0].astype(jnp.float32)
    own = lax.broadcasted_iota(jnp.int32, (padded, cols), 1) // HEAD_DIM == lax.broadcasted_iota(
        jnp.int32, (padded, cols), 0
    )
    spread = jnp.concatenate(
        [jnp.where(own, wide[n : n + 1, :], 0.0) for n in range(steps)], axis=0
    ).astype(jnp.bfloat16)
    scores = lax.dot_general(
        k_ref[0], spread, (((1,), (1,)), ((), ())), preferred_element_type=jnp.float32
    ) * (HEAD_DIM ** (-0.5))
    live = lax.broadcasted_iota(jnp.int32, (size, steps * padded), 0) < count
    scores = jnp.where(live, scores, LOWEST)
    peak = jnp.max(scores, axis=0, keepdims=True)
    weights = jnp.where(live, jnp.exp(scores - peak), 0.0)
    peak_ref[0] = peak
    total_ref[0] = jnp.sum(weights, axis=0, keepdims=True)
    mixed = lax.dot_general(
        weights.astype(jnp.bfloat16),
        v_ref[0],
        (((0,), (0,)), ((), ())),
        preferred_element_type=jnp.float32,
    )
    for n in range(steps):
        part = jnp.where(own, mixed[n * padded : (n + 1) * padded, :], 0.0)
        sum_ref[0, n : n + 1, :] = jnp.sum(part, axis=0, keepdims=True)


def page_parts(owner, count, query, keys, values):
    pages, size, cols = keys.shape
    steps = query.shape[1]
    heads = cols // HEAD_DIM
    padded = -(-heads // 8) * 8
    sums, peak, total = pl.pallas_call(
        page_kernel,
        grid_spec=pltpu.PrefetchScalarGridSpec(
            num_scalar_prefetch=2,
            grid=(pages,),
            in_specs=[
                pl.BlockSpec((1, steps, cols), lambda p, o, c: (o[p], 0, 0)),
                pl.BlockSpec((1, size, cols), lambda p, o, c: (p, 0, 0)),
                pl.BlockSpec((1, size, cols), lambda p, o, c: (p, 0, 0)),
            ],
            out_specs=[
                pl.BlockSpec((1, steps, cols), lambda p, o, c: (p, 0, 0)),
                pl.BlockSpec((1, 1, steps * padded), lambda p, o, c: (p, 0, 0)),
                pl.BlockSpec((1, 1, steps * padded), lambda p, o, c: (p, 0, 0)),
            ],
        ),
        out_shape=(
            jax.ShapeDtypeStruct((pages, steps, cols), jnp.float32),
            jax.ShapeDtypeStruct((pages, 1, steps * padded), jnp.float32),
            jax.ShapeDtypeStruct((pages, 1, steps * padded), jnp.float32),
        ),
        cost_estimate=pl.CostEstimate(
            flops=4 * pages * steps * padded * size * cols,
            bytes_accessed=4 * pages * size * cols,
            transcendentals=pages * steps * padded * size,
        ),
    )(owner, count, query, keys, values)
    peak = peak.reshape(pages, steps, padded)[:, :, :heads]
    total = total.reshape(pages, steps, padded)[:, :, :heads]
    return sums, peak, total


def pieces(value, count):
    out = []
    for _ in range(count):
        part = lax.reduce_precision(value, 8, 7)
        out.append(part.astype(jnp.bfloat16))
        value = value - part
    return out


def exchange(blocks):
    return lax.all_to_all(blocks, "seq", split_axis=0, concat_axis=0, tiled=True)


def col_scatter(rows):
    if lax.axis_size("col") == 2:
        half = rows.shape[0] // 2
        me = lax.axis_index("col")
        mine = lax.dynamic_slice_in_dim(rows, me * half, half, 0)
        theirs = lax.dynamic_slice_in_dim(rows, (1 - me) * half, half, 0)
        return mine + lax.ppermute(theirs, "col", [(0, 1), (1, 0)])
    return lax.psum_scatter(rows, "col", scatter_dimension=0, tiled=True)


def col_gather(rows):
    if lax.axis_size("col") == 2:
        me = lax.axis_index("col")
        other = lax.ppermute(rows, "col", [(0, 1), (1, 0)])
        first = jnp.where(me == 0, rows, other)
        second = jnp.where(me == 0, other, rows)
        return jnp.concatenate([first, second], axis=0)
    return lax.all_gather(rows, "col", axis=0, tiled=True)


def local(
    hidden,
    key_cache,
    value_cache,
    page_table,
    cache_len,
    order,
    route_ids,
    w_qkv,
    w_out,
    w_router,
    w_gate_up,
    w_down,
):
    steps, requests, width_loc = hidden.shape
    pages_loc, page_size, cols = key_cache.shape
    heads = cols // HEAD_DIM
    shards = lax.axis_size("seq")
    width_all = width_loc * shards
    experts_loc = w_gate_up.shape[0]
    ff_loc = w_gate_up.shape[3]
    expert_count = w_router.shape[1]
    expert_base = lax.axis_index("col") * experts_loc
    seq_index = lax.axis_index("seq")
    share = -(-requests // shards)
    filler = share * shards - requests
    row_count = steps * requests
    own_rows = share * steps

    placing = (order[:, None] == jnp.arange(requests)[None, :]).astype(jnp.bfloat16)
    inputs = jnp.einsum("nsc,sr->rnc", hidden, placing, preferred_element_type=jnp.float32).astype(
        jnp.bfloat16
    )
    flat_in = inputs.reshape(row_count, width_loc)
    wide_in = flat_in.astype(jnp.float32)
    squares = jnp.sum(wide_in * wide_in, axis=1, keepdims=True)
    partial = jnp.dot(
        flat_in, w_qkv.reshape(width_loc, 3 * cols), preferred_element_type=jnp.float32
    ).astype(jnp.bfloat16)
    tail = jnp.pad(jnp.concatenate(pieces(squares, 3), axis=1), ((0, 0), (0, 125)))
    sent = jnp.pad(jnp.concatenate([partial, tail], axis=1), ((0, filler * steps), (0, 0)))
    sent = sent.reshape(shards, own_rows, 3 * cols + 128)
    got = jnp.sum(exchange(sent).astype(jnp.float32), axis=0)
    inv_one = lax.rsqrt(jnp.sum(got[:, 3 * cols :], axis=1) / width_all + EPSILON)
    proj = got[:, : 3 * cols] * inv_one[:, None]
    own_len = lax.dynamic_slice_in_dim(jnp.pad(cache_len, (0, filler)), seq_index * share, share, 0)
    positions = (own_len[:, None] + jnp.arange(steps)[None, :]).reshape(own_rows)
    query = rotate(proj[:, :cols], positions, HEAD_DIM).astype(jnp.bfloat16)
    fresh_key = rotate(proj[:, cols : 2 * cols], positions, HEAD_DIM).astype(jnp.bfloat16)
    fresh_value = proj[:, 2 * cols :].astype(jnp.bfloat16)
    all_query = lax.all_gather(query, "seq", axis=0, tiled=True)[:row_count]
    all_query, fresh_pair = lax.optimization_barrier(
        (all_query, jnp.concatenate([fresh_key, fresh_value], axis=1))
    )
    all_pair = lax.all_gather(fresh_pair, "seq", axis=0, tiled=True)[:row_count]
    all_pair = all_pair.reshape(requests, steps, 2 * cols).transpose(1, 0, 2)

    needed = (cache_len + steps + page_size - 1) // page_size
    columns = jnp.arange(page_table.shape[1])
    in_use = columns[None, :] < needed[:, None]
    local_pages = page_table - seq_index * pages_loc
    page_hits = in_use[:, :, None] & (
        local_pages[:, :, None] == jnp.arange(pages_loc)[None, None, :]
    )
    owned_by = jnp.any(page_hits, axis=1)
    page_starts = jnp.sum(jnp.where(page_hits, columns[None, :, None] * page_size, 0), axis=(0, 1))
    page_len = jnp.sum(jnp.where(owned_by, cache_len[:, None], 0), axis=0)
    owner = jnp.sum(jnp.where(owned_by, jnp.arange(requests)[:, None], 0), axis=0)
    count = page_len - page_starts
    page_sums, page_peak, page_total = page_parts(
        owner.astype(jnp.int32),
        count.astype(jnp.int32),
        all_query.reshape(requests, steps, cols),
        key_cache,
        value_cache,
    )
    mask = owned_by[:, :, None, None]
    req_peak = jnp.max(jnp.where(mask, page_peak[None], LOWEST), axis=1)
    back_peak = jnp.max(jnp.where(mask, req_peak[:, None], LOWEST), axis=0)
    factor = jnp.exp(page_peak - back_peak)
    factor = jnp.where((count > 0)[:, None, None] & jnp.any(owned_by, axis=0)[:, None, None], factor, 0.0)
    owner_float = owned_by.astype(jnp.float32)
    req_total = jnp.einsum(
        "rp,pnh->rnh", owner_float, page_total * factor, precision=lax.Precision.HIGHEST
    )
    scaled = page_sums * jnp.repeat(factor, HEAD_DIM, axis=2)
    req_sums = jnp.einsum("rp,pnc->rnc", owner_float, scaled, precision=lax.Precision.HIGHEST)
    extra = jnp.concatenate(pieces(req_peak, 3) + pieces(req_total, 3), axis=2)
    spare = -extra.shape[2] % 128
    extra = jnp.pad(extra, ((0, 0), (0, 0), (0, spare)))
    sent = jnp.concatenate([req_sums.astype(jnp.bfloat16), extra], axis=2)
    sent = jnp.pad(sent, ((0, filler), (0, 0), (0, 0)))
    got = exchange(sent.reshape(shards, own_rows, sent.shape[2])).astype(jnp.float32)
    sums = got[:, :, :cols]
    bits = got[:, :, cols : cols + 6 * heads].reshape(shards, own_rows, 6, heads)
    peaks = bits[:, :, 0] + bits[:, :, 1] + bits[:, :, 2]
    totals = bits[:, :, 3] + bits[:, :, 4] + bits[:, :, 5]
    q_own = query.astype(jnp.float32).reshape(share, steps, 1, heads, HEAD_DIM)
    k_own = fresh_key.astype(jnp.float32).reshape(share, 1, steps, heads, HEAD_DIM)
    v_own = fresh_value.astype(jnp.float32).reshape(share, 1, steps, cols)
    fresh_scores = jnp.sum(q_own * k_own, axis=4) * (HEAD_DIM ** (-0.5))
    seen = (jnp.arange(steps)[None, :] <= jnp.arange(steps)[:, None])[None, :, :, None]
    fresh_scores = jnp.where(seen, fresh_scores, LOWEST)
    best = jnp.maximum(
        jnp.max(peaks, axis=0).reshape(share, steps, heads), jnp.max(fresh_scores, axis=2)
    )
    fresh_weights = jnp.where(seen, jnp.exp(fresh_scores - best[:, :, None]), 0.0)
    scale = jnp.exp(peaks - best.reshape(1, own_rows, heads))
    denominator = jnp.sum(totals * scale, axis=0) + jnp.sum(fresh_weights, axis=2).reshape(
        own_rows, heads
    )
    lowered = lax.reduce_precision(fresh_weights, 8, 7)
    numerator = jnp.sum(sums * jnp.repeat(scale, HEAD_DIM, axis=2), axis=0) + jnp.sum(
        jnp.repeat(lowered, HEAD_DIM, axis=3) * v_own, axis=2
    ).reshape(own_rows, cols)
    attended = (numerator / jnp.repeat(denominator, HEAD_DIM, axis=1)).astype(jnp.bfloat16)
    all_attended = lax.all_gather(attended, "seq", axis=0, tiled=True)[:row_count]
    projected = col_scatter(jnp.dot(all_attended, w_out, preferred_element_type=jnp.float32))
    half = projected.shape[0]
    wide_half = lax.dynamic_slice_in_dim(wide_in, lax.axis_index("col") * half, half, 0)
    residual = (wide_half + projected).astype(jnp.bfloat16)
    flat_rows = col_gather(lax.all_gather(residual, "seq", axis=1, tiled=True))

    chosen = route_ids.transpose(1, 0, 2).reshape(row_count, 2)
    expert_ids = jnp.arange(expert_count)
    w_pair = w_gate_up.reshape(experts_loc, width_all, 2 * ff_loc)
    pair_sum = jnp.einsum("rc,ecf->ref", flat_rows, w_pair, preferred_element_type=jnp.float32)
    wide_rows = flat_rows.astype(jnp.float32)
    square_sum = jnp.sum(wide_rows * wide_rows, axis=1)
    router_sum = jnp.dot(flat_rows, w_router, preferred_element_type=jnp.float32)
    inv_two = lax.rsqrt(square_sum / width_all + EPSILON)
    logits = router_sum * inv_two[:, None]
    first_pick = chosen[:, 0:1] == expert_ids[None, :]
    second_pick = chosen[:, 1:2] == expert_ids[None, :]
    first_share = jax.nn.sigmoid(
        jnp.sum(jnp.where(first_pick, logits, 0.0), axis=1)
        - jnp.sum(jnp.where(second_pick, logits, 0.0), axis=1)
    )
    gate_rows = jnp.where(first_pick, first_share[:, None], 0.0) + jnp.where(
        second_pick, 1.0 - first_share[:, None], 0.0
    )
    gate_local = lax.dynamic_slice_in_dim(gate_rows, expert_base, experts_loc, 1)
    pair_sum = pair_sum * inv_two[:, None, None]
    active = (jax.nn.silu(pair_sum[..., :ff_loc]) * pair_sum[..., ff_loc:]).astype(jnp.bfloat16)
    outputs = jnp.einsum("ref,efd->red", active, w_down, preferred_element_type=jnp.float32)
    weighted = jnp.sum(outputs * gate_local[:, :, None], axis=1)
    joined = col_scatter(weighted).astype(jnp.bfloat16)
    blocks = joined.reshape(half, shards, width_loc).transpose(1, 0, 2)
    mixture = jnp.sum(exchange(blocks).astype(jnp.float32), axis=0)
    layer_half = (residual.astype(jnp.float32) + mixture).astype(jnp.bfloat16)
    layer_rows = col_gather(layer_half).reshape(requests, steps, width_loc).transpose(1, 0, 2)
    return (layer_rows, all_pair[:, :, :cols], all_pair[:, :, cols:])


def places():
    s, c = lax.axis_index("seq"), lax.axis_index("col")
    z, y, x = s // 4, (s // 2) % 2, s % 2

    def to(dz, p):
        return ((z + dz) % 4) * 4 + ((y + p // 2) % 2) * 2 + (x + p % 2) % 2

    def source(dz, p):
        return ((z + 4 - dz) % 4) * 4 + ((y + p // 2) % 2) * 2 + (x + p % 2) % 2

    return s, c, to, source


OFFSETS = [(d, p) for p in range(4) for d in range(4)]
PEERS = OFFSETS[1:]


def send(src, dst, sems, slot, seq, col):
    return pltpu.make_async_remote_copy(
        src_ref=src,
        dst_ref=dst,
        send_sem=sems[0].at[slot],
        recv_sem=sems[1].at[slot],
        device_id=(seq, col),
        device_id_type=pl.DeviceIdType.MESH,
    )


NEAR = [(d, p) for d, p in PEERS if d == 0 or p == 0]


def greet(peers=NEAR):
    s, c, to, _ = places()
    barrier = pltpu.get_barrier_semaphore()
    for d, p in peers:
        pl.semaphore_signal(
            barrier, inc=1, device_id=(to(d, p), c), device_id_type=pl.DeviceIdType.MESH
        )
    pl.semaphore_signal(
        barrier, inc=1, device_id=(s, 1 - c), device_id_type=pl.DeviceIdType.MESH
    )
    pl.semaphore_wait(barrier, len(peers) + 1)


def gather_open(block, sems):
    s, c, to, _ = places()
    for d in range(1, 4):
        send(block(s), block(s), sems, d, to(d, 0), c).start()
    for p in range(1, 4):
        send(block(s), block(s), sems, 4 * p, to(0, p), c).start()


def gather_pass(block, sems):
    s, c, to, source = places()
    for d in range(1, 4):
        j = source(d, 0)
        send(block(j), block(j), sems, d, j, c).wait_recv()
        for p in range(1, 4):
            send(block(j), block(j), sems, 4 * p + d, to(0, p), c).start()


def gather_take(block, sems, d, p):
    _, c, _, source = places()
    j = source(d, p)
    send(block(j), block(j), sems, 4 * p + d, j, c).wait_recv()
    return j


def gather_close(block, sems):
    s, c, to, _ = places()
    for d, p in PEERS:
        send(block(s), block(s), sems, 4 * p + d, to(d, p), c).wait_send()


def share_open(block, sems, d, p):
    s, c, _, source = places()
    j = source(d, p)
    send(block(j), block(j), sems, 4 * p + d, s, 1 - c).start()


def share_take(block, other, sems, d, p):
    s, c, _, source = places()
    j = source(d, p)
    send(block(j), other(j), sems, 4 * p + d, s, 1 - c).wait_recv()
    return j


def share_close(block, sems):
    s, c, _, _ = places()
    for d, p in OFFSETS:
        send(block(s), block(s), sems, 4 * p + d, s, 1 - c).wait_send()


def halves(ref):
    c = lax.axis_index("col")
    mine, other = pl.multiple_of(c * 80, 16), pl.multiple_of((1 - c) * 80, 16)
    return (lambda j: ref.at[j, pl.ds(mine, 80), :]), (lambda j: ref.at[j, pl.ds(other, 80), :])


def dot(a, b, dims, precision=None):
    return lax.dot_general(
        a, b, (dims, ((), ())), precision=precision, preferred_element_type=jnp.float32
    )


NN = ((1,), (0,))
NT = ((1,), (1,))
TN = ((0,), (0,))


def iota(shape, axis):
    return lax.broadcasted_iota(jnp.int32, shape, axis)


def list_pages(table, lens, lists, pages, size):
    requests = table.shape[0]
    base = lax.axis_index("seq") * pages
    column = iota((1, table.shape[1]), 1)
    page = iota((pages, table.shape[1]), 0)

    def add(r, codes):
        left = lens[r] - column * size
        code = jnp.where(left > 0, r * 256 + jnp.minimum(left, size), 0)
        return codes + jnp.where(page == table[pl.ds(r, 1), :] - base, code, 0)

    codes = lax.fori_loop(0, requests, add, jnp.zeros(page.shape, jnp.int32))
    code = jnp.sum(codes.astype(jnp.float32), axis=1, keepdims=True)
    taken = jnp.where(code > 0.0, jnp.ones((1, 128), jnp.float32), 0.0)
    below = (iota((pages, pages), 1) < iota((pages, pages), 0)).astype(jnp.float32)
    before = dot(below.astype(jnp.bfloat16), taken.astype(jnp.bfloat16), NN)
    slot = iota((pages, 128), 1).astype(jnp.float32)
    placed = jnp.where(before == slot, taken, 0.0)
    at = jnp.sum(placed * iota((pages, 128), 0).astype(jnp.float32), axis=0, keepdims=True)
    packed = jnp.sum(placed * code, axis=0, keepdims=True).astype(jnp.int32)
    lists[...] = jnp.concatenate(
        [
            at.astype(jnp.int32),
            packed >> 8,
            packed & 255,
            jnp.sum(taken, axis=0, keepdims=True).astype(jnp.int32),
            jnp.zeros((4, 128), jnp.int32),
        ],
        axis=0,
    )


def project_kernel(
    pages, size, hid, order, w3, cos, sin, table, lens, q_all, kv, own_in, lists,
    hbuf, wsend, wrecv, hs, hr, ss, sr, ws, wr, qs, qr,
):
    s, c, to, source = places()
    steps, width, requests = hid.shape
    rows = steps * requests
    greet(PEERS)
    mine, other = halves(hbuf)
    hsem, ssem, wsem, qsem = (hs, hr), (ss, sr), (ws, wr), (qs, qr)
    j_at = iota((rows, requests), 0)
    same = (j_at // steps) == order[...]
    placed = jnp.zeros((width, rows), jnp.float32)
    for n in range(steps):
        pick = jnp.where(same & (j_at % steps == n), 1.0, 0.0).astype(jnp.bfloat16)
        placed = placed + dot(hid[n], pick, NT)
    own = jnp.concatenate([placed, jnp.zeros((160 - width, rows), jnp.float32)], axis=0)
    own = own.astype(jnp.bfloat16)
    own_in[...] = own
    here = pl.multiple_of(c * 80, 16)
    hbuf[s, pl.ds(here, 80), :] = own_in[pl.ds(here, 80), :]
    gather_open(mine, hsem)
    share_open(mine, ssem, 0, 0)
    low = iota((width, 128), 1) < HEAD_DIM
    low_v = iota((80, 128), 1) < HEAD_DIM
    for pair in range(8):
        at = slice(128 * pair, 128 * pair + 128)
        wq, wk, wv = [w3[i, :, at].astype(jnp.float32) for i in range(3)]
        va = wv[:80]
        vb = jnp.concatenate([wv[80:], jnp.zeros((160 - width, 128), jnp.float32)], axis=0)
        turn = functools.partial(pltpu.roll, shift=64, axis=1)
        wsend[2 * pair, :width] = jnp.where(low, wq, turn(wk)).astype(jnp.bfloat16)
        wsend[2 * pair + 1, :width] = jnp.where(low, turn(wq), wk).astype(jnp.bfloat16)
        wsend[2 * pair, width:] = jnp.where(low_v, va, turn(vb)).astype(jnp.bfloat16)
        wsend[2 * pair + 1, width:] = jnp.where(low_v, turn(va), vb).astype(jnp.bfloat16)
    for d, p in PEERS:
        j = to(d, p)
        send(wsend.at[j], wrecv.at[s], wsem, 4 * p + d, j, c).start()
    gather_pass(mine, hsem)
    for d in range(1, 4):
        share_open(mine, ssem, d, 0)
    list_pages(table, lens, lists, pages, size)
    for p in range(1, 4):
        for d in range(4):
            gather_take(mine, hsem, d, p)
            share_open(mine, ssem, d, p)
    wrecv[s] = wsend[s]
    qk = jnp.zeros((128, rows), jnp.float32)
    v0 = jnp.zeros((128, rows), jnp.float32)
    v1 = jnp.zeros((128, rows), jnp.float32)
    squares = jnp.zeros((1, rows), jnp.float32)
    for d, p in OFFSETS:
        j = share_take(mine, other, ssem, d, p)
        if d or p:
            send(wrecv.at[j], wrecv.at[j], wsem, 4 * p + d, j, c).wait_recv()
        h = hbuf[j]
        w = wrecv[j]
        qk = qk + dot(w[:width], h[:width], TN)
        v0 = v0 + dot(w[width:], h[:80], TN)
        v1 = v1 + dot(w[width : width + 64], h[80:width], TN)
        wide = h.astype(jnp.float32)
        squares = squares + jnp.sum(wide * wide, axis=0, keepdims=True)
    inv = lax.rsqrt(squares / (width * 16) + EPSILON)
    half = HEAD_DIM // 2

    def turned(part):
        a, b = part[:half], part[half:]
        return jnp.concatenate([a * cos[...] - b * sin[...], b * cos[...] + a * sin[...]], axis=0)

    q_all[s] = turned(qk[:HEAD_DIM] * inv).astype(jnp.bfloat16)
    gather_open(lambda j: q_all.at[j], qsem)
    kv[:HEAD_DIM] = turned(qk[HEAD_DIM:] * inv).astype(jnp.bfloat16)
    kv[HEAD_DIM:] = ((v0[:HEAD_DIM] + v1[HEAD_DIM:]) * inv).astype(jnp.bfloat16)
    gather_pass(lambda j: q_all.at[j], qsem)
    for p in range(1, 4):
        for d in range(4):
            gather_take(lambda j: q_all.at[j], qsem, d, p)
    gather_close(mine, hsem)
    share_close(mine, ssem)
    for d, p in PEERS:
        send(wsend.at[s], wrecv.at[s], wsem, 4 * p + d, to(d, p), c).wait_send()
    gather_close(lambda j: q_all.at[j], qsem)


def vmem():
    return pl.BlockSpec(memory_space=pltpu.VMEM)


def pair_sems(count=16):
    return [pltpu.SemaphoreType.DMA((count,)), pltpu.SemaphoreType.DMA((count,))]


def project(hid, order, w3, cos, sin, table, lens, pages, size):
    steps, width, requests = hid.shape
    rows = steps * requests
    bf16 = jnp.bfloat16
    return pl.pallas_call(
        functools.partial(project_kernel, pages, size),
        out_shape=(
            jax.ShapeDtypeStruct((16, HEAD_DIM, rows), bf16),
            jax.ShapeDtypeStruct((2 * HEAD_DIM, rows), bf16),
            jax.ShapeDtypeStruct((160, rows), bf16),
            jax.ShapeDtypeStruct((8, 128), jnp.int32),
        ),
        in_specs=[vmem()] * 6 + [pl.BlockSpec(memory_space=pltpu.SMEM)],
        out_specs=[vmem()] * 4,
        scratch_shapes=[
            pltpu.VMEM((16, 160, rows), bf16),
            pltpu.VMEM((16, width + 80, 128), bf16),
            pltpu.VMEM((16, width + 80, 128), bf16),
            *pair_sems(), *pair_sems(), *pair_sems(), *pair_sems(),
        ],
        compiler_params=pltpu.CompilerParams(
            collective_id=0, has_side_effects=True, vmem_limit_bytes=40 * MIB
        ),
        name="project",
    )(hid, order, w3, cos, sin, table, lens)


def attend_kernel(lists, q_all, *refs):
    keys, values = refs[:GROUP], refs[GROUP : 2 * GROUP]
    out, tops, flat, acc, peaks, totals, rowed = refs[2 * GROUP :]
    step = pl.program_id(0)
    rows = flat.shape[0]
    requests = rows // 4
    own = (iota((16, 1024), 1) % 256) // HEAD_DIM == iota((16, 1024), 0) // 4

    @pl.when(step == 0)
    def _():
        turned = q_all[...].reshape(16 * HEAD_DIM, rows).astype(jnp.float32)
        flat[...] = jnp.transpose(turned)

        @pl.loop(0, requests)
        def _(r):
            acc[r] = jnp.zeros((64, 256), jnp.float32)
            peaks[r] = jnp.full((64, 128), LOWEST, jnp.float32)
            totals[r] = jnp.zeros((64, 128), jnp.float32)

    @pl.when(step * GROUP < lists[3, 0])
    def _():
        token = iota((64, 128), 1)
        found = []
        for g in range(GROUP):
            at = step * GROUP + g
            r = lists[1, at]
            live = token < lists[2, at]
            lines = [flat[pl.ds(4 * r + n, 1), :] for n in range(4)]
            spread = jnp.where(own, jnp.concatenate(lines * 4, axis=0), 0.0).astype(jnp.bfloat16)
            scores = jnp.concatenate(
                [
                    dot(spread[:, 256 * i : 256 * i + 256], keys[g][0, :, 256 * i : 256 * i + 256], NT)
                    for i in range(4)
                ],
                axis=0,
            )
            scores = jnp.where(live, scores * (HEAD_DIM**-0.5), LOWEST)
            top = jnp.max(scores, axis=1, keepdims=True)
            weights = jnp.where(live, jnp.exp(scores - top), 0.0)
            total = jnp.sum(weights, axis=1, keepdims=True)
            lowered = weights.astype(jnp.bfloat16)
            mixed = jnp.concatenate(
                [
                    dot(lowered[16 * i : 16 * i + 16], values[g][0, :, 256 * i : 256 * i + 256], NN)
                    for i in range(4)
                ],
                axis=0,
            )
            found.append((r, top, total, mixed))
        for r, top, total, mixed in found:
            old = peaks[r]
            new = jnp.maximum(old, top)
            keep = jnp.exp(old - new)
            add = jnp.exp(top - new)
            peaks[r] = new
            totals[r] = totals[r] * keep + total * add
            acc[r] = acc[r] * jnp.concatenate([keep, keep], axis=1) + mixed * jnp.concatenate(
                [add, add], axis=1
            )

    @pl.when(step == pl.num_programs(0) - 1)
    def _():
        diagonal = iota((64, 128), 0) == iota((64, 128), 1)
        rowed[...] = jnp.zeros_like(rowed)

        @pl.loop(0, requests // 2)
        def _(pair):
            parts = []
            for e in range(2):
                r = 2 * pair + e
                whole = acc[r]
                lines = []
                for i in range(4):
                    x = jnp.where(own[:, :256], whole[16 * i : 16 * i + 16], 0.0)
                    y = x[:8] + x[8:]
                    lines.append(y[:4] + y[4:])
                parts.append(jnp.concatenate(lines, axis=1))
                rowed[0, pl.ds(r, 1), :] = jnp.sum(
                    jnp.where(diagonal, peaks[r], 0.0), axis=0, keepdims=True
                )
                rowed[1, pl.ds(r, 1), :] = jnp.sum(
                    jnp.where(diagonal, totals[r], 0.0), axis=0, keepdims=True
                )
            flat[pl.ds(pl.multiple_of(8 * pair, 8), 8), :] = jnp.concatenate(parts, axis=0)

        out[...] = (
            jnp.transpose(flat[...]).astype(jnp.bfloat16).reshape(16, HEAD_DIM, rows)
        )
        place = (iota((128, rows), 1) // 4 == iota((128, rows), 0)).astype(jnp.float32)
        match = iota((64, rows), 0) % 4 == iota((64, rows), 1) % 4
        fold = (iota((16, 64), 1) // 4 == iota((16, 64), 0)).astype(jnp.float32)
        for k in range(2):
            spread = dot(jnp.transpose(rowed[k])[:64], place, NN, lax.Precision.HIGHEST)
            by_head = dot(fold, jnp.where(match, spread, 0.0), NN, lax.Precision.HIGHEST)
            for h in range(16):
                for t in range(3):
                    tops[h, 3 * k + t : 3 * k + t + 1, :] = by_head[
                        h : h + 1, 128 * t : 128 * t + 128
                    ]
        tops[:, 6:8, :] = jnp.zeros((16, 2, 128), jnp.float32)


def attend(lists, q_all, keys, values):
    pages, size, cols = keys.shape
    rows = q_all.shape[2]
    requests = rows // 4

    def page_spec(g):
        def index(i, lists):
            at = jnp.minimum(i * GROUP + g, jnp.maximum(lists[3, 0] - 1, 0))
            return (lists[0, at], 0, 0)

        return pl.BlockSpec((1, size, cols), index)

    specs = [page_spec(g) for g in range(GROUP)]
    return pl.pallas_call(
        attend_kernel,
        grid_spec=pltpu.PrefetchScalarGridSpec(
            num_scalar_prefetch=1,
            grid=(pages // GROUP,),
            in_specs=[pl.BlockSpec((16, HEAD_DIM, rows), lambda *_: (0, 0, 0))] + specs + specs,
            out_specs=[
                pl.BlockSpec((16, HEAD_DIM, rows), lambda *_: (0, 0, 0)),
                pl.BlockSpec((16, 8, 128), lambda *_: (0, 0, 0)),
            ],
            scratch_shapes=[
                pltpu.VMEM((rows, cols), jnp.float32),
                pltpu.VMEM((requests, 64, 256), jnp.float32),
                pltpu.VMEM((requests, 64, 128), jnp.float32),
                pltpu.VMEM((requests, 64, 128), jnp.float32),
                pltpu.VMEM((2, 128, 128), jnp.float32),
            ],
        ),
        out_shape=(
            jax.ShapeDtypeStruct((16, HEAD_DIM, rows), jnp.bfloat16),
            jax.ShapeDtypeStruct((16, 8, 128), jnp.float32),
        ),
        compiler_params=pltpu.CompilerParams(vmem_limit_bytes=48 * MIB),
        cost_estimate=pl.CostEstimate(
            flops=4 * pages * 64 * size * cols,
            bytes_accessed=4 * pages * size * cols,
            transcendentals=pages * 64 * size,
        ),
        name="attend",
    )(lists, q_all, *([keys] * GROUP), *([values] * GROUP))


def combine_kernel(
    parts, tops, q_all, kv, own_in, w_out, mid_all, mid_own,
    got, got_tops, far, far_tops, stage, stage_tops, attended, partial, theirs, mbuf,
    gs, gr, ts, tr, fs, fr, us, ur, as_, ar, ps, pr, ms, mr, ss, sr,
):
    s, c, to, source = places()
    rows = kv.shape[1]
    greet()
    gsem, tsem, fsem, usem, asem, psem, msem, ssem = (
        (gs, gr), (ts, tr), (fs, fr), (us, ur), (as_, ar), (ps, pr), (ms, mr), (ss, sr)
    )
    order = (1, 2, 3, 0)
    sent = []
    for d in order:
        for p in range(1, 4):
            j, near = to(d, p), to(0, p)
            sent.append(send(tops.at[j], got_tops.at[p, d], tsem, 4 * p + d, near, c))
            sent.append(send(parts.at[j], got.at[p, d], gsem, 4 * p + d, near, c))
    for copy in sent:
        copy.start()
    q = q_all[s].astype(jnp.float32)
    k = kv[:HEAD_DIM].astype(jnp.float32)
    v = kv[HEAD_DIM:].astype(jnp.float32)
    moment = iota((1, rows), 1) % 4
    fresh = []
    for back in range(4):
        moved = k if back == 0 else pltpu.roll(k, shift=back, axis=1)
        score = jnp.sum(q * moved, axis=0, keepdims=True) * (HEAD_DIM**-0.5)
        fresh.append(jnp.where(moment >= back, score, LOWEST))

    def lines(block):
        return [
            jnp.concatenate([block[3 * k + t : 3 * k + t + 1] for t in range(3)], axis=1)
            for k in range(2)
        ]

    def merge(items, extra):
        best = functools.reduce(jnp.maximum, extra + [item[0] for item in items])
        bottom = jnp.zeros((1, rows), jnp.float32)
        top = jnp.zeros((HEAD_DIM, rows), jnp.float32)
        for peak, total, block in items:
            scale = jnp.exp(peak - best)
            bottom = bottom + total * scale
            top = top + block.astype(jnp.float32) * scale
        return best, bottom, top

    for d in order:
        items = [(*lines(tops[to(d, 0)]), parts[to(d, 0)])]
        for p in range(1, 4):
            near = to(0, p)
            send(tops.at[s], got_tops.at[p, d], tsem, 4 * p + d, near, c).wait_recv()
            send(parts.at[s], got.at[p, d], gsem, 4 * p + d, near, c).wait_recv()
            items.append((*lines(got_tops[p, d]), got[p, d]))
        best, bottom, top = merge(items, [])
        if d:
            stage[d] = top.astype(jnp.bfloat16)
            for k, row in enumerate((best, bottom)):
                for t in range(3):
                    stage_tops[d, 3 * k + t : 3 * k + t + 1, :] = row[:, 128 * t : 128 * t + 128]
            stage_tops[d, 6:8, :] = jnp.zeros((2, 128), jnp.float32)
            for copy in (
                send(stage_tops.at[d], far_tops.at[d], usem, d, to(d, 0), c),
                send(stage.at[d], far.at[d], fsem, d, to(d, 0), c),
            ):
                copy.start()
                sent.append(copy)
    items = [(best, bottom, top)]
    for d in range(1, 4):
        send(stage_tops.at[d], far_tops.at[d], usem, d, source(d, 0), c).wait_recv()
        send(stage.at[d], far.at[d], fsem, d, source(d, 0), c).wait_recv()
        items.append((*lines(far_tops[d]), far[d]))
    best, bottom, top = merge(items, fresh)
    for back in range(4):
        weight = jnp.where(moment >= back, jnp.exp(fresh[back] - best), 0.0)
        bottom = bottom + weight
        moved = v if back == 0 else pltpu.roll(v, shift=back, axis=1)
        top = top + weight.astype(jnp.bfloat16).astype(jnp.float32) * moved
    attended[s] = (top / bottom).astype(jnp.bfloat16)
    whole = lambda j: attended.at[j]
    gather_open(whole, asem)
    gather_pass(whole, asem)
    for p in range(1, 4):
        for d in range(4):
            gather_take(whole, asem, d, p)
    width = w_out.shape[0]
    partial[:width] = dot(w_out[...], attended[...].reshape(16 * HEAD_DIM, rows), NN)
    partial[width:] = jnp.zeros((160 - width, rows), jnp.float32)
    here, there = pl.multiple_of(c * 80, 16), pl.multiple_of((1 - c) * 80, 16)
    swap = send(partial.at[pl.ds(there, 80), :], theirs, psem, 0, s, 1 - c)
    swap.start()
    swap.wait_recv()
    mid = own_in[pl.ds(here, 80), :].astype(jnp.float32) + partial[pl.ds(here, 80), :] + theirs[...]
    mid = mid.astype(jnp.bfloat16)
    mid_own[...] = mid
    mbuf[s, pl.ds(here, 80), :] = mid
    mine, other = halves(mbuf)
    gather_open(mine, msem)
    share_open(mine, ssem, 0, 0)
    gather_pass(mine, msem)
    for d in range(1, 4):
        share_open(mine, ssem, d, 0)
    for p in range(1, 4):
        for d in range(4):
            gather_take(mine, msem, d, p)
            share_open(mine, ssem, d, p)
    for d, p in OFFSETS:
        share_take(mine, other, ssem, d, p)
    for j in range(16):
        mid_all[width * j : width * j + width] = mbuf[j, :width]
    swap.wait_send()
    for copy in sent:
        copy.wait_send()
    gather_close(whole, asem)
    gather_close(mine, msem)
    share_close(mine, ssem)


def combine(parts, tops, q_all, kv, own_in, w_out):
    rows = kv.shape[1]
    width = w_out.shape[0]
    bf16 = jnp.bfloat16
    return pl.pallas_call(
        combine_kernel,
        out_shape=(
            jax.ShapeDtypeStruct((16 * width, rows), bf16),
            jax.ShapeDtypeStruct((80, rows), bf16),
        ),
        in_specs=[vmem()] * 6,
        out_specs=[vmem()] * 2,
        scratch_shapes=[
            pltpu.VMEM((4, 4, HEAD_DIM, rows), bf16),
            pltpu.VMEM((4, 4, 8, 128), jnp.float32),
            pltpu.VMEM((4, HEAD_DIM, rows), bf16),
            pltpu.VMEM((4, 8, 128), jnp.float32),
            pltpu.VMEM((4, HEAD_DIM, rows), bf16),
            pltpu.VMEM((4, 8, 128), jnp.float32),
            pltpu.VMEM((16, HEAD_DIM, rows), bf16),
            pltpu.VMEM((160, rows), jnp.float32),
            pltpu.VMEM((80, rows), jnp.float32),
            pltpu.VMEM((16, 160, rows), bf16),
            *pair_sems(), *pair_sems(), *pair_sems(4), *pair_sems(4),
            *pair_sems(), *pair_sems(1), *pair_sems(), *pair_sems(),
        ],
        compiler_params=pltpu.CompilerParams(
            collective_id=1, has_side_effects=True, vmem_limit_bytes=40 * MIB
        ),
        name="combine",
    )(parts, tops, q_all, kv, own_in, w_out)


def expert_kernel(
    mid, pair, down_hbm, router, routes, kv, out, keys, values,
    inv, gates, active, down, mixed, kvbuf, sem, ks, kr,
):
    e = pl.program_id(0)
    count = pl.num_programs(0)
    width_all, rows = mid.shape
    ff = pair.shape[2]
    fetch = pltpu.make_async_copy(down_hbm, down, sem)
    whole, ksem = (lambda j: kvbuf.at[j]), (ks, kr)

    @pl.when(e == 0)
    def _():
        fetch.start()
        greet()
        kvbuf[lax.axis_index("seq")] = kv[...]
        gather_open(whole, ksem)
        total = jnp.zeros((1, rows), jnp.float32)
        for i in range(16):
            at = width_all // 16
            wide = mid[at * i : at * i + at].astype(jnp.float32)
            total = total + jnp.sum(wide * wide, axis=0, keepdims=True)
        inv[...] = lax.rsqrt(total / width_all + EPSILON)
        logits = dot(router[...], mid[...], NN) * inv[...]
        which = iota(logits.shape, 0)
        first, second = which == routes[0:1], which == routes[1:2]
        share = jax.nn.sigmoid(
            jnp.sum(jnp.where(first, logits, 0.0), axis=0, keepdims=True)
            - jnp.sum(jnp.where(second, logits, 0.0), axis=0, keepdims=True)
        )
        gates[...] = jnp.where(first, share, 0.0) + jnp.where(second, 1.0 - share, 0.0)

    @pl.when(e == 1)
    def _():
        gather_pass(whole, ksem)

    expert = lax.axis_index("col") * count + e
    gate = jnp.sum(jnp.where(iota(gates.shape, 0) == expert, gates[...], 0.0), axis=0, keepdims=True)
    front = dot(pair[0, 0], mid[...], NN) * inv[...]
    back = dot(pair[0, 1], mid[...], NN) * inv[...]
    value = (front / (1.0 + jnp.exp(-front))) * back
    active[e] = jnp.transpose((value * gate)).astype(jnp.bfloat16)

    @pl.when(e == count - 1)
    def _():
        fetch.wait()
        for i in range(width_all // 256):
            at = slice(256 * i, 256 * i + 256)
            part = dot(active[0], down[0, :, at], NN)
            for k in range(1, down.shape[0]):
                part = part + dot(active[k], down[k, :, at], NN)
            mixed[at] = jnp.transpose(part).astype(jnp.bfloat16)
        width = width_all // 16
        for j in range(16):
            out[j, :width] = mixed[width * j : width * j + width]
            out[j, width:] = jnp.zeros((160 - width, rows), jnp.bfloat16)
        for p in range(1, 4):
            for d in range(4):
                gather_take(whole, ksem, d, p)
        steps, requests, _ = keys.shape
        for n in range(steps):
            at = (requests, rows)
            pick = jnp.where(iota(at, 1) == iota(at, 0) * steps + n, 1.0, 0.0).astype(jnp.bfloat16)
            for h in range(8):
                lanes = slice(128 * h, 128 * h + 128)
                for first, result in ((0, keys), (HEAD_DIM, values)):
                    two = kvbuf[2 * h : 2 * h + 2, first : first + HEAD_DIM, :]
                    result[n, :, lanes] = dot(pick, two.reshape(128, rows), NT).astype(jnp.bfloat16)
        gather_close(whole, ksem)


def experts(mid, pair, down, router, routes, kv, steps):
    width_all, rows = mid.shape
    count, _, ff, _ = pair.shape
    whole = lambda *shape: pl.BlockSpec(shape, lambda e: (0,) * len(shape))
    return pl.pallas_call(
        expert_kernel,
        grid=(count,),
        in_specs=[
            whole(width_all, rows),
            pl.BlockSpec((1, 2, ff, width_all), lambda e: (e, 0, 0, 0)),
            pl.BlockSpec(memory_space=pl.ANY),
            whole(*router.shape),
            whole(*routes.shape),
            whole(*kv.shape),
        ],
        out_specs=[
            whole(16, 160, rows),
            whole(steps, rows // steps, 16 * HEAD_DIM),
            whole(steps, rows // steps, 16 * HEAD_DIM),
        ],
        out_shape=(
            jax.ShapeDtypeStruct((16, 160, rows), jnp.bfloat16),
            jax.ShapeDtypeStruct((steps, rows // steps, 16 * HEAD_DIM), jnp.bfloat16),
            jax.ShapeDtypeStruct((steps, rows // steps, 16 * HEAD_DIM), jnp.bfloat16),
        ),
        scratch_shapes=[
            pltpu.VMEM((1, rows), jnp.float32),
            pltpu.VMEM((router.shape[0], rows), jnp.float32),
            pltpu.VMEM((count, rows, ff), jnp.bfloat16),
            pltpu.VMEM(down.shape, jnp.bfloat16),
            pltpu.VMEM((width_all, rows), jnp.bfloat16),
            pltpu.VMEM((16, *kv.shape), jnp.bfloat16),
            pltpu.SemaphoreType.DMA,
            *pair_sems(),
        ],
        compiler_params=pltpu.CompilerParams(
            collective_id=3, has_side_effects=True, vmem_limit_bytes=56 * MIB
        ),
        cost_estimate=pl.CostEstimate(
            flops=6 * count * rows * ff * width_all,
            bytes_accessed=6 * count * ff * width_all,
            transcendentals=count * rows * ff,
        ),
        name="experts",
    )(mid, pair, down, router, routes, kv)


def close_kernel(
    mixed, mid_own, out, theirs, summed, got, far, final, cs, cr, gs, gr, ds, dr, fs, fr
):
    s, c, to, source = places()
    rows = mid_own.shape[1]
    steps, width, requests = out.shape
    csem, gsem, dsem, fsem = (cs, cr), (gs, gr), (ds, dr), (fs, fr)
    greet()
    here, there = pl.multiple_of(c * 80, 16), pl.multiple_of((1 - c) * 80, 16)
    order = [(d, p) for d in (1, 2, 3, 0) for p in (3, 1, 2, 0)]
    swaps, sent = [], []
    for d, p in order:
        j = to(d, p)
        swap = send(mixed.at[j, pl.ds(there, 80), :], theirs.at[j], csem, 4 * p + d, s, 1 - c)
        swap.start()
        swaps.append(swap)
    for (d, p), swap in zip(order, swaps):
        j = to(d, p)
        swap.wait_recv()
        summed[j] = (
            mixed[j, pl.ds(here, 80), :].astype(jnp.float32) + theirs[j].astype(jnp.float32)
        ).astype(jnp.bfloat16)
        if p:
            copy = send(summed.at[j], got.at[p, d], gsem, 4 * p + d, to(0, p), c)
            copy.start()
            sent.append(copy)
    for d in (1, 2, 3, 0):
        total = summed[to(d, 0)].astype(jnp.float32)
        for p in range(1, 4):
            send(summed.at[s], got.at[p, d], gsem, 4 * p + d, to(0, p), c).wait_recv()
            total = total + got[p, d].astype(jnp.float32)
        if d:
            theirs[to(d, 0)] = total.astype(jnp.bfloat16)
            copy = send(theirs.at[to(d, 0)], far.at[d], dsem, d, to(d, 0), c)
            copy.start()
            sent.append(copy)
    total = total + mid_own[...].astype(jnp.float32)
    for d in range(1, 4):
        send(summed.at[s], far.at[d], dsem, d, source(d, 0), c).wait_recv()
        total = total + far[d].astype(jnp.float32)
    final[pl.ds(here, 80), :] = total.astype(jnp.bfloat16)
    half, other = final.at[pl.ds(here, 80), :], final.at[pl.ds(there, 80), :]
    last = send(half, half, fsem, 0, s, 1 - c)
    last.start()
    send(half, other, fsem, 0, s, 1 - c).wait_recv()
    j_at = iota((rows, requests), 0)
    for n in range(steps):
        pick = jnp.where(j_at == iota((rows, requests), 1) * steps + n, 1.0, 0.0)
        out[n] = dot(final[:width], pick.astype(jnp.bfloat16), NN).astype(jnp.bfloat16)
    last.wait_send()
    for swap in swaps:
        swap.wait_send()
    for copy in sent:
        copy.wait_send()


def close(mixed, mid_own, steps, width):
    rows = mid_own.shape[1]
    bf16 = jnp.bfloat16
    return pl.pallas_call(
        close_kernel,
        out_shape=jax.ShapeDtypeStruct((steps, width, rows // steps), bf16),
        in_specs=[vmem()] * 2,
        out_specs=vmem(),
        scratch_shapes=[
            pltpu.VMEM((16, 80, rows), bf16),
            pltpu.VMEM((16, 80, rows), bf16),
            pltpu.VMEM((4, 4, 80, rows), bf16),
            pltpu.VMEM((4, 80, rows), bf16),
            pltpu.VMEM((160, rows), bf16),
            *pair_sems(), *pair_sems(), *pair_sems(4), *pair_sems(1),
        ],
        compiler_params=pltpu.CompilerParams(
            collective_id=2, has_side_effects=True, vmem_limit_bytes=40 * MIB
        ),
        name="close",
    )(mixed, mid_own)


def fast(
    hidden,
    key_cache,
    value_cache,
    page_table,
    cache_len,
    order,
    route_ids,
    w_qkv,
    w_out,
    w_router,
    w_gate_up,
    w_down,
):
    steps, requests, width = hidden.shape
    pages, size, cols = key_cache.shape
    rows = steps * requests
    half = HEAD_DIM // 2
    frequency = jnp.exp(
        -jnp.log(10000.0) * 2.0 * jnp.arange(half, dtype=jnp.float32) / HEAD_DIM
    )
    positions = (cache_len[:, None] + jnp.arange(steps)[None, :]).reshape(rows)
    angles = frequency[:, None] * positions.astype(jnp.float32)[None, :]
    q_all, kv, own_in, lists = project(
        hidden.transpose(0, 2, 1),
        order[None, :],
        w_qkv.transpose(1, 0, 2),
        jnp.cos(angles),
        jnp.sin(angles),
        page_table,
        cache_len,
        pages,
        size,
    )
    parts, tops = attend(lists, q_all, key_cache, value_cache)
    mid, mid_own = combine(parts, tops, q_all, kv, own_in, w_out.T)
    routes = route_ids.transpose(2, 1, 0).reshape(2, rows)
    mixed, keys, values = experts(
        mid, w_gate_up.transpose(0, 2, 3, 1), w_down, w_router.T, routes, kv, steps
    )
    layer = close(mixed, mid_own, steps, width)
    return layer.transpose(0, 2, 1), keys, values


def solution(mesh):
    placed = (
        P(None, None, "seq"),
        P("seq", None, "col"),
        P("seq", None, "col"),
        P(),
        P(),
        P(),
        P(),
        P("seq", None, "col"),
        P("col", "seq"),
        P(),
        P("col", None, None, "seq"),
        P("col", "seq", None),
    )
    small = mesh.shape["seq"] == 16 and mesh.shape["col"] == 2
    return jax.shard_map(
        fast if small else local,
        mesh=mesh,
        in_specs=placed,
        out_specs=(P(None, None, "seq"), P(None, None, "col"), P(None, None, "col")),
        check_vma=False,
    )
```

```python
import functools

import jax
import jax.numpy as jnp
from jax import lax
from jax.experimental import pallas as pl
from jax.experimental.pallas import tpu as pltpu
from jax.sharding import PartitionSpec as P

HEAD_DIM = 64
EPSILON = 1e-05
LOWEST = -1e30
GROUP = 4
MIB = 1024 * 1024


def rotate(row_data, positions, head_dim):
    head_count = row_data.shape[1] // head_dim
    half_dim = head_dim // 2
    frequency = jnp.exp(
        -jnp.log(10000.0) * 2.0 * jnp.arange(half_dim, dtype=jnp.float32) / head_dim
    )
    angles = positions.astype(jnp.float32)[:, None] * frequency[None, :]
    cosine = jnp.cos(angles)[:, None, :]
    sines = jnp.sin(angles)[:, None, :]
    by_head = row_data.reshape(row_data.shape[0], head_count, head_dim)
    front_half = by_head[:, :, :half_dim]
    back_half = by_head[:, :, half_dim:]
    turned = jnp.concatenate(
        [front_half * cosine - back_half * sines, back_half * cosine + front_half * sines], axis=2
    )
    return turned.reshape(row_data.shape)


def page_kernel(owner_ref, count_ref, q_ref, k_ref, v_ref, sum_ref, peak_ref, total_ref):
    page = pl.program_id(0)
    steps, cols = q_ref.shape[1], q_ref.shape[2]
    size = k_ref.shape[1]
    padded = peak_ref.shape[2] // steps
    count = count_ref[page]
    wide = q_ref[0].astype(jnp.float32)
    own = lax.broadcasted_iota(jnp.int32, (padded, cols), 1) // HEAD_DIM == lax.broadcasted_iota(
        jnp.int32, (padded, cols), 0
    )
    spread = jnp.concatenate(
        [jnp.where(own, wide[n : n + 1, :], 0.0) for n in range(steps)], axis=0
    ).astype(jnp.bfloat16)
    scores = lax.dot_general(
        k_ref[0], spread, (((1,), (1,)), ((), ())), preferred_element_type=jnp.float32
    ) * (HEAD_DIM ** (-0.5))
    live = lax.broadcasted_iota(jnp.int32, (size, steps * padded), 0) < count
    scores = jnp.where(live, scores, LOWEST)
    peak = jnp.max(scores, axis=0, keepdims=True)
    weights = jnp.where(live, jnp.exp(scores - peak), 0.0)
    peak_ref[0] = peak
    total_ref[0] = jnp.sum(weights, axis=0, keepdims=True)
    mixed = lax.dot_general(
        weights.astype(jnp.bfloat16),
        v_ref[0],
        (((0,), (0,)), ((), ())),
        preferred_element_type=jnp.float32,
    )
    for n in range(steps):
        part = jnp.where(own, mixed[n * padded : (n + 1) * padded, :], 0.0)
        sum_ref[0, n : n + 1, :] = jnp.sum(part, axis=0, keepdims=True)


def page_parts(owner, count, query, keys, values):
    pages, size, cols = keys.shape
    steps = query.shape[1]
    heads = cols // HEAD_DIM
    padded = -(-heads // 8) * 8
    sums, peak, total = pl.pallas_call(
        page_kernel,
        grid_spec=pltpu.PrefetchScalarGridSpec(
            num_scalar_prefetch=2,
            grid=(pages,),
            in_specs=[
                pl.BlockSpec((1, steps, cols), lambda p, o, c: (o[p], 0, 0)),
                pl.BlockSpec((1, size, cols), lambda p, o, c: (p, 0, 0)),
                pl.BlockSpec((1, size, cols), lambda p, o, c: (p, 0, 0)),
            ],
            out_specs=[
                pl.BlockSpec((1, steps, cols), lambda p, o, c: (p, 0, 0)),
                pl.BlockSpec((1, 1, steps * padded), lambda p, o, c: (p, 0, 0)),
                pl.BlockSpec((1, 1, steps * padded), lambda p, o, c: (p, 0, 0)),
            ],
        ),
        out_shape=(
            jax.ShapeDtypeStruct((pages, steps, cols), jnp.float32),
            jax.ShapeDtypeStruct((pages, 1, steps * padded), jnp.float32),
            jax.ShapeDtypeStruct((pages, 1, steps * padded), jnp.float32),
        ),
        cost_estimate=pl.CostEstimate(
            flops=4 * pages * steps * padded * size * cols,
            bytes_accessed=4 * pages * size * cols,
            transcendentals=pages * steps * padded * size,
        ),
    )(owner, count, query, keys, values)
    peak = peak.reshape(pages, steps, padded)[:, :, :heads]
    total = total.reshape(pages, steps, padded)[:, :, :heads]
    return sums, peak, total


def pieces(value, count):
    out = []
    for _ in range(count):
        part = lax.reduce_precision(value, 8, 7)
        out.append(part.astype(jnp.bfloat16))
        value = value - part
    return out


def exchange(blocks):
    return lax.all_to_all(blocks, "seq", split_axis=0, concat_axis=0, tiled=True)


def col_scatter(rows):
    if lax.axis_size("col") == 2:
        half = rows.shape[0] // 2
        me = lax.axis_index("col")
        mine = lax.dynamic_slice_in_dim(rows, me * half, half, 0)
        theirs = lax.dynamic_slice_in_dim(rows, (1 - me) * half, half, 0)
        return mine + lax.ppermute(theirs, "col", [(0, 1), (1, 0)])
    return lax.psum_scatter(rows, "col", scatter_dimension=0, tiled=True)


def col_gather(rows):
    if lax.axis_size("col") == 2:
        me = lax.axis_index("col")
        other = lax.ppermute(rows, "col", [(0, 1), (1, 0)])
        first = jnp.where(me == 0, rows, other)
        second = jnp.where(me == 0, other, rows)
        return jnp.concatenate([first, second], axis=0)
    return lax.all_gather(rows, "col", axis=0, tiled=True)


def local(
    hidden,
    key_cache,
    value_cache,
    page_table,
    cache_len,
    order,
    route_ids,
    w_qkv,
    w_out,
    w_router,
    w_gate_up,
    w_down,
):
    steps, requests, width_loc = hidden.shape
    pages_loc, page_size, cols = key_cache.shape
    heads = cols // HEAD_DIM
    shards = lax.axis_size("seq")
    width_all = width_loc * shards
    experts_loc = w_gate_up.shape[0]
    ff_loc = w_gate_up.shape[3]
    expert_count = w_router.shape[1]
    expert_base = lax.axis_index("col") * experts_loc
    seq_index = lax.axis_index("seq")
    share = -(-requests // shards)
    filler = share * shards - requests
    row_count = steps * requests
    own_rows = share * steps

    placing = (order[:, None] == jnp.arange(requests)[None, :]).astype(jnp.bfloat16)
    inputs = jnp.einsum("nsc,sr->rnc", hidden, placing, preferred_element_type=jnp.float32).astype(
        jnp.bfloat16
    )
    flat_in = inputs.reshape(row_count, width_loc)
    wide_in = flat_in.astype(jnp.float32)
    squares = jnp.sum(wide_in * wide_in, axis=1, keepdims=True)
    partial = jnp.dot(
        flat_in, w_qkv.reshape(width_loc, 3 * cols), preferred_element_type=jnp.float32
    ).astype(jnp.bfloat16)
    tail = jnp.pad(jnp.concatenate(pieces(squares, 3), axis=1), ((0, 0), (0, 125)))
    sent = jnp.pad(jnp.concatenate([partial, tail], axis=1), ((0, filler * steps), (0, 0)))
    sent = sent.reshape(shards, own_rows, 3 * cols + 128)
    got = jnp.sum(exchange(sent).astype(jnp.float32), axis=0)
    inv_one = lax.rsqrt(jnp.sum(got[:, 3 * cols :], axis=1) / width_all + EPSILON)
    proj = got[:, : 3 * cols] * inv_one[:, None]
    own_len = lax.dynamic_slice_in_dim(jnp.pad(cache_len, (0, filler)), seq_index * share, share, 0)
    positions = (own_len[:, None] + jnp.arange(steps)[None, :]).reshape(own_rows)
    query = rotate(proj[:, :cols], positions, HEAD_DIM).astype(jnp.bfloat16)
    fresh_key = rotate(proj[:, cols : 2 * cols], positions, HEAD_DIM).astype(jnp.bfloat16)
    fresh_value = proj[:, 2 * cols :].astype(jnp.bfloat16)
    all_query = lax.all_gather(query, "seq", axis=0, tiled=True)[:row_count]
    all_query, fresh_pair = lax.optimization_barrier(
        (all_query, jnp.concatenate([fresh_key, fresh_value], axis=1))
    )
    all_pair = lax.all_gather(fresh_pair, "seq", axis=0, tiled=True)[:row_count]
    all_pair = all_pair.reshape(requests, steps, 2 * cols).transpose(1, 0, 2)

    needed = (cache_len + steps + page_size - 1) // page_size
    columns = jnp.arange(page_table.shape[1])
    in_use = columns[None, :] < needed[:, None]
    local_pages = page_table - seq_index * pages_loc
    page_hits = in_use[:, :, None] & (
        local_pages[:, :, None] == jnp.arange(pages_loc)[None, None, :]
    )
    owned_by = jnp.any(page_hits, axis=1)
    page_starts = jnp.sum(jnp.where(page_hits, columns[None, :, None] * page_size, 0), axis=(0, 1))
    page_len = jnp.sum(jnp.where(owned_by, cache_len[:, None], 0), axis=0)
    owner = jnp.sum(jnp.where(owned_by, jnp.arange(requests)[:, None], 0), axis=0)
    count = page_len - page_starts
    page_sums, page_peak, page_total = page_parts(
        owner.astype(jnp.int32),
        count.astype(jnp.int32),
        all_query.reshape(requests, steps, cols),
        key_cache,
        value_cache,
    )
    mask = owned_by[:, :, None, None]
    req_peak = jnp.max(jnp.where(mask, page_peak[None], LOWEST), axis=1)
    back_peak = jnp.max(jnp.where(mask, req_peak[:, None], LOWEST), axis=0)
    factor = jnp.exp(page_peak - back_peak)
    factor = jnp.where((count > 0)[:, None, None] & jnp.any(owned_by, axis=0)[:, None, None], factor, 0.0)
    owner_float = owned_by.astype(jnp.float32)
    req_total = jnp.einsum(
        "rp,pnh->rnh", owner_float, page_total * factor, precision=lax.Precision.HIGHEST
    )
    scaled = page_sums * jnp.repeat(factor, HEAD_DIM, axis=2)
    req_sums = jnp.einsum("rp,pnc->rnc", owner_float, scaled, precision=lax.Precision.HIGHEST)
    extra = jnp.concatenate(pieces(req_peak, 3) + pieces(req_total, 3), axis=2)
    spare = -extra.shape[2] % 128
    extra = jnp.pad(extra, ((0, 0), (0, 0), (0, spare)))
    sent = jnp.concatenate([req_sums.astype(jnp.bfloat16), extra], axis=2)
    sent = jnp.pad(sent, ((0, filler), (0, 0), (0, 0)))
    got = exchange(sent.reshape(shards, own_rows, sent.shape[2])).astype(jnp.float32)
    sums = got[:, :, :cols]
    bits = got[:, :, cols : cols + 6 * heads].reshape(shards, own_rows, 6, heads)
    peaks = bits[:, :, 0] + bits[:, :, 1] + bits[:, :, 2]
    totals = bits[:, :, 3] + bits[:, :, 4] + bits[:, :, 5]
    q_own = query.astype(jnp.float32).reshape(share, steps, 1, heads, HEAD_DIM)
    k_own = fresh_key.astype(jnp.float32).reshape(share, 1, steps, heads, HEAD_DIM)
    v_own = fresh_value.astype(jnp.float32).reshape(share, 1, steps, cols)
    fresh_scores = jnp.sum(q_own * k_own, axis=4) * (HEAD_DIM ** (-0.5))
    seen = (jnp.arange(steps)[None, :] <= jnp.arange(steps)[:, None])[None, :, :, None]
    fresh_scores = jnp.where(seen, fresh_scores, LOWEST)
    best = jnp.maximum(
        jnp.max(peaks, axis=0).reshape(share, steps, heads), jnp.max(fresh_scores, axis=2)
    )
    fresh_weights = jnp.where(seen, jnp.exp(fresh_scores - best[:, :, None]), 0.0)
    scale = jnp.exp(peaks - best.reshape(1, own_rows, heads))
    denominator = jnp.sum(totals * scale, axis=0) + jnp.sum(fresh_weights, axis=2).reshape(
        own_rows, heads
    )
    lowered = lax.reduce_precision(fresh_weights, 8, 7)
    numerator = jnp.sum(sums * jnp.repeat(scale, HEAD_DIM, axis=2), axis=0) + jnp.sum(
        jnp.repeat(lowered, HEAD_DIM, axis=3) * v_own, axis=2
    ).reshape(own_rows, cols)
    attended = (numerator / jnp.repeat(denominator, HEAD_DIM, axis=1)).astype(jnp.bfloat16)
    all_attended = lax.all_gather(attended, "seq", axis=0, tiled=True)[:row_count]
    projected = col_scatter(jnp.dot(all_attended, w_out, preferred_element_type=jnp.float32))
    half = projected.shape[0]
    wide_half = lax.dynamic_slice_in_dim(wide_in, lax.axis_index("col") * half, half, 0)
    residual = (wide_half + projected).astype(jnp.bfloat16)
    flat_rows = col_gather(lax.all_gather(residual, "seq", axis=1, tiled=True))

    chosen = route_ids.transpose(1, 0, 2).reshape(row_count, 2)
    expert_ids = jnp.arange(expert_count)
    w_pair = w_gate_up.reshape(experts_loc, width_all, 2 * ff_loc)
    pair_sum = jnp.einsum("rc,ecf->ref", flat_rows, w_pair, preferred_element_type=jnp.float32)
    wide_rows = flat_rows.astype(jnp.float32)
    square_sum = jnp.sum(wide_rows * wide_rows, axis=1)
    router_sum = jnp.dot(flat_rows, w_router, preferred_element_type=jnp.float32)
    inv_two = lax.rsqrt(square_sum / width_all + EPSILON)
    logits = router_sum * inv_two[:, None]
    first_pick = chosen[:, 0:1] == expert_ids[None, :]
    second_pick = chosen[:, 1:2] == expert_ids[None, :]
    first_share = jax.nn.sigmoid(
        jnp.sum(jnp.where(first_pick, logits, 0.0), axis=1)
        - jnp.sum(jnp.where(second_pick, logits, 0.0), axis=1)
    )
    gate_rows = jnp.where(first_pick, first_share[:, None], 0.0) + jnp.where(
        second_pick, 1.0 - first_share[:, None], 0.0
    )
    gate_local = lax.dynamic_slice_in_dim(gate_rows, expert_base, experts_loc, 1)
    pair_sum = pair_sum * inv_two[:, None, None]
    active = (jax.nn.silu(pair_sum[..., :ff_loc]) * pair_sum[..., ff_loc:]).astype(jnp.bfloat16)
    outputs = jnp.einsum("ref,efd->red", active, w_down, preferred_element_type=jnp.float32)
    weighted = jnp.sum(outputs * gate_local[:, :, None], axis=1)
    joined = col_scatter(weighted).astype(jnp.bfloat16)
    blocks = joined.reshape(half, shards, width_loc).transpose(1, 0, 2)
    mixture = jnp.sum(exchange(blocks).astype(jnp.float32), axis=0)
    layer_half = (residual.astype(jnp.float32) + mixture).astype(jnp.bfloat16)
    layer_rows = col_gather(layer_half).reshape(requests, steps, width_loc).transpose(1, 0, 2)
    return (layer_rows, all_pair[:, :, :cols], all_pair[:, :, cols:])


def places():
    s, c = lax.axis_index("seq"), lax.axis_index("col")
    z, y, x = s // 4, (s // 2) % 2, s % 2

    def to(dz, p):
        return ((z + dz) % 4) * 4 + ((y + p // 2) % 2) * 2 + (x + p % 2) % 2

    def source(dz, p):
        return ((z + 4 - dz) % 4) * 4 + ((y + p // 2) % 2) * 2 + (x + p % 2) % 2

    return s, c, to, source


OFFSETS = [(d, p) for p in range(4) for d in range(4)]
PEERS = OFFSETS[1:]


def send(src, dst, sems, slot, seq, col):
    return pltpu.make_async_remote_copy(
        src_ref=src,
        dst_ref=dst,
        send_sem=sems[0].at[slot],
        recv_sem=sems[1].at[slot],
        device_id=(seq, col),
        device_id_type=pl.DeviceIdType.MESH,
    )


NEAR = [(d, p) for d, p in PEERS if d == 0 or p == 0]


def greet(peers=NEAR):
    s, c, to, _ = places()
    barrier = pltpu.get_barrier_semaphore()
    for d, p in peers:
        pl.semaphore_signal(
            barrier, inc=1, device_id=(to(d, p), c), device_id_type=pl.DeviceIdType.MESH
        )
    pl.semaphore_signal(
        barrier, inc=1, device_id=(s, 1 - c), device_id_type=pl.DeviceIdType.MESH
    )
    pl.semaphore_wait(barrier, len(peers) + 1)


def gather_open(block, sems):
    s, c, to, _ = places()
    for d in range(1, 4):
        send(block(s), block(s), sems, d, to(d, 0), c).start()
    for p in range(1, 4):
        send(block(s), block(s), sems, 4 * p, to(0, p), c).start()


def gather_pass(block, sems):
    s, c, to, source = places()
    for d in range(1, 4):
        j = source(d, 0)
        send(block(j), block(j), sems, d, j, c).wait_recv()
        for p in range(1, 4):
            send(block(j), block(j), sems, 4 * p + d, to(0, p), c).start()


def gather_take(block, sems, d, p):
    _, c, _, source = places()
    j = source(d, p)
    send(block(j), block(j), sems, 4 * p + d, j, c).wait_recv()
    return j


def gather_close(block, sems):
    s, c, to, _ = places()
    for d, p in PEERS:
        send(block(s), block(s), sems, 4 * p + d, to(d, p), c).wait_send()


def share_open(block, sems, d, p):
    s, c, _, source = places()
    j = source(d, p)
    send(block(j), block(j), sems, 4 * p + d, s, 1 - c).start()


def share_take(block, other, sems, d, p):
    s, c, _, source = places()
    j = source(d, p)
    send(block(j), other(j), sems, 4 * p + d, s, 1 - c).wait_recv()
    return j


def share_close(block, sems):
    s, c, _, _ = places()
    for d, p in OFFSETS:
        send(block(s), block(s), sems, 4 * p + d, s, 1 - c).wait_send()


def halves(ref):
    c = lax.axis_index("col")
    mine, other = pl.multiple_of(c * 80, 16), pl.multiple_of((1 - c) * 80, 16)
    return (lambda j: ref.at[j, pl.ds(mine, 80), :]), (lambda j: ref.at[j, pl.ds(other, 80), :])


def dot(a, b, dims, precision=None):
    return lax.dot_general(
        a, b, (dims, ((), ())), precision=precision, preferred_element_type=jnp.float32
    )


NN = ((1,), (0,))
NT = ((1,), (1,))
TN = ((0,), (0,))


def iota(shape, axis):
    return lax.broadcasted_iota(jnp.int32, shape, axis)


def list_pages(table, lens, lists, pages, size):
    requests = table.shape[0]
    base = lax.axis_index("seq") * pages
    column = iota((1, table.shape[1]), 1)
    page = iota((pages, table.shape[1]), 0)

    def add(r, codes):
        left = lens[r] - column * size
        code = jnp.where(left > 0, r * 256 + jnp.minimum(left, size), 0)
        return codes + jnp.where(page == table[pl.ds(r, 1), :] - base, code, 0)

    codes = lax.fori_loop(0, requests, add, jnp.zeros(page.shape, jnp.int32))
    code = jnp.sum(codes.astype(jnp.float32), axis=1, keepdims=True)
    taken = jnp.where(code > 0.0, jnp.ones((1, 128), jnp.float32), 0.0)
    below = (iota((pages, pages), 1) < iota((pages, pages), 0)).astype(jnp.float32)
    before = dot(below.astype(jnp.bfloat16), taken.astype(jnp.bfloat16), NN)
    slot = iota((pages, 128), 1).astype(jnp.float32)
    placed = jnp.where(before == slot, taken, 0.0)
    at = jnp.sum(placed * iota((pages, 128), 0).astype(jnp.float32), axis=0, keepdims=True)
    packed = jnp.sum(placed * code, axis=0, keepdims=True).astype(jnp.int32)
    lists[...] = jnp.concatenate(
        [
            at.astype(jnp.int32),
            packed >> 8,
            packed & 255,
            jnp.sum(taken, axis=0, keepdims=True).astype(jnp.int32),
            jnp.zeros((4, 128), jnp.int32),
        ],
        axis=0,
    )


def project_kernel(
    pages, size, hid, order, w3, cos, sin, table, lens, q_all, kv_z, own_in, lists,
    hbuf, wsend, wrecv, hs, hr, ss, sr, ws, wr, qs, qr, ks, kr,
):
    s, c, to, source = places()
    steps, width, requests = hid.shape
    rows = steps * requests
    greet(PEERS)
    mine, other = halves(hbuf)
    hsem, ssem, wsem, qsem = (hs, hr), (ss, sr), (ws, wr), (qs, qr)
    j_at = iota((rows, requests), 0)
    same = (j_at // steps) == order[...]
    placed = jnp.zeros((width, rows), jnp.float32)
    for n in range(steps):
        pick = jnp.where(same & (j_at % steps == n), 1.0, 0.0).astype(jnp.bfloat16)
        placed = placed + dot(hid[n], pick, NT)
    own = jnp.concatenate([placed, jnp.zeros((160 - width, rows), jnp.float32)], axis=0)
    own = own.astype(jnp.bfloat16)
    own_in[...] = own
    here = pl.multiple_of(c * 80, 16)
    hbuf[s, pl.ds(here, 80), :] = own_in[pl.ds(here, 80), :]
    gather_open(mine, hsem)
    share_open(mine, ssem, 0, 0)
    low = iota((width, 128), 1) < HEAD_DIM
    low_v = iota((80, 128), 1) < HEAD_DIM
    for pair in range(8):
        at = slice(128 * pair, 128 * pair + 128)
        wq, wk, wv = [w3[i, :, at].astype(jnp.float32) for i in range(3)]
        va = wv[:80]
        vb = jnp.concatenate([wv[80:], jnp.zeros((160 - width, 128), jnp.float32)], axis=0)
        turn = functools.partial(pltpu.roll, shift=64, axis=1)
        wsend[2 * pair, :width] = jnp.where(low, wq, turn(wk)).astype(jnp.bfloat16)
        wsend[2 * pair + 1, :width] = jnp.where(low, turn(wq), wk).astype(jnp.bfloat16)
        wsend[2 * pair, width:] = jnp.where(low_v, va, turn(vb)).astype(jnp.bfloat16)
        wsend[2 * pair + 1, width:] = jnp.where(low_v, turn(va), vb).astype(jnp.bfloat16)
    for d, p in PEERS:
        j = to(d, p)
        send(wsend.at[j], wrecv.at[s], wsem, 4 * p + d, j, c).start()
    gather_pass(mine, hsem)
    for d in range(1, 4):
        share_open(mine, ssem, d, 0)
    list_pages(table, lens, lists, pages, size)
    for p in range(1, 4):
        for d in range(4):
            gather_take(mine, hsem, d, p)
            share_open(mine, ssem, d, p)
    wrecv[s] = wsend[s]
    qk = jnp.zeros((128, rows), jnp.float32)
    v0 = jnp.zeros((128, rows), jnp.float32)
    v1 = jnp.zeros((128, rows), jnp.float32)
    squares = jnp.zeros((1, rows), jnp.float32)
    for d, p in OFFSETS:
        j = share_take(mine, other, ssem, d, p)
        if d or p:
            send(wrecv.at[j], wrecv.at[j], wsem, 4 * p + d, j, c).wait_recv()
        h = hbuf[j]
        w = wrecv[j]
        qk = qk + dot(w[:width], h[:width], TN)
        v0 = v0 + dot(w[width:], h[:80], TN)
        v1 = v1 + dot(w[width : width + 64], h[80:width], TN)
        wide = h.astype(jnp.float32)
        squares = squares + jnp.sum(wide * wide, axis=0, keepdims=True)
    inv = lax.rsqrt(squares / (width * 16) + EPSILON)
    half = HEAD_DIM // 2

    def turned(part):
        a, b = part[:half], part[half:]
        return jnp.concatenate([a * cos[...] - b * sin[...], b * cos[...] + a * sin[...]], axis=0)

    q_all[s] = turned(qk[:HEAD_DIM] * inv).astype(jnp.bfloat16)
    gather_open(lambda j: q_all.at[j], qsem)
    z = s // 4
    kv_z[z, :HEAD_DIM] = turned(qk[HEAD_DIM:] * inv).astype(jnp.bfloat16)
    kv_z[z, HEAD_DIM:] = ((v0[:HEAD_DIM] + v1[HEAD_DIM:]) * inv).astype(jnp.bfloat16)
    gather_pass(lambda j: q_all.at[j], qsem)
    for d in range(1, 4):
        send(kv_z.at[z], kv_z.at[z], (ks, kr), d, to(d, 0), c).start()
    for p in range(1, 4):
        for d in range(4):
            gather_take(lambda j: q_all.at[j], qsem, d, p)
    for d in range(1, 4):
        block = kv_z.at[(z + 4 - d) % 4]
        send(block, block, (ks, kr), d, source(d, 0), c).wait_recv()
    for d in range(1, 4):
        send(kv_z.at[z], kv_z.at[z], (ks, kr), d, to(d, 0), c).wait_send()
    gather_close(mine, hsem)
    share_close(mine, ssem)
    for d, p in PEERS:
        send(wsend.at[s], wrecv.at[s], wsem, 4 * p + d, to(d, p), c).wait_send()
    gather_close(lambda j: q_all.at[j], qsem)


def vmem():
    return pl.BlockSpec(memory_space=pltpu.VMEM)


def pair_sems(count=16):
    return [pltpu.SemaphoreType.DMA((count,)), pltpu.SemaphoreType.DMA((count,))]


def project(hid, order, w3, cos, sin, table, lens, pages, size):
    steps, width, requests = hid.shape
    rows = steps * requests
    bf16 = jnp.bfloat16
    return pl.pallas_call(
        functools.partial(project_kernel, pages, size),
        out_shape=(
            jax.ShapeDtypeStruct((16, HEAD_DIM, rows), bf16),
            jax.ShapeDtypeStruct((4, 2 * HEAD_DIM, rows), bf16),
            jax.ShapeDtypeStruct((160, rows), bf16),
            jax.ShapeDtypeStruct((8, 128), jnp.int32),
        ),
        in_specs=[vmem()] * 6 + [pl.BlockSpec(memory_space=pltpu.SMEM)],
        out_specs=[vmem()] * 4,
        scratch_shapes=[
            pltpu.VMEM((16, 160, rows), bf16),
            pltpu.VMEM((16, width + 80, 128), bf16),
            pltpu.VMEM((16, width + 80, 128), bf16),
            *pair_sems(), *pair_sems(), *pair_sems(), *pair_sems(), *pair_sems(4),
        ],
        compiler_params=pltpu.CompilerParams(
            collective_id=0, has_side_effects=True, vmem_limit_bytes=58 * MIB
        ),
        name="project",
    )(hid, order, w3, cos, sin, table, lens)


def attend_kernel(lists, q_all, *refs):
    keys, values = refs[:GROUP], refs[GROUP : 2 * GROUP]
    out, tops, flat, acc, peaks, totals, rowed = refs[2 * GROUP :]
    step = pl.program_id(0)
    rows = flat.shape[0]
    requests = rows // 4
    own = (iota((16, 1024), 1) % 256) // HEAD_DIM == iota((16, 1024), 0) // 4

    @pl.when(step == 0)
    def _():
        turned = q_all[...].reshape(16 * HEAD_DIM, rows).astype(jnp.float32)
        flat[...] = jnp.transpose(turned)

        @pl.loop(0, requests, unroll=4)
        def _(r):
            acc[r] = jnp.zeros((64, 256), jnp.float32)
            peaks[r] = jnp.full((64, 128), LOWEST, jnp.float32)
            totals[r] = jnp.zeros((64, 128), jnp.float32)

    @pl.when(step * GROUP < lists[3, 0])
    def _():
        token = iota((64, 128), 1)
        found = []
        for g in range(GROUP):
            at = step * GROUP + g
            r = lists[1, at]
            live = token < lists[2, at]
            lines = [flat[pl.ds(4 * r + n, 1), :] for n in range(4)]
            spread = jnp.where(own, jnp.concatenate(lines * 4, axis=0), 0.0).astype(jnp.bfloat16)
            scores = jnp.concatenate(
                [
                    dot(spread[:, 256 * i : 256 * i + 256], keys[g][0, :, 256 * i : 256 * i + 256], NT)
                    for i in range(4)
                ],
                axis=0,
            )
            scores = jnp.where(live, scores * (HEAD_DIM**-0.5), LOWEST)
            top = jnp.max(scores, axis=1, keepdims=True)
            weights = jnp.where(live, jnp.exp(scores - top), 0.0)
            total = jnp.sum(weights, axis=1, keepdims=True)
            lowered = weights.astype(jnp.bfloat16)
            mixed = jnp.concatenate(
                [
                    dot(lowered[16 * i : 16 * i + 16], values[g][0, :, 256 * i : 256 * i + 256], NN)
                    for i in range(4)
                ],
                axis=0,
            )
            found.append((r, top, total, mixed))
        for r, top, total, mixed in found:
            old = peaks[r]
            new = jnp.maximum(old, top)
            keep = jnp.exp(old - new)
            add = jnp.exp(top - new)
            peaks[r] = new
            totals[r] = totals[r] * keep + total * add
            acc[r] = acc[r] * jnp.concatenate([keep, keep], axis=1) + mixed * jnp.concatenate(
                [add, add], axis=1
            )

    @pl.when(step == pl.num_programs(0) - 1)
    def _():
        diagonal = iota((64, 128), 0) == iota((64, 128), 1)
        rowed[...] = jnp.zeros_like(rowed)

        @pl.loop(0, requests // 2, unroll=4)
        def _(pair):
            parts = []
            for e in range(2):
                r = 2 * pair + e
                whole = acc[r]
                lines = []
                for i in range(4):
                    x = jnp.where(own[:, :256], whole[16 * i : 16 * i + 16], 0.0)
                    y = x[:8] + x[8:]
                    lines.append(y[:4] + y[4:])
                parts.append(jnp.concatenate(lines, axis=1))
                rowed[0, pl.ds(r, 1), :] = jnp.sum(
                    jnp.where(diagonal, peaks[r], 0.0), axis=0, keepdims=True
                )
                rowed[1, pl.ds(r, 1), :] = jnp.sum(
                    jnp.where(diagonal, totals[r], 0.0), axis=0, keepdims=True
                )
            flat[pl.ds(pl.multiple_of(8 * pair, 8), 8), :] = jnp.concatenate(parts, axis=0)

        out[...] = (
            jnp.transpose(flat[...]).astype(jnp.bfloat16).reshape(16, HEAD_DIM, rows)
        )
        place = (iota((128, rows), 1) // 4 == iota((128, rows), 0)).astype(jnp.float32)
        match = iota((64, rows), 0) % 4 == iota((64, rows), 1) % 4
        fold = (iota((16, 64), 1) // 4 == iota((16, 64), 0)).astype(jnp.float32)
        for k in range(2):
            spread = dot(jnp.transpose(rowed[k])[:64], place, NN, lax.Precision.HIGHEST)
            by_head = dot(fold, jnp.where(match, spread, 0.0), NN, lax.Precision.HIGHEST)
            for h in range(16):
                for t in range(3):
                    tops[h, 3 * k + t : 3 * k + t + 1, :] = by_head[
                        h : h + 1, 128 * t : 128 * t + 128
                    ]
        tops[:, 6:8, :] = jnp.zeros((16, 2, 128), jnp.float32)


def attend(lists, q_all, keys, values):
    pages, size, cols = keys.shape
    rows = q_all.shape[2]
    requests = rows // 4

    def page_spec(g):
        def index(i, lists):
            at = jnp.minimum(i * GROUP + g, jnp.maximum(lists[3, 0] - 1, 0))
            return (lists[0, at], 0, 0)

        return pl.BlockSpec((1, size, cols), index)

    specs = [page_spec(g) for g in range(GROUP)]
    return pl.pallas_call(
        attend_kernel,
        grid_spec=pltpu.PrefetchScalarGridSpec(
            num_scalar_prefetch=1,
            grid=(pages // GROUP,),
            in_specs=[pl.BlockSpec((16, HEAD_DIM, rows), lambda *_: (0, 0, 0))] + specs + specs,
            out_specs=[
                pl.BlockSpec((16, HEAD_DIM, rows), lambda *_: (0, 0, 0)),
                pl.BlockSpec((16, 8, 128), lambda *_: (0, 0, 0)),
            ],
            scratch_shapes=[
                pltpu.VMEM((rows, cols), jnp.float32),
                pltpu.VMEM((requests, 64, 256), jnp.float32),
                pltpu.VMEM((requests, 64, 128), jnp.float32),
                pltpu.VMEM((requests, 64, 128), jnp.float32),
                pltpu.VMEM((2, 128, 128), jnp.float32),
            ],
        ),
        out_shape=(
            jax.ShapeDtypeStruct((16, HEAD_DIM, rows), jnp.bfloat16),
            jax.ShapeDtypeStruct((16, 8, 128), jnp.float32),
        ),
        compiler_params=pltpu.CompilerParams(vmem_limit_bytes=48 * MIB),
        cost_estimate=pl.CostEstimate(
            flops=4 * pages * 64 * size * cols,
            bytes_accessed=4 * pages * size * cols,
            transcendentals=pages * 64 * size,
        ),
        name="attend",
    )(lists, q_all, *([keys] * GROUP), *([values] * GROUP))


def finish_kernel(
    parts, tops, q_all, kv_z, own_in, w_out, pair_hbm, down_hbm, router, routes, final,
    got, got_tops, far, far_tops, stage, stage_tops, attended, partial, theirs, mbuf,
    mid_all, pair, down, gates, active, mixed, swapped, summed, near_sums, sums, far_sums, kept,
    gs, gr, ts, tr, fs, fr, us, ur, as_, ar, ps, pr, ms, mr, ss, sr,
    cs, cr, hs, hr, ds, dr, ls, lr, pair_sem, down_sem,
):
    s, c, to, source = places()
    rows = kv_z.shape[2]
    fetches = [
        pltpu.make_async_copy(pair_hbm.at[e], pair.at[e], pair_sem.at[e])
        for e in range(pair.shape[0])
    ] + [pltpu.make_async_copy(down_hbm, down, down_sem)]
    greet()
    gsem, tsem, fsem, usem, asem, psem, msem, ssem = (
        (gs, gr), (ts, tr), (fs, fr), (us, ur), (as_, ar), (ps, pr), (ms, mr), (ss, sr)
    )
    order = (1, 2, 3, 0)
    sent = []
    for d in order:
        for p in range(1, 4):
            j, near = to(d, p), to(0, p)
            sent.append(send(tops.at[j], got_tops.at[p, d], tsem, 4 * p + d, near, c))
            sent.append(send(parts.at[j], got.at[p, d], gsem, 4 * p + d, near, c))
    for copy in sent:
        copy.start()
    for fetch in fetches:
        fetch.start()
    q = q_all[s].astype(jnp.float32)
    k = kv_z[s // 4, :HEAD_DIM].astype(jnp.float32)
    v = kv_z[s // 4, HEAD_DIM:].astype(jnp.float32)
    moment = iota((1, rows), 1) % 4
    fresh = []
    for back in range(4):
        moved = k if back == 0 else pltpu.roll(k, shift=back, axis=1)
        score = jnp.sum(q * moved, axis=0, keepdims=True) * (HEAD_DIM**-0.5)
        fresh.append(jnp.where(moment >= back, score, LOWEST))

    def lines(block):
        return [
            jnp.concatenate([block[3 * k + t : 3 * k + t + 1] for t in range(3)], axis=1)
            for k in range(2)
        ]

    def merge(items, extra):
        best = functools.reduce(jnp.maximum, extra + [item[0] for item in items])
        bottom = jnp.zeros((1, rows), jnp.float32)
        top = jnp.zeros((HEAD_DIM, rows), jnp.float32)
        for peak, total, block in items:
            scale = jnp.exp(peak - best)
            bottom = bottom + total * scale
            top = top + block.astype(jnp.float32) * scale
        return best, bottom, top

    for d in order:
        items = [(*lines(tops[to(d, 0)]), parts[to(d, 0)])]
        for p in range(1, 4):
            near = to(0, p)
            send(tops.at[s], got_tops.at[p, d], tsem, 4 * p + d, near, c).wait_recv()
            send(parts.at[s], got.at[p, d], gsem, 4 * p + d, near, c).wait_recv()
            items.append((*lines(got_tops[p, d]), got[p, d]))
        best, bottom, top = merge(items, [])
        if d:
            stage[d] = top.astype(jnp.bfloat16)
            for k, row in enumerate((best, bottom)):
                for t in range(3):
                    stage_tops[d, 3 * k + t : 3 * k + t + 1, :] = row[:, 128 * t : 128 * t + 128]
            stage_tops[d, 6:8, :] = jnp.zeros((2, 128), jnp.float32)
            for copy in (
                send(stage_tops.at[d], far_tops.at[d], usem, d, to(d, 0), c),
                send(stage.at[d], far.at[d], fsem, d, to(d, 0), c),
            ):
                copy.start()
                sent.append(copy)
    items = [(best, bottom, top)]
    for d in range(1, 4):
        send(stage_tops.at[d], far_tops.at[d], usem, d, source(d, 0), c).wait_recv()
        send(stage.at[d], far.at[d], fsem, d, source(d, 0), c).wait_recv()
        items.append((*lines(far_tops[d]), far[d]))
    best, bottom, top = merge(items, fresh)
    for back in range(4):
        weight = jnp.where(moment >= back, jnp.exp(fresh[back] - best), 0.0)
        bottom = bottom + weight
        moved = v if back == 0 else pltpu.roll(v, shift=back, axis=1)
        top = top + weight.astype(jnp.bfloat16).astype(jnp.float32) * moved
    attended[s] = (top / bottom).astype(jnp.bfloat16)
    whole = lambda j: attended.at[j]
    gather_open(whole, asem)
    gather_pass(whole, asem)
    for p in range(1, 4):
        for d in range(4):
            gather_take(whole, asem, d, p)
    width = w_out.shape[0]
    partial[:width] = dot(w_out[...], attended[...].reshape(16 * HEAD_DIM, rows), NN)
    partial[width:] = jnp.zeros((160 - width, rows), jnp.float32)
    here, there = pl.multiple_of(c * 80, 16), pl.multiple_of((1 - c) * 80, 16)
    swap = send(partial.at[pl.ds(there, 80), :], theirs, psem, 0, s, 1 - c)
    swap.start()
    swap.wait_recv()
    mid = own_in[pl.ds(here, 80), :].astype(jnp.float32) + partial[pl.ds(here, 80), :] + theirs[...]
    mid = mid.astype(jnp.bfloat16)
    mbuf[s, pl.ds(here, 80), :] = mid
    mine, other = halves(mbuf)
    gather_open(mine, msem)
    share_open(mine, ssem, 0, 0)
    gather_pass(mine, msem)
    for d in range(1, 4):
        share_open(mine, ssem, d, 0)
    for p in range(1, 4):
        for d in range(4):
            gather_take(mine, msem, d, p)
            share_open(mine, ssem, d, p)
    for d, p in OFFSETS:
        share_take(mine, other, ssem, d, p)
    squares = jnp.zeros((1, rows), jnp.float32)
    for j in range(16):
        block = mbuf[j, :width]
        mid_all[width * j : width * j + width] = block
        wide = block.astype(jnp.float32)
        squares = squares + jnp.sum(wide * wide, axis=0, keepdims=True)

    inv = lax.rsqrt(squares / (width * 16) + EPSILON)
    logits = dot(router[...], mid_all[...], NN) * inv
    which = iota(logits.shape, 0)
    first, second = which == routes[0:1], which == routes[1:2]
    share = jax.nn.sigmoid(
        jnp.sum(jnp.where(first, logits, 0.0), axis=0, keepdims=True)
        - jnp.sum(jnp.where(second, logits, 0.0), axis=0, keepdims=True)
    )
    gates[...] = jnp.where(first, share, 0.0) + jnp.where(second, 1.0 - share, 0.0)
    count = pair.shape[0]

    def expert(e):
        pltpu.make_async_copy(pair_hbm.at[e], pair.at[e], pair_sem.at[e]).wait()
        mask = iota(gates.shape, 0) == c * count + e
        gate = jnp.sum(jnp.where(mask, gates[...], 0.0), axis=0, keepdims=True)
        front = dot(pair[e, 0], mid_all[...], NN) * inv
        back = dot(pair[e, 1], mid_all[...], NN) * inv
        value = (front / (1.0 + jnp.exp(-front))) * back
        active[e] = jnp.transpose(value * gate).astype(jnp.bfloat16)

    @pl.loop(0, count)
    def _(e):
        expert(e)

    fetches[-1].wait()
    csem, hsem, lsem = (cs, cr), (hs, hr), (ls, lr)
    step = 384
    z = s // 4
    here_seq = s % 4

    def mix(i):
        at = slice(step * i, step * i + step)
        part = dot(active[0], down[0, :, at], NN)
        for k in range(1, count):
            part = part + dot(active[k], down[k, :, at], NN)
        mixed[at] = jnp.transpose(part).astype(jnp.bfloat16)

    def trade(half):
        for j in range(8 * half, 8 * half + 8):
            at = width * j

            @pl.when(c == 0)
            def _(j=j, at=at):
                swapped[0, j, : width - 80] = mixed[at + 80 : at + width]

            @pl.when(c == 1)
            def _(j=j, at=at):
                swapped[0, j] = mixed[at : at + 80]

            send(swapped.at[0, j], swapped.at[1, j], csem, j, s, 1 - c).start()

    def spread(zt):
        for k in range(4):
            j = 4 * zt + k
            send(swapped.at[0, j], swapped.at[1, j], csem, j, s, 1 - c).wait_recv()
            at = width * j

            @pl.when(c == 0)
            def _(j=j, at=at):
                mine_part = mixed[at : at + 80].astype(jnp.float32)
                summed[j] = (mine_part + swapped[1, j].astype(jnp.float32)).astype(jnp.bfloat16)

            @pl.when(c == 1)
            def _(j=j, at=at):
                mine_part = mixed[at + 80 : at + width].astype(jnp.float32)
                rest = width - 80
                summed[j, :rest] = (mine_part + swapped[1, j, :rest].astype(jnp.float32)).astype(
                    jnp.bfloat16
                )

        for p in (3, 1, 2):
            near = to(0, p)
            send(
                summed.at[4 * zt + near % 4], near_sums.at[p, zt], hsem, 4 * p + zt, near, c
            ).start()

    for i in range(3):
        mix(i)
    trade(0)
    mix(3)
    spread(0)
    mix(4)
    spread(1)
    mix(5)
    trade(1)
    spread(2)
    spread(3)

    def far_copy(zt, zs):
        return pltpu.make_async_remote_copy(
            src_ref=sums.at[zt],
            dst_ref=far_sums.at[zs],
            send_sem=ds.at[zt],
            recv_sem=dr.at[zs],
            device_id=(4 * zt + here_seq, c),
            device_id_type=pl.DeviceIdType.MESH,
        )

    for zt in range(4):
        total = summed[4 * zt + here_seq].astype(jnp.float32)
        for p in range(1, 4):
            send(summed.at[0], near_sums.at[p, zt], hsem, 4 * p + zt, to(0, p), c).wait_recv()
            total = total + near_sums[p, zt].astype(jnp.float32)

        @pl.when(zt == z)
        def _(total=total):
            kept[...] = total

        @pl.when(zt != z)
        def _(total=total, zt=zt):
            sums[zt] = total.astype(jnp.bfloat16)
            far_copy(zt, z).start()

    total = kept[...] + mbuf[s, pl.ds(here, 80), :].astype(jnp.float32)
    for d in range(1, 4):
        zs = (z + d) % 4
        far_copy(zs, zs).wait_recv()
        total = total + far_sums[zs].astype(jnp.float32)
    final[pl.ds(here, 80), :] = total.astype(jnp.bfloat16)
    half, rest = final.at[pl.ds(here, 80), :], final.at[pl.ds(there, 80), :]
    last = send(half, half, lsem, 0, s, 1 - c)
    last.start()
    send(half, rest, lsem, 0, s, 1 - c).wait_recv()
    last.wait_send()
    swap.wait_send()
    for copy in sent:
        copy.wait_send()
    gather_close(whole, asem)
    gather_close(mine, msem)
    share_close(mine, ssem)
    for j in range(16):
        send(swapped.at[0, j], swapped.at[1, j], csem, j, s, 1 - c).wait_send()
    for p in range(1, 4):
        for zt in range(4):
            send(summed.at[0], near_sums.at[p, zt], hsem, 4 * p + zt, to(0, p), c).wait_send()
    for d in range(1, 4):
        far_copy((z + d) % 4, z).wait_send()


def finish(parts, tops, q_all, kv_z, own_in, w_out, pair, down, router, routes):
    rows = kv_z.shape[2]
    width = w_out.shape[0]
    bf16, f32 = jnp.bfloat16, jnp.float32
    anywhere = pl.BlockSpec(memory_space=pl.ANY)
    return pl.pallas_call(
        finish_kernel,
        out_shape=jax.ShapeDtypeStruct((160, rows), bf16),
        in_specs=[vmem()] * 6 + [anywhere] * 2 + [vmem()] * 2,
        out_specs=vmem(),
        scratch_shapes=[
            pltpu.VMEM((4, 4, HEAD_DIM, rows), bf16),
            pltpu.VMEM((4, 4, 8, 128), f32),
            pltpu.VMEM((4, HEAD_DIM, rows), bf16),
            pltpu.VMEM((4, 8, 128), f32),
            pltpu.VMEM((4, HEAD_DIM, rows), bf16),
            pltpu.VMEM((4, 8, 128), f32),
            pltpu.VMEM((16, HEAD_DIM, rows), bf16),
            pltpu.VMEM((160, rows), f32),
            pltpu.VMEM((80, rows), f32),
            pltpu.VMEM((16, 160, rows), bf16),
            pltpu.VMEM((16 * width, rows), bf16),
            pltpu.VMEM(pair.shape, bf16),
            pltpu.VMEM(down.shape, bf16),
            pltpu.VMEM((router.shape[0], rows), f32),
            pltpu.VMEM((pair.shape[0], rows, pair.shape[2]), bf16),
            pltpu.VMEM((16 * width, rows), bf16),
            pltpu.VMEM((2, 16, 80, rows), bf16),
            pltpu.VMEM((16, 80, rows), bf16),
            pltpu.VMEM((4, 4, 80, rows), bf16),
            pltpu.VMEM((4, 80, rows), bf16),
            pltpu.VMEM((4, 80, rows), bf16),
            pltpu.VMEM((80, rows), f32),
            *pair_sems(), *pair_sems(), *pair_sems(4), *pair_sems(4),
            *pair_sems(), *pair_sems(1), *pair_sems(), *pair_sems(),
            *pair_sems(), *pair_sems(), *pair_sems(4), *pair_sems(1),
            pltpu.SemaphoreType.DMA((pair.shape[0],)), pltpu.SemaphoreType.DMA,
        ],
        compiler_params=pltpu.CompilerParams(
            collective_id=1, has_side_effects=True, vmem_limit_bytes=58 * MIB
        ),
        name="finish",
    )(parts, tops, q_all, kv_z, own_in, w_out, pair, down, router, routes)


def unpack_kernel(*refs):
    planes, (final, layer, keys, values) = refs[:4], refs[4:]
    steps, requests, _ = keys.shape
    rows = planes[0].shape[2]
    at = (rows, rows)
    row = iota(at, 0)
    pick = iota(at, 1) == (row % requests) * steps + row // requests
    pick = jnp.where(pick, 1.0, 0.0).astype(jnp.bfloat16)

    @pl.when(pl.program_id(0) == 0)
    def _():
        width = layer.shape[1]
        done = dot(final[...], pick, NT).astype(jnp.bfloat16)
        for n in range(steps):
            layer[n] = done[:width, n * requests : n * requests + requests]

    mine = lax.axis_index("seq") % 4
    heads = []
    for k in range(4):
        offset = ((k // 2 + 2 - mine // 2) % 2) * 2 + (k + 2 - mine) % 2
        block = planes[0][0]
        for p in range(1, 4):
            block = jnp.where(offset == p, planes[p][0], block)
        heads.append(block)
    for first, result in ((0, keys), (HEAD_DIM, values)):
        four = jnp.concatenate([head[first : first + HEAD_DIM] for head in heads], axis=0)
        done = dot(pick, four, NT).astype(jnp.bfloat16)
        for n in range(steps):
            result[n] = done[n * requests : n * requests + requests]


def unpack(planes, final, steps, width):
    _, both, rows = planes[0].shape
    shape = (steps, rows // steps, 16 * HEAD_DIM)
    first = (steps, width, rows // steps)
    spec = pl.BlockSpec((*shape[:2], 4 * HEAD_DIM), lambda z: (0, 0, z))
    return pl.pallas_call(
        unpack_kernel,
        grid=(4,),
        in_specs=[pl.BlockSpec((1, both, rows), lambda z: (z, 0, 0))] * 4
        + [pl.BlockSpec(final.shape, lambda z: (0, 0))],
        out_specs=[pl.BlockSpec(first, lambda z: (0, 0, 0)), spec, spec],
        out_shape=(
            jax.ShapeDtypeStruct(first, jnp.bfloat16),
            jax.ShapeDtypeStruct(shape, jnp.bfloat16),
            jax.ShapeDtypeStruct(shape, jnp.bfloat16),
        ),
        cost_estimate=pl.CostEstimate(
            flops=4 * rows * rows * shape[2], bytes_accessed=8 * rows * shape[2], transcendentals=0
        ),
        name="unpack",
    )(*planes, final)


def plane_shift(block, p):
    pairs = [(i, i // 4 * 4 + (i % 4 ^ p)) for i in range(16)]
    return lax.ppermute(block, "seq", pairs)


def fast(
    hidden,
    key_cache,
    value_cache,
    page_table,
    cache_len,
    order,
    route_ids,
    w_qkv,
    w_out,
    w_router,
    w_gate_up,
    w_down,
):
    steps, requests, width = hidden.shape
    pages, size, cols = key_cache.shape
    rows = steps * requests
    half = HEAD_DIM // 2
    frequency = jnp.exp(
        -jnp.log(10000.0) * 2.0 * jnp.arange(half, dtype=jnp.float32) / HEAD_DIM
    )
    positions = (cache_len[:, None] + jnp.arange(steps)[None, :]).reshape(rows)
    angles = frequency[:, None] * positions.astype(jnp.float32)[None, :]
    q_all, kv_z, own_in, lists = project(
        hidden.transpose(0, 2, 1),
        order[None, :],
        w_qkv.transpose(1, 0, 2),
        jnp.cos(angles),
        jnp.sin(angles),
        page_table,
        cache_len,
        pages,
        size,
    )
    planes = [kv_z] + [plane_shift(kv_z, p) for p in range(1, 4)]
    parts, tops = attend(lists, q_all, key_cache, value_cache)
    routes = route_ids.transpose(2, 1, 0).reshape(2, rows)
    final = finish(
        parts, tops, q_all, kv_z, own_in, w_out.T,
        w_gate_up.transpose(0, 2, 3, 1), w_down, w_router.T, routes,
    )
    layer, keys, values = unpack(planes, final, steps, width)
    return layer.transpose(0, 2, 1), keys, values


def solution(mesh):
    placed = (
        P(None, None, "seq"),
        P("seq", None, "col"),
        P("seq", None, "col"),
        P(),
        P(),
        P(),
        P(),
        P("seq", None, "col"),
        P("col", "seq"),
        P(),
        P("col", None, None, "seq"),
        P("col", "seq", None),
    )
    small = mesh.shape["seq"] == 16 and mesh.shape["col"] == 2
    return jax.shard_map(
        fast if small else local,
        mesh=mesh,
        in_specs=placed,
        out_specs=(P(None, None, "seq"), P(None, None, "col"), P(None, None, "col")),
        check_vma=False,
    )
```

```python
import functools

import jax
import jax.numpy as jnp
from jax import lax
from jax.experimental import pallas as pl
from jax.experimental.pallas import tpu as pltpu
from jax.sharding import PartitionSpec as P

HEAD_DIM = 64
EPSILON = 1e-05
LOWEST = -1e30
GROUP = 4
MIB = 1024 * 1024


def rotate(row_data, positions, head_dim):
    head_count = row_data.shape[1] // head_dim
    half_dim = head_dim // 2
    frequency = jnp.exp(
        -jnp.log(10000.0) * 2.0 * jnp.arange(half_dim, dtype=jnp.float32) / head_dim
    )
    angles = positions.astype(jnp.float32)[:, None] * frequency[None, :]
    cosine = jnp.cos(angles)[:, None, :]
    sines = jnp.sin(angles)[:, None, :]
    by_head = row_data.reshape(row_data.shape[0], head_count, head_dim)
    front_half = by_head[:, :, :half_dim]
    back_half = by_head[:, :, half_dim:]
    turned = jnp.concatenate(
        [front_half * cosine - back_half * sines, back_half * cosine + front_half * sines], axis=2
    )
    return turned.reshape(row_data.shape)


def page_kernel(owner_ref, count_ref, q_ref, k_ref, v_ref, sum_ref, peak_ref, total_ref):
    page = pl.program_id(0)
    steps, cols = q_ref.shape[1], q_ref.shape[2]
    size = k_ref.shape[1]
    padded = peak_ref.shape[2] // steps
    count = count_ref[page]
    wide = q_ref[0].astype(jnp.float32)
    own = lax.broadcasted_iota(jnp.int32, (padded, cols), 1) // HEAD_DIM == lax.broadcasted_iota(
        jnp.int32, (padded, cols), 0
    )
    spread = jnp.concatenate(
        [jnp.where(own, wide[n : n + 1, :], 0.0) for n in range(steps)], axis=0
    ).astype(jnp.bfloat16)
    scores = lax.dot_general(
        k_ref[0], spread, (((1,), (1,)), ((), ())), preferred_element_type=jnp.float32
    ) * (HEAD_DIM ** (-0.5))
    live = lax.broadcasted_iota(jnp.int32, (size, steps * padded), 0) < count
    scores = jnp.where(live, scores, LOWEST)
    peak = jnp.max(scores, axis=0, keepdims=True)
    weights = jnp.where(live, jnp.exp(scores - peak), 0.0)
    peak_ref[0] = peak
    total_ref[0] = jnp.sum(weights, axis=0, keepdims=True)
    mixed = lax.dot_general(
        weights.astype(jnp.bfloat16),
        v_ref[0],
        (((0,), (0,)), ((), ())),
        preferred_element_type=jnp.float32,
    )
    for n in range(steps):
        part = jnp.where(own, mixed[n * padded : (n + 1) * padded, :], 0.0)
        sum_ref[0, n : n + 1, :] = jnp.sum(part, axis=0, keepdims=True)


def page_parts(owner, count, query, keys, values):
    pages, size, cols = keys.shape
    steps = query.shape[1]
    heads = cols // HEAD_DIM
    padded = -(-heads // 8) * 8
    sums, peak, total = pl.pallas_call(
        page_kernel,
        grid_spec=pltpu.PrefetchScalarGridSpec(
            num_scalar_prefetch=2,
            grid=(pages,),
            in_specs=[
                pl.BlockSpec((1, steps, cols), lambda p, o, c: (o[p], 0, 0)),
                pl.BlockSpec((1, size, cols), lambda p, o, c: (p, 0, 0)),
                pl.BlockSpec((1, size, cols), lambda p, o, c: (p, 0, 0)),
            ],
            out_specs=[
                pl.BlockSpec((1, steps, cols), lambda p, o, c: (p, 0, 0)),
                pl.BlockSpec((1, 1, steps * padded), lambda p, o, c: (p, 0, 0)),
                pl.BlockSpec((1, 1, steps * padded), lambda p, o, c: (p, 0, 0)),
            ],
        ),
        out_shape=(
            jax.ShapeDtypeStruct((pages, steps, cols), jnp.float32),
            jax.ShapeDtypeStruct((pages, 1, steps * padded), jnp.float32),
            jax.ShapeDtypeStruct((pages, 1, steps * padded), jnp.float32),
        ),
        cost_estimate=pl.CostEstimate(
            flops=4 * pages * steps * padded * size * cols,
            bytes_accessed=4 * pages * size * cols,
            transcendentals=pages * steps * padded * size,
        ),
    )(owner, count, query, keys, values)
    peak = peak.reshape(pages, steps, padded)[:, :, :heads]
    total = total.reshape(pages, steps, padded)[:, :, :heads]
    return sums, peak, total


def pieces(value, count):
    out = []
    for _ in range(count):
        part = lax.reduce_precision(value, 8, 7)
        out.append(part.astype(jnp.bfloat16))
        value = value - part
    return out


def exchange(blocks):
    return lax.all_to_all(blocks, "seq", split_axis=0, concat_axis=0, tiled=True)


def col_scatter(rows):
    if lax.axis_size("col") == 2:
        half = rows.shape[0] // 2
        me = lax.axis_index("col")
        mine = lax.dynamic_slice_in_dim(rows, me * half, half, 0)
        theirs = lax.dynamic_slice_in_dim(rows, (1 - me) * half, half, 0)
        return mine + lax.ppermute(theirs, "col", [(0, 1), (1, 0)])
    return lax.psum_scatter(rows, "col", scatter_dimension=0, tiled=True)


def col_gather(rows):
    if lax.axis_size("col") == 2:
        me = lax.axis_index("col")
        other = lax.ppermute(rows, "col", [(0, 1), (1, 0)])
        first = jnp.where(me == 0, rows, other)
        second = jnp.where(me == 0, other, rows)
        return jnp.concatenate([first, second], axis=0)
    return lax.all_gather(rows, "col", axis=0, tiled=True)


def local(
    hidden,
    key_cache,
    value_cache,
    page_table,
    cache_len,
    order,
    route_ids,
    w_qkv,
    w_out,
    w_router,
    w_gate_up,
    w_down,
):
    steps, requests, width_loc = hidden.shape
    pages_loc, page_size, cols = key_cache.shape
    heads = cols // HEAD_DIM
    shards = lax.axis_size("seq")
    width_all = width_loc * shards
    experts_loc = w_gate_up.shape[0]
    ff_loc = w_gate_up.shape[3]
    expert_count = w_router.shape[1]
    expert_base = lax.axis_index("col") * experts_loc
    seq_index = lax.axis_index("seq")
    share = -(-requests // shards)
    filler = share * shards - requests
    row_count = steps * requests
    own_rows = share * steps

    placing = (order[:, None] == jnp.arange(requests)[None, :]).astype(jnp.bfloat16)
    inputs = jnp.einsum("nsc,sr->rnc", hidden, placing, preferred_element_type=jnp.float32).astype(
        jnp.bfloat16
    )
    flat_in = inputs.reshape(row_count, width_loc)
    wide_in = flat_in.astype(jnp.float32)
    squares = jnp.sum(wide_in * wide_in, axis=1, keepdims=True)
    partial = jnp.dot(
        flat_in, w_qkv.reshape(width_loc, 3 * cols), preferred_element_type=jnp.float32
    ).astype(jnp.bfloat16)
    tail = jnp.pad(jnp.concatenate(pieces(squares, 3), axis=1), ((0, 0), (0, 125)))
    sent = jnp.pad(jnp.concatenate([partial, tail], axis=1), ((0, filler * steps), (0, 0)))
    sent = sent.reshape(shards, own_rows, 3 * cols + 128)
    got = jnp.sum(exchange(sent).astype(jnp.float32), axis=0)
    inv_one = lax.rsqrt(jnp.sum(got[:, 3 * cols :], axis=1) / width_all + EPSILON)
    proj = got[:, : 3 * cols] * inv_one[:, None]
    own_len = lax.dynamic_slice_in_dim(jnp.pad(cache_len, (0, filler)), seq_index * share, share, 0)
    positions = (own_len[:, None] + jnp.arange(steps)[None, :]).reshape(own_rows)
    query = rotate(proj[:, :cols], positions, HEAD_DIM).astype(jnp.bfloat16)
    fresh_key = rotate(proj[:, cols : 2 * cols], positions, HEAD_DIM).astype(jnp.bfloat16)
    fresh_value = proj[:, 2 * cols :].astype(jnp.bfloat16)
    all_query = lax.all_gather(query, "seq", axis=0, tiled=True)[:row_count]
    all_query, fresh_pair = lax.optimization_barrier(
        (all_query, jnp.concatenate([fresh_key, fresh_value], axis=1))
    )
    all_pair = lax.all_gather(fresh_pair, "seq", axis=0, tiled=True)[:row_count]
    all_pair = all_pair.reshape(requests, steps, 2 * cols).transpose(1, 0, 2)

    needed = (cache_len + steps + page_size - 1) // page_size
    columns = jnp.arange(page_table.shape[1])
    in_use = columns[None, :] < needed[:, None]
    local_pages = page_table - seq_index * pages_loc
    page_hits = in_use[:, :, None] & (
        local_pages[:, :, None] == jnp.arange(pages_loc)[None, None, :]
    )
    owned_by = jnp.any(page_hits, axis=1)
    page_starts = jnp.sum(jnp.where(page_hits, columns[None, :, None] * page_size, 0), axis=(0, 1))
    page_len = jnp.sum(jnp.where(owned_by, cache_len[:, None], 0), axis=0)
    owner = jnp.sum(jnp.where(owned_by, jnp.arange(requests)[:, None], 0), axis=0)
    count = page_len - page_starts
    page_sums, page_peak, page_total = page_parts(
        owner.astype(jnp.int32),
        count.astype(jnp.int32),
        all_query.reshape(requests, steps, cols),
        key_cache,
        value_cache,
    )
    mask = owned_by[:, :, None, None]
    req_peak = jnp.max(jnp.where(mask, page_peak[None], LOWEST), axis=1)
    back_peak = jnp.max(jnp.where(mask, req_peak[:, None], LOWEST), axis=0)
    factor = jnp.exp(page_peak - back_peak)
    factor = jnp.where((count > 0)[:, None, None] & jnp.any(owned_by, axis=0)[:, None, None], factor, 0.0)
    owner_float = owned_by.astype(jnp.float32)
    req_total = jnp.einsum(
        "rp,pnh->rnh", owner_float, page_total * factor, precision=lax.Precision.HIGHEST
    )
    scaled = page_sums * jnp.repeat(factor, HEAD_DIM, axis=2)
    req_sums = jnp.einsum("rp,pnc->rnc", owner_float, scaled, precision=lax.Precision.HIGHEST)
    extra = jnp.concatenate(pieces(req_peak, 3) + pieces(req_total, 3), axis=2)
    spare = -extra.shape[2] % 128
    extra = jnp.pad(extra, ((0, 0), (0, 0), (0, spare)))
    sent = jnp.concatenate([req_sums.astype(jnp.bfloat16), extra], axis=2)
    sent = jnp.pad(sent, ((0, filler), (0, 0), (0, 0)))
    got = exchange(sent.reshape(shards, own_rows, sent.shape[2])).astype(jnp.float32)
    sums = got[:, :, :cols]
    bits = got[:, :, cols : cols + 6 * heads].reshape(shards, own_rows, 6, heads)
    peaks = bits[:, :, 0] + bits[:, :, 1] + bits[:, :, 2]
    totals = bits[:, :, 3] + bits[:, :, 4] + bits[:, :, 5]
    q_own = query.astype(jnp.float32).reshape(share, steps, 1, heads, HEAD_DIM)
    k_own = fresh_key.astype(jnp.float32).reshape(share, 1, steps, heads, HEAD_DIM)
    v_own = fresh_value.astype(jnp.float32).reshape(share, 1, steps, cols)
    fresh_scores = jnp.sum(q_own * k_own, axis=4) * (HEAD_DIM ** (-0.5))
    seen = (jnp.arange(steps)[None, :] <= jnp.arange(steps)[:, None])[None, :, :, None]
    fresh_scores = jnp.where(seen, fresh_scores, LOWEST)
    best = jnp.maximum(
        jnp.max(peaks, axis=0).reshape(share, steps, heads), jnp.max(fresh_scores, axis=2)
    )
    fresh_weights = jnp.where(seen, jnp.exp(fresh_scores - best[:, :, None]), 0.0)
    scale = jnp.exp(peaks - best.reshape(1, own_rows, heads))
    denominator = jnp.sum(totals * scale, axis=0) + jnp.sum(fresh_weights, axis=2).reshape(
        own_rows, heads
    )
    lowered = lax.reduce_precision(fresh_weights, 8, 7)
    numerator = jnp.sum(sums * jnp.repeat(scale, HEAD_DIM, axis=2), axis=0) + jnp.sum(
        jnp.repeat(lowered, HEAD_DIM, axis=3) * v_own, axis=2
    ).reshape(own_rows, cols)
    attended = (numerator / jnp.repeat(denominator, HEAD_DIM, axis=1)).astype(jnp.bfloat16)
    all_attended = lax.all_gather(attended, "seq", axis=0, tiled=True)[:row_count]
    projected = col_scatter(jnp.dot(all_attended, w_out, preferred_element_type=jnp.float32))
    half = projected.shape[0]
    wide_half = lax.dynamic_slice_in_dim(wide_in, lax.axis_index("col") * half, half, 0)
    residual = (wide_half + projected).astype(jnp.bfloat16)
    flat_rows = col_gather(lax.all_gather(residual, "seq", axis=1, tiled=True))

    chosen = route_ids.transpose(1, 0, 2).reshape(row_count, 2)
    expert_ids = jnp.arange(expert_count)
    w_pair = w_gate_up.reshape(experts_loc, width_all, 2 * ff_loc)
    pair_sum = jnp.einsum("rc,ecf->ref", flat_rows, w_pair, preferred_element_type=jnp.float32)
    wide_rows = flat_rows.astype(jnp.float32)
    square_sum = jnp.sum(wide_rows * wide_rows, axis=1)
    router_sum = jnp.dot(flat_rows, w_router, preferred_element_type=jnp.float32)
    inv_two = lax.rsqrt(square_sum / width_all + EPSILON)
    logits = router_sum * inv_two[:, None]
    first_pick = chosen[:, 0:1] == expert_ids[None, :]
    second_pick = chosen[:, 1:2] == expert_ids[None, :]
    first_share = jax.nn.sigmoid(
        jnp.sum(jnp.where(first_pick, logits, 0.0), axis=1)
        - jnp.sum(jnp.where(second_pick, logits, 0.0), axis=1)
    )
    gate_rows = jnp.where(first_pick, first_share[:, None], 0.0) + jnp.where(
        second_pick, 1.0 - first_share[:, None], 0.0
    )
    gate_local = lax.dynamic_slice_in_dim(gate_rows, expert_base, experts_loc, 1)
    pair_sum = pair_sum * inv_two[:, None, None]
    active = (jax.nn.silu(pair_sum[..., :ff_loc]) * pair_sum[..., ff_loc:]).astype(jnp.bfloat16)
    outputs = jnp.einsum("ref,efd->red", active, w_down, preferred_element_type=jnp.float32)
    weighted = jnp.sum(outputs * gate_local[:, :, None], axis=1)
    joined = col_scatter(weighted).astype(jnp.bfloat16)
    blocks = joined.reshape(half, shards, width_loc).transpose(1, 0, 2)
    mixture = jnp.sum(exchange(blocks).astype(jnp.float32), axis=0)
    layer_half = (residual.astype(jnp.float32) + mixture).astype(jnp.bfloat16)
    layer_rows = col_gather(layer_half).reshape(requests, steps, width_loc).transpose(1, 0, 2)
    return (layer_rows, all_pair[:, :, :cols], all_pair[:, :, cols:])


def places():
    s, c = lax.axis_index("seq"), lax.axis_index("col")
    z, y, x = s // 4, (s // 2) % 2, s % 2

    def to(dz, p):
        return ((z + dz) % 4) * 4 + ((y + p // 2) % 2) * 2 + (x + p % 2) % 2

    def source(dz, p):
        return ((z + 4 - dz) % 4) * 4 + ((y + p // 2) % 2) * 2 + (x + p % 2) % 2

    return s, c, to, source


OFFSETS = [(d, p) for p in range(4) for d in range(4)]
PEERS = OFFSETS[1:]


def send(src, dst, sems, slot, seq, col):
    return pltpu.make_async_remote_copy(
        src_ref=src,
        dst_ref=dst,
        send_sem=sems[0].at[slot],
        recv_sem=sems[1].at[slot],
        device_id=(seq, col),
        device_id_type=pl.DeviceIdType.MESH,
    )


NEAR = [(d, p) for d, p in PEERS if d == 0 or p == 0]


def greet(peers=NEAR):
    s, c, to, _ = places()
    barrier = pltpu.get_barrier_semaphore()
    for d, p in peers:
        pl.semaphore_signal(
            barrier, inc=1, device_id=(to(d, p), c), device_id_type=pl.DeviceIdType.MESH
        )
    pl.semaphore_signal(
        barrier, inc=1, device_id=(s, 1 - c), device_id_type=pl.DeviceIdType.MESH
    )
    pl.semaphore_wait(barrier, len(peers) + 1)


def gather_open(block, sems):
    s, c, to, _ = places()
    for d in range(1, 4):
        send(block(s), block(s), sems, d, to(d, 0), c).start()
    for p in range(1, 4):
        send(block(s), block(s), sems, 4 * p, to(0, p), c).start()


def gather_pass(block, sems):
    s, c, to, source = places()
    for d in range(1, 4):
        j = source(d, 0)
        send(block(j), block(j), sems, d, j, c).wait_recv()
        for p in range(1, 4):
            send(block(j), block(j), sems, 4 * p + d, to(0, p), c).start()


def gather_take(block, sems, d, p):
    _, c, _, source = places()
    j = source(d, p)
    send(block(j), block(j), sems, 4 * p + d, j, c).wait_recv()
    return j


def gather_close(block, sems):
    s, c, to, _ = places()
    for d, p in PEERS:
        send(block(s), block(s), sems, 4 * p + d, to(d, p), c).wait_send()


def share_open(block, sems, d, p):
    s, c, _, source = places()
    j = source(d, p)
    send(block(j), block(j), sems, 4 * p + d, s, 1 - c).start()


def share_take(block, other, sems, d, p):
    s, c, _, source = places()
    j = source(d, p)
    send(block(j), other(j), sems, 4 * p + d, s, 1 - c).wait_recv()
    return j


def share_close(block, sems):
    s, c, _, _ = places()
    for d, p in OFFSETS:
        send(block(s), block(s), sems, 4 * p + d, s, 1 - c).wait_send()


def halves(ref):
    c = lax.axis_index("col")
    mine, other = pl.multiple_of(c * 80, 16), pl.multiple_of((1 - c) * 80, 16)
    return (lambda j: ref.at[j, pl.ds(mine, 80), :]), (lambda j: ref.at[j, pl.ds(other, 80), :])


def dot(a, b, dims, precision=None):
    return lax.dot_general(
        a, b, (dims, ((), ())), precision=precision, preferred_element_type=jnp.float32
    )


NN = ((1,), (0,))
NT = ((1,), (1,))
TN = ((0,), (0,))


def iota(shape, axis):
    return lax.broadcasted_iota(jnp.int32, shape, axis)


def list_pages(table, lens, lists, pages, size):
    requests = table.shape[0]
    base = lax.axis_index("seq") * pages
    column = iota((1, table.shape[1]), 1)
    page = iota((pages, table.shape[1]), 0)

    def add(r, codes):
        left = lens[r] - column * size
        code = jnp.where(left > 0, r * 256 + jnp.minimum(left, size), 0)
        return codes + jnp.where(page == table[pl.ds(r, 1), :] - base, code, 0)

    codes = lax.fori_loop(0, requests, add, jnp.zeros(page.shape, jnp.int32))
    code = jnp.sum(codes.astype(jnp.float32), axis=1, keepdims=True)
    taken = jnp.where(code > 0.0, jnp.ones((1, 128), jnp.float32), 0.0)
    below = (iota((pages, pages), 1) < iota((pages, pages), 0)).astype(jnp.float32)
    before = dot(below.astype(jnp.bfloat16), taken.astype(jnp.bfloat16), NN)
    slot = iota((pages, 128), 1).astype(jnp.float32)
    placed = jnp.where(before == slot, taken, 0.0)
    at = jnp.sum(placed * iota((pages, 128), 0).astype(jnp.float32), axis=0, keepdims=True)
    packed = jnp.sum(placed * code, axis=0, keepdims=True).astype(jnp.int32)
    lists[...] = jnp.concatenate(
        [
            at.astype(jnp.int32),
            packed >> 8,
            packed & 255,
            jnp.sum(taken, axis=0, keepdims=True).astype(jnp.int32),
            jnp.zeros((4, 128), jnp.int32),
        ],
        axis=0,
    )


def project_kernel(
    pages, size, hid, order, w3, cos, sin, table, lens, q_all, kv_z, own_in, lists,
    hbuf, wsend, wrecv, stage, far, square, square_far,
    hs, hr, ss, sr, ws, wr, vs, vr, ts, tr, us, ur, ns, nr, qs, qr, ks, kr,
):
    s, c, to, source = places()
    steps, width, requests = hid.shape
    rows = steps * requests
    z, spot = s // 4, s % 4
    greet()
    mine, other = halves(hbuf)
    hsem, ssem, wsem, vsem, tsem, usem, nsem, qsem, ksem = (
        (hs, hr), (ss, sr), (ws, wr), (vs, vr), (ts, tr), (us, ur), (ns, nr), (qs, qr), (ks, kr)
    )
    j_at = iota((rows, requests), 0)
    same = (j_at // steps) == order[...]
    placed = jnp.zeros((width, rows), jnp.float32)
    for n in range(steps):
        pick = jnp.where(same & (j_at % steps == n), 1.0, 0.0).astype(jnp.bfloat16)
        placed = placed + dot(hid[n], pick, NT)
    own = jnp.concatenate([placed, jnp.zeros((160 - width, rows), jnp.float32)], axis=0)
    own_in[...] = own.astype(jnp.bfloat16)
    here = pl.multiple_of(c * 80, 16)
    hbuf[spot, pl.ds(here, 80), :] = own_in[pl.ds(here, 80), :]
    sent = []

    def post(*what):
        copy = send(*what)
        copy.start()
        sent.append(copy)

    for p in range(1, 4):
        post(mine(spot), mine(spot), hsem, p, to(0, p), c)
    post(mine(spot), mine(spot), ssem, 0, s, 1 - c)
    low = iota((width, 128), 1) < HEAD_DIM
    low_v = iota((80, 128), 1) < HEAD_DIM
    for pair in range(8):
        at = slice(128 * pair, 128 * pair + 128)
        wq, wk, wv = [w3[i, :, at].astype(jnp.float32) for i in range(3)]
        va = wv[:80]
        vb = jnp.concatenate([wv[80:], jnp.zeros((160 - width, 128), jnp.float32)], axis=0)
        turn = functools.partial(pltpu.roll, shift=64, axis=1)
        wsend[2 * pair, :width] = jnp.where(low, wq, turn(wk)).astype(jnp.bfloat16)
        wsend[2 * pair + 1, :width] = jnp.where(low, turn(wq), wk).astype(jnp.bfloat16)
        wsend[2 * pair, width:] = jnp.where(low_v, va, turn(vb)).astype(jnp.bfloat16)
        wsend[2 * pair + 1, width:] = jnp.where(low_v, turn(va), vb).astype(jnp.bfloat16)
    upper, lower = pl.ds(0, width), pl.ds(width, 80)
    turns = (1, 2, 3, 0)
    for part, sems in ((upper, wsem), (lower, vsem)):
        for d in turns:
            for p in range(1, 4):
                j = to(d, p)
                post(wsend.at[j, part], wrecv.at[p, d, part], sems, 4 * p + d, to(0, p), c)
    list_pages(table, lens, lists, pages, size)
    for p in range(1, 4):
        k = to(0, p) % 4
        send(mine(k), mine(k), hsem, p, to(0, p), c).wait_recv()
        post(mine(k), mine(k), ssem, p, s, 1 - c)
    squares = jnp.zeros((1, rows), jnp.float32)
    for p in range(4):
        k = to(0, p) % 4
        send(mine(k), other(k), ssem, p, s, 1 - c).wait_recv()
        wide = hbuf[k].astype(jnp.float32)
        squares = squares + jnp.sum(wide * wide, axis=0, keepdims=True)
    for t in range(3):
        square[t : t + 1, :] = squares[:, 128 * t : 128 * t + 128]
    square[3:8, :] = jnp.zeros((5, 128), jnp.float32)
    for d in range(1, 4):
        post(square, square_far.at[d], nsem, d, to(d, 0), c)

    def weights(p, d, part, sems):
        if p == 0:
            return wsend[to(d, 0), part]
        send(wsend.at[s, part], wrecv.at[p, d, part], sems, 4 * p + d, to(0, p), c).wait_recv()
        return wrecv[p, d, part]

    head = pl.ds(0, HEAD_DIM)
    tail = pl.ds(HEAD_DIM, 2 * HEAD_DIM)
    for d in turns:
        qk = jnp.zeros((128, rows), jnp.float32)
        for p in range(4):
            qk = qk + dot(weights(p, d, upper, wsem), hbuf[to(0, p) % 4, :width], TN)
        if d:
            stage[d, :128] = qk.astype(jnp.bfloat16)
            post(stage.at[d, head], far.at[d, head], tsem, d, to(d, 0), c)
    for d in turns:
        v0 = jnp.zeros((128, rows), jnp.float32)
        v1 = jnp.zeros((128, rows), jnp.float32)
        for p in range(4):
            w = weights(p, d, lower, vsem)
            k = to(0, p) % 4
            v0 = v0 + dot(w, hbuf[k, :80], TN)
            v1 = v1 + dot(w[: width - 80], hbuf[k, 80:width], TN)
        v = v0[:HEAD_DIM] + v1[HEAD_DIM:]
        if d:
            stage[d, 128:] = v.astype(jnp.bfloat16)
            post(stage.at[d, tail], far.at[d, tail], usem, d, to(d, 0), c)
    for d in range(1, 4):
        send(square, square_far.at[d], nsem, d, source(d, 0), c).wait_recv()
        squares = squares + jnp.concatenate(
            [square_far[d, t : t + 1, :] for t in range(3)], axis=1
        )
    inv = lax.rsqrt(squares / (width * 16) + EPSILON)
    half = HEAD_DIM // 2

    def turned(part):
        a, b = part[:half], part[half:]
        return jnp.concatenate([a * cos[...] - b * sin[...], b * cos[...] + a * sin[...]], axis=0)

    query, key = qk[:HEAD_DIM], qk[HEAD_DIM:]
    for d in range(1, 4):
        send(stage.at[d, head], far.at[d, head], tsem, d, source(d, 0), c).wait_recv()
        query = query + far[d, :HEAD_DIM].astype(jnp.float32)
    q_all[s] = turned(query * inv).astype(jnp.bfloat16)
    gather_open(lambda j: q_all.at[j], qsem)
    for d in range(1, 4):
        send(stage.at[d, tail], far.at[d, tail], usem, d, source(d, 0), c).wait_recv()
        key = key + far[d, HEAD_DIM:128].astype(jnp.float32)
        v = v + far[d, 128:].astype(jnp.float32)
    kv_z[z, :HEAD_DIM] = turned(key * inv).astype(jnp.bfloat16)
    kv_z[z, HEAD_DIM:] = (v * inv).astype(jnp.bfloat16)
    gather_pass(lambda j: q_all.at[j], qsem)
    for d in range(1, 4):
        post(kv_z.at[z], kv_z.at[z], ksem, d, to(d, 0), c)
    for p in range(1, 4):
        for d in range(4):
            gather_take(lambda j: q_all.at[j], qsem, d, p)
    for d in range(1, 4):
        block = kv_z.at[(z + 4 - d) % 4]
        send(block, block, ksem, d, source(d, 0), c).wait_recv()
    for copy in sent:
        copy.wait_send()
    gather_close(lambda j: q_all.at[j], qsem)


def vmem():
    return pl.BlockSpec(memory_space=pltpu.VMEM)


def pair_sems(count=16):
    return [pltpu.SemaphoreType.DMA((count,)), pltpu.SemaphoreType.DMA((count,))]


def project(hid, order, w3, cos, sin, table, lens, pages, size):
    steps, width, requests = hid.shape
    rows = steps * requests
    bf16 = jnp.bfloat16
    return pl.pallas_call(
        functools.partial(project_kernel, pages, size),
        out_shape=(
            jax.ShapeDtypeStruct((16, HEAD_DIM, rows), bf16),
            jax.ShapeDtypeStruct((4, 2 * HEAD_DIM, rows), bf16),
            jax.ShapeDtypeStruct((160, rows), bf16),
            jax.ShapeDtypeStruct((8, 128), jnp.int32),
        ),
        in_specs=[vmem()] * 6 + [pl.BlockSpec(memory_space=pltpu.SMEM)],
        out_specs=[vmem()] * 4,
        scratch_shapes=[
            pltpu.VMEM((4, 160, rows), bf16),
            pltpu.VMEM((16, width + 80, 128), bf16),
            pltpu.VMEM((4, 4, width + 80, 128), bf16),
            pltpu.VMEM((4, 3 * HEAD_DIM, rows), bf16),
            pltpu.VMEM((4, 3 * HEAD_DIM, rows), bf16),
            pltpu.VMEM((8, 128), jnp.float32),
            pltpu.VMEM((4, 8, 128), jnp.float32),
            *pair_sems(4), *pair_sems(4), *pair_sems(), *pair_sems(),
            *pair_sems(4), *pair_sems(4), *pair_sems(4), *pair_sems(), *pair_sems(4),
        ],
        compiler_params=pltpu.CompilerParams(
            collective_id=0, has_side_effects=True, vmem_limit_bytes=58 * MIB
        ),
        name="project",
    )(hid, order, w3, cos, sin, table, lens)


def attend_kernel(lists, q_all, *refs):
    keys, values = refs[:GROUP], refs[GROUP : 2 * GROUP]
    out, tops, flat, acc, peaks, totals, rowed = refs[2 * GROUP :]
    step = pl.program_id(0)
    rows = flat.shape[0]
    requests = rows // 4
    own = (iota((16, 1024), 1) % 256) // HEAD_DIM == iota((16, 1024), 0) // 4

    @pl.when(step == 0)
    def _():
        turned = q_all[...].reshape(16 * HEAD_DIM, rows).astype(jnp.float32)
        flat[...] = jnp.transpose(turned)

        @pl.loop(0, requests, unroll=4)
        def _(r):
            acc[r] = jnp.zeros((64, 256), jnp.float32)
            peaks[r] = jnp.full((64, 128), LOWEST, jnp.float32)
            totals[r] = jnp.zeros((64, 128), jnp.float32)

    @pl.when(step * GROUP < lists[3, 0])
    def _():
        token = iota((64, 128), 1)
        found = []
        for g in range(GROUP):
            at = step * GROUP + g
            r = lists[1, at]
            live = token < lists[2, at]
            lines = [flat[pl.ds(4 * r + n, 1), :] for n in range(4)]
            spread = jnp.where(own, jnp.concatenate(lines * 4, axis=0), 0.0).astype(jnp.bfloat16)
            scores = jnp.concatenate(
                [
                    dot(spread[:, 256 * i : 256 * i + 256], keys[g][0, :, 256 * i : 256 * i + 256], NT)
                    for i in range(4)
                ],
                axis=0,
            )
            scores = jnp.where(live, scores * (HEAD_DIM**-0.5), LOWEST)
            top = jnp.max(scores, axis=1, keepdims=True)
            weights = jnp.where(live, jnp.exp(scores - top), 0.0)
            total = jnp.sum(weights, axis=1, keepdims=True)
            lowered = weights.astype(jnp.bfloat16)
            mixed = jnp.concatenate(
                [
                    dot(lowered[16 * i : 16 * i + 16], values[g][0, :, 256 * i : 256 * i + 256], NN)
                    for i in range(4)
                ],
                axis=0,
            )
            found.append((r, top, total, mixed))
        for r, top, total, mixed in found:
            old = peaks[r]
            new = jnp.maximum(old, top)
            keep = jnp.exp(old - new)
            add = jnp.exp(top - new)
            peaks[r] = new
            totals[r] = totals[r] * keep + total * add
            acc[r] = acc[r] * jnp.concatenate([keep, keep], axis=1) + mixed * jnp.concatenate(
                [add, add], axis=1
            )

    @pl.when(step == pl.num_programs(0) - 1)
    def _():
        diagonal = iota((64, 128), 0) == iota((64, 128), 1)
        rowed[...] = jnp.zeros_like(rowed)

        @pl.loop(0, requests // 2, unroll=4)
        def _(pair):
            parts = []
            for e in range(2):
                r = 2 * pair + e
                whole = acc[r]
                lines = []
                for i in range(4):
                    x = jnp.where(own[:, :256], whole[16 * i : 16 * i + 16], 0.0)
                    y = x[:8] + x[8:]
                    lines.append(y[:4] + y[4:])
                parts.append(jnp.concatenate(lines, axis=1))
                rowed[0, pl.ds(r, 1), :] = jnp.sum(
                    jnp.where(diagonal, peaks[r], 0.0), axis=0, keepdims=True
                )
                rowed[1, pl.ds(r, 1), :] = jnp.sum(
                    jnp.where(diagonal, totals[r], 0.0), axis=0, keepdims=True
                )
            flat[pl.ds(pl.multiple_of(8 * pair, 8), 8), :] = jnp.concatenate(parts, axis=0)

        out[...] = (
            jnp.transpose(flat[...]).astype(jnp.bfloat16).reshape(16, HEAD_DIM, rows)
        )
        place = (iota((128, rows), 1) // 4 == iota((128, rows), 0)).astype(jnp.float32)
        match = iota((64, rows), 0) % 4 == iota((64, rows), 1) % 4
        fold = (iota((16, 64), 1) // 4 == iota((16, 64), 0)).astype(jnp.float32)
        for k in range(2):
            spread = dot(jnp.transpose(rowed[k])[:64], place, NN, lax.Precision.HIGHEST)
            by_head = dot(fold, jnp.where(match, spread, 0.0), NN, lax.Precision.HIGHEST)
            for h in range(16):
                for t in range(3):
                    tops[h, 3 * k + t : 3 * k + t + 1, :] = by_head[
                        h : h + 1, 128 * t : 128 * t + 128
                    ]
        tops[:, 6:8, :] = jnp.zeros((16, 2, 128), jnp.float32)


def attend(lists, q_all, keys, values):
    pages, size, cols = keys.shape
    rows = q_all.shape[2]
    requests = rows // 4

    def page_spec(g):
        def index(i, lists):
            at = jnp.minimum(i * GROUP + g, jnp.maximum(lists[3, 0] - 1, 0))
            return (lists[0, at], 0, 0)

        return pl.BlockSpec((1, size, cols), index)

    specs = [page_spec(g) for g in range(GROUP)]
    return pl.pallas_call(
        attend_kernel,
        grid_spec=pltpu.PrefetchScalarGridSpec(
            num_scalar_prefetch=1,
            grid=(pages // GROUP,),
            in_specs=[pl.BlockSpec((16, HEAD_DIM, rows), lambda *_: (0, 0, 0))] + specs + specs,
            out_specs=[
                pl.BlockSpec((16, HEAD_DIM, rows), lambda *_: (0, 0, 0)),
                pl.BlockSpec((16, 8, 128), lambda *_: (0, 0, 0)),
            ],
            scratch_shapes=[
                pltpu.VMEM((rows, cols), jnp.float32),
                pltpu.VMEM((requests, 64, 256), jnp.float32),
                pltpu.VMEM((requests, 64, 128), jnp.float32),
                pltpu.VMEM((requests, 64, 128), jnp.float32),
                pltpu.VMEM((2, 128, 128), jnp.float32),
            ],
        ),
        out_shape=(
            jax.ShapeDtypeStruct((16, HEAD_DIM, rows), jnp.bfloat16),
            jax.ShapeDtypeStruct((16, 8, 128), jnp.float32),
        ),
        compiler_params=pltpu.CompilerParams(vmem_limit_bytes=48 * MIB),
        cost_estimate=pl.CostEstimate(
            flops=4 * pages * 64 * size * cols,
            bytes_accessed=4 * pages * size * cols,
            transcendentals=pages * 64 * size,
        ),
        name="attend",
    )(lists, q_all, *([keys] * GROUP), *([values] * GROUP))


def finish_kernel(
    parts, tops, q_all, kv_z, own_in, w_out, pair_hbm, down_hbm, router, routes, final,
    got, got_tops, far, far_tops, stage, stage_tops, attended, partial, theirs, mbuf,
    mid_all, pair, down, gates, active, mixed, swapped, summed, near_sums, sums, far_sums, kept,
    gs, gr, ts, tr, fs, fr, us, ur, as_, ar, ps, pr, ms, mr, ss, sr,
    cs, cr, hs, hr, ds, dr, ls, lr, pair_sem, down_sem,
):
    s, c, to, source = places()
    rows = kv_z.shape[2]
    fetches = [
        pltpu.make_async_copy(pair_hbm.at[e], pair.at[e], pair_sem.at[e])
        for e in range(pair.shape[0])
    ] + [pltpu.make_async_copy(down_hbm, down, down_sem)]
    greet()
    gsem, tsem, fsem, usem, asem, psem, msem, ssem = (
        (gs, gr), (ts, tr), (fs, fr), (us, ur), (as_, ar), (ps, pr), (ms, mr), (ss, sr)
    )
    order = (1, 2, 3, 0)
    sent = []
    for d in order:
        for p in range(1, 4):
            j, near = to(d, p), to(0, p)
            sent.append(send(tops.at[j], got_tops.at[p, d], tsem, 4 * p + d, near, c))
            sent.append(send(parts.at[j], got.at[p, d], gsem, 4 * p + d, near, c))
    for copy in sent:
        copy.start()
    for fetch in fetches:
        fetch.start()
    q = q_all[s].astype(jnp.float32)
    k = kv_z[s // 4, :HEAD_DIM].astype(jnp.float32)
    v = kv_z[s // 4, HEAD_DIM:].astype(jnp.float32)
    moment = iota((1, rows), 1) % 4
    fresh = []
    for back in range(4):
        moved = k if back == 0 else pltpu.roll(k, shift=back, axis=1)
        score = jnp.sum(q * moved, axis=0, keepdims=True) * (HEAD_DIM**-0.5)
        fresh.append(jnp.where(moment >= back, score, LOWEST))

    def lines(block):
        return [
            jnp.concatenate([block[3 * k + t : 3 * k + t + 1] for t in range(3)], axis=1)
            for k in range(2)
        ]

    def merge(items, extra):
        best = functools.reduce(jnp.maximum, extra + [item[0] for item in items])
        bottom = jnp.zeros((1, rows), jnp.float32)
        top = jnp.zeros((HEAD_DIM, rows), jnp.float32)
        for peak, total, block in items:
            scale = jnp.exp(peak - best)
            bottom = bottom + total * scale
            top = top + block.astype(jnp.float32) * scale
        return best, bottom, top

    for d in order:
        items = [(*lines(tops[to(d, 0)]), parts[to(d, 0)])]
        for p in range(1, 4):
            near = to(0, p)
            send(tops.at[s], got_tops.at[p, d], tsem, 4 * p + d, near, c).wait_recv()
            send(parts.at[s], got.at[p, d], gsem, 4 * p + d, near, c).wait_recv()
            items.append((*lines(got_tops[p, d]), got[p, d]))
        best, bottom, top = merge(items, [])
        if d:
            stage[d] = top.astype(jnp.bfloat16)
            for k, row in enumerate((best, bottom)):
                for t in range(3):
                    stage_tops[d, 3 * k + t : 3 * k + t + 1, :] = row[:, 128 * t : 128 * t + 128]
            stage_tops[d, 6:8, :] = jnp.zeros((2, 128), jnp.float32)
            for copy in (
                send(stage_tops.at[d], far_tops.at[d], usem, d, to(d, 0), c),
                send(stage.at[d], far.at[d], fsem, d, to(d, 0), c),
            ):
                copy.start()
                sent.append(copy)
    items = [(best, bottom, top)]
    for d in range(1, 4):
        send(stage_tops.at[d], far_tops.at[d], usem, d, source(d, 0), c).wait_recv()
        send(stage.at[d], far.at[d], fsem, d, source(d, 0), c).wait_recv()
        items.append((*lines(far_tops[d]), far[d]))
    best, bottom, top = merge(items, fresh)
    for back in range(4):
        weight = jnp.where(moment >= back, jnp.exp(fresh[back] - best), 0.0)
        bottom = bottom + weight
        moved = v if back == 0 else pltpu.roll(v, shift=back, axis=1)
        top = top + weight.astype(jnp.bfloat16).astype(jnp.float32) * moved
    attended[s] = (top / bottom).astype(jnp.bfloat16)
    whole = lambda j: attended.at[j]
    gather_open(whole, asem)
    gather_pass(whole, asem)
    for p in range(1, 4):
        for d in range(4):
            gather_take(whole, asem, d, p)
    width = w_out.shape[0]
    partial[:width] = dot(w_out[...], attended[...].reshape(16 * HEAD_DIM, rows), NN)
    partial[width:] = jnp.zeros((160 - width, rows), jnp.float32)
    here, there = pl.multiple_of(c * 80, 16), pl.multiple_of((1 - c) * 80, 16)
    swap = send(partial.at[pl.ds(there, 80), :], theirs, psem, 0, s, 1 - c)
    swap.start()
    swap.wait_recv()
    mid = own_in[pl.ds(here, 80), :].astype(jnp.float32) + partial[pl.ds(here, 80), :] + theirs[...]
    mid = mid.astype(jnp.bfloat16)
    mbuf[s, pl.ds(here, 80), :] = mid
    mine, other = halves(mbuf)
    gather_open(mine, msem)
    share_open(mine, ssem, 0, 0)
    gather_pass(mine, msem)
    for d in range(1, 4):
        share_open(mine, ssem, d, 0)
    for p in range(1, 4):
        for d in range(4):
            gather_take(mine, msem, d, p)
            share_open(mine, ssem, d, p)
    for d, p in OFFSETS:
        share_take(mine, other, ssem, d, p)
    squares = jnp.zeros((1, rows), jnp.float32)
    for j in range(16):
        block = mbuf[j, :width]
        mid_all[width * j : width * j + width] = block
        wide = block.astype(jnp.float32)
        squares = squares + jnp.sum(wide * wide, axis=0, keepdims=True)

    inv = lax.rsqrt(squares / (width * 16) + EPSILON)
    logits = dot(router[...], mid_all[...], NN) * inv
    which = iota(logits.shape, 0)
    first, second = which == routes[0:1], which == routes[1:2]
    share = jax.nn.sigmoid(
        jnp.sum(jnp.where(first, logits, 0.0), axis=0, keepdims=True)
        - jnp.sum(jnp.where(second, logits, 0.0), axis=0, keepdims=True)
    )
    gates[...] = jnp.where(first, share, 0.0) + jnp.where(second, 1.0 - share, 0.0)
    count = pair.shape[0]

    def expert(e):
        pltpu.make_async_copy(pair_hbm.at[e], pair.at[e], pair_sem.at[e]).wait()
        mask = iota(gates.shape, 0) == c * count + e
        gate = jnp.sum(jnp.where(mask, gates[...], 0.0), axis=0, keepdims=True)
        front = dot(pair[e, 0], mid_all[...], NN) * inv
        back = dot(pair[e, 1], mid_all[...], NN) * inv
        value = (front / (1.0 + jnp.exp(-front))) * back
        active[e] = jnp.transpose(value * gate).astype(jnp.bfloat16)

    @pl.loop(0, count)
    def _(e):
        expert(e)

    fetches[-1].wait()
    csem, hsem, lsem = (cs, cr), (hs, hr), (ls, lr)
    step = 384
    z = s // 4
    here_seq = s % 4

    def mix(i):
        at = slice(step * i, step * i + step)
        part = dot(active[0], down[0, :, at], NN)
        for k in range(1, count):
            part = part + dot(active[k], down[k, :, at], NN)
        mixed[at] = jnp.transpose(part).astype(jnp.bfloat16)

    def trade(half):
        for j in range(8 * half, 8 * half + 8):
            at = width * j

            @pl.when(c == 0)
            def _(j=j, at=at):
                swapped[0, j, : width - 80] = mixed[at + 80 : at + width]

            @pl.when(c == 1)
            def _(j=j, at=at):
                swapped[0, j] = mixed[at : at + 80]

            send(swapped.at[0, j], swapped.at[1, j], csem, j, s, 1 - c).start()

    def spread(zt):
        for k in range(4):
            j = 4 * zt + k
            send(swapped.at[0, j], swapped.at[1, j], csem, j, s, 1 - c).wait_recv()
            at = width * j

            @pl.when(c == 0)
            def _(j=j, at=at):
                mine_part = mixed[at : at + 80].astype(jnp.float32)
                summed[j] = (mine_part + swapped[1, j].astype(jnp.float32)).astype(jnp.bfloat16)

            @pl.when(c == 1)
            def _(j=j, at=at):
                mine_part = mixed[at + 80 : at + width].astype(jnp.float32)
                rest = width - 80
                summed[j, :rest] = (mine_part + swapped[1, j, :rest].astype(jnp.float32)).astype(
                    jnp.bfloat16
                )

        for p in (3, 1, 2):
            near = to(0, p)
            send(
                summed.at[4 * zt + near % 4], near_sums.at[p, zt], hsem, 4 * p + zt, near, c
            ).start()

    for i in range(3):
        mix(i)
    trade(0)
    mix(3)
    spread(0)
    mix(4)
    spread(1)
    mix(5)
    trade(1)
    spread(2)
    spread(3)

    def far_copy(zt, zs):
        return pltpu.make_async_remote_copy(
            src_ref=sums.at[zt],
            dst_ref=far_sums.at[zs],
            send_sem=ds.at[zt],
            recv_sem=dr.at[zs],
            device_id=(4 * zt + here_seq, c),
            device_id_type=pl.DeviceIdType.MESH,
        )

    for zt in range(4):
        total = summed[4 * zt + here_seq].astype(jnp.float32)
        for p in range(1, 4):
            send(summed.at[0], near_sums.at[p, zt], hsem, 4 * p + zt, to(0, p), c).wait_recv()
            total = total + near_sums[p, zt].astype(jnp.float32)

        @pl.when(zt == z)
        def _(total=total):
            kept[...] = total

        @pl.when(zt != z)
        def _(total=total, zt=zt):
            sums[zt] = total.astype(jnp.bfloat16)
            far_copy(zt, z).start()

    total = kept[...] + mbuf[s, pl.ds(here, 80), :].astype(jnp.float32)
    for d in range(1, 4):
        zs = (z + d) % 4
        far_copy(zs, zs).wait_recv()
        total = total + far_sums[zs].astype(jnp.float32)
    final[pl.ds(here, 80), :] = total.astype(jnp.bfloat16)
    half, rest = final.at[pl.ds(here, 80), :], final.at[pl.ds(there, 80), :]
    last = send(half, half, lsem, 0, s, 1 - c)
    last.start()
    send(half, rest, lsem, 0, s, 1 - c).wait_recv()
    last.wait_send()
    swap.wait_send()
    for copy in sent:
        copy.wait_send()
    gather_close(whole, asem)
    gather_close(mine, msem)
    share_close(mine, ssem)
    for j in range(16):
        send(swapped.at[0, j], swapped.at[1, j], csem, j, s, 1 - c).wait_send()
    for p in range(1, 4):
        for zt in range(4):
            send(summed.at[0], near_sums.at[p, zt], hsem, 4 * p + zt, to(0, p), c).wait_send()
    for d in range(1, 4):
        far_copy((z + d) % 4, z).wait_send()


def finish(parts, tops, q_all, kv_z, own_in, w_out, pair, down, router, routes):
    rows = kv_z.shape[2]
    width = w_out.shape[0]
    bf16, f32 = jnp.bfloat16, jnp.float32
    anywhere = pl.BlockSpec(memory_space=pl.ANY)
    return pl.pallas_call(
        finish_kernel,
        out_shape=jax.ShapeDtypeStruct((160, rows), bf16),
        in_specs=[vmem()] * 6 + [anywhere] * 2 + [vmem()] * 2,
        out_specs=vmem(),
        scratch_shapes=[
            pltpu.VMEM((4, 4, HEAD_DIM, rows), bf16),
            pltpu.VMEM((4, 4, 8, 128), f32),
            pltpu.VMEM((4, HEAD_DIM, rows), bf16),
            pltpu.VMEM((4, 8, 128), f32),
            pltpu.VMEM((4, HEAD_DIM, rows), bf16),
            pltpu.VMEM((4, 8, 128), f32),
            pltpu.VMEM((16, HEAD_DIM, rows), bf16),
            pltpu.VMEM((160, rows), f32),
            pltpu.VMEM((80, rows), f32),
            pltpu.VMEM((16, 160, rows), bf16),
            pltpu.VMEM((16 * width, rows), bf16),
            pltpu.VMEM(pair.shape, bf16),
            pltpu.VMEM(down.shape, bf16),
            pltpu.VMEM((router.shape[0], rows), f32),
            pltpu.VMEM((pair.shape[0], rows, pair.shape[2]), bf16),
            pltpu.VMEM((16 * width, rows), bf16),
            pltpu.VMEM((2, 16, 80, rows), bf16),
            pltpu.VMEM((16, 80, rows), bf16),
            pltpu.VMEM((4, 4, 80, rows), bf16),
            pltpu.VMEM((4, 80, rows), bf16),
            pltpu.VMEM((4, 80, rows), bf16),
            pltpu.VMEM((80, rows), f32),
            *pair_sems(), *pair_sems(), *pair_sems(4), *pair_sems(4),
            *pair_sems(), *pair_sems(1), *pair_sems(), *pair_sems(),
            *pair_sems(), *pair_sems(), *pair_sems(4), *pair_sems(1),
            pltpu.SemaphoreType.DMA((pair.shape[0],)), pltpu.SemaphoreType.DMA,
        ],
        compiler_params=pltpu.CompilerParams(
            collective_id=1, has_side_effects=True, vmem_limit_bytes=58 * MIB
        ),
        name="finish",
    )(parts, tops, q_all, kv_z, own_in, w_out, pair, down, router, routes)


def unpack_kernel(*refs):
    planes, (final, layer, keys, values) = refs[:4], refs[4:]
    steps, requests, _ = keys.shape
    rows = planes[0].shape[2]
    at = (rows, rows)
    row = iota(at, 0)
    pick = iota(at, 1) == (row % requests) * steps + row // requests
    pick = jnp.where(pick, 1.0, 0.0).astype(jnp.bfloat16)

    @pl.when(pl.program_id(0) == 0)
    def _():
        width = layer.shape[1]
        done = dot(final[...], pick, NT).astype(jnp.bfloat16)
        for n in range(steps):
            layer[n] = done[:width, n * requests : n * requests + requests]

    mine = lax.axis_index("seq") % 4
    heads = []
    for k in range(4):
        offset = ((k // 2 + 2 - mine // 2) % 2) * 2 + (k + 2 - mine) % 2
        block = planes[0][0]
        for p in range(1, 4):
            block = jnp.where(offset == p, planes[p][0], block)
        heads.append(block)
    for first, result in ((0, keys), (HEAD_DIM, values)):
        four = jnp.concatenate([head[first : first + HEAD_DIM] for head in heads], axis=0)
        done = dot(pick, four, NT).astype(jnp.bfloat16)
        for n in range(steps):
            result[n] = done[n * requests : n * requests + requests]


def unpack(planes, final, steps, width):
    _, both, rows = planes[0].shape
    shape = (steps, rows // steps, 16 * HEAD_DIM)
    first = (steps, width, rows // steps)
    spec = pl.BlockSpec((*shape[:2], 4 * HEAD_DIM), lambda z: (0, 0, z))
    return pl.pallas_call(
        unpack_kernel,
        grid=(4,),
        in_specs=[pl.BlockSpec((1, both, rows), lambda z: (z, 0, 0))] * 4
        + [pl.BlockSpec(final.shape, lambda z: (0, 0))],
        out_specs=[pl.BlockSpec(first, lambda z: (0, 0, 0)), spec, spec],
        out_shape=(
            jax.ShapeDtypeStruct(first, jnp.bfloat16),
            jax.ShapeDtypeStruct(shape, jnp.bfloat16),
            jax.ShapeDtypeStruct(shape, jnp.bfloat16),
        ),
        cost_estimate=pl.CostEstimate(
            flops=4 * rows * rows * shape[2], bytes_accessed=8 * rows * shape[2], transcendentals=0
        ),
        name="unpack",
    )(*planes, final)


def plane_shift(block, p):
    pairs = [(i, i // 4 * 4 + (i % 4 ^ p)) for i in range(16)]
    return lax.ppermute(block, "seq", pairs)


def fast(
    hidden,
    key_cache,
    value_cache,
    page_table,
    cache_len,
    order,
    route_ids,
    w_qkv,
    w_out,
    w_router,
    w_gate_up,
    w_down,
):
    steps, requests, width = hidden.shape
    pages, size, cols = key_cache.shape
    rows = steps * requests
    half = HEAD_DIM // 2
    frequency = jnp.exp(
        -jnp.log(10000.0) * 2.0 * jnp.arange(half, dtype=jnp.float32) / HEAD_DIM
    )
    positions = (cache_len[:, None] + jnp.arange(steps)[None, :]).reshape(rows)
    angles = frequency[:, None] * positions.astype(jnp.float32)[None, :]
    q_all, kv_z, own_in, lists = project(
        hidden.transpose(0, 2, 1),
        order[None, :],
        w_qkv.transpose(1, 0, 2),
        jnp.cos(angles),
        jnp.sin(angles),
        page_table,
        cache_len,
        pages,
        size,
    )
    planes = [kv_z] + [plane_shift(kv_z, p) for p in range(1, 4)]
    parts, tops = attend(lists, q_all, key_cache, value_cache)
    routes = route_ids.transpose(2, 1, 0).reshape(2, rows)
    final = finish(
        parts, tops, q_all, kv_z, own_in, w_out.T,
        w_gate_up.transpose(0, 2, 3, 1), w_down, w_router.T, routes,
    )
    layer, keys, values = unpack(planes, final, steps, width)
    return layer.transpose(0, 2, 1), keys, values


def solution(mesh):
    placed = (
        P(None, None, "seq"),
        P("seq", None, "col"),
        P("seq", None, "col"),
        P(),
        P(),
        P(),
        P(),
        P("seq", None, "col"),
        P("col", "seq"),
        P(),
        P("col", None, None, "seq"),
        P("col", "seq", None),
    )
    small = mesh.shape["seq"] == 16 and mesh.shape["col"] == 2
    return jax.shard_map(
        fast if small else local,
        mesh=mesh,
        in_specs=placed,
        out_specs=(P(None, None, "seq"), P(None, None, "col"), P(None, None, "col")),
        check_vma=False,
    )
```

```python
import functools

import jax
import jax.numpy as jnp
from jax import lax
from jax.experimental import pallas as pl
from jax.experimental.pallas import tpu as pltpu
from jax.sharding import PartitionSpec as P

HEAD_DIM = 64
EPSILON = 1e-05
LOWEST = -1e30
GROUP = 4
CHUNKS = 3
MIB = 1024 * 1024


def rotate(row_data, positions, head_dim):
    head_count = row_data.shape[1] // head_dim
    half_dim = head_dim // 2
    frequency = jnp.exp(
        -jnp.log(10000.0) * 2.0 * jnp.arange(half_dim, dtype=jnp.float32) / head_dim
    )
    angles = positions.astype(jnp.float32)[:, None] * frequency[None, :]
    cosine = jnp.cos(angles)[:, None, :]
    sines = jnp.sin(angles)[:, None, :]
    by_head = row_data.reshape(row_data.shape[0], head_count, head_dim)
    front_half = by_head[:, :, :half_dim]
    back_half = by_head[:, :, half_dim:]
    turned = jnp.concatenate(
        [front_half * cosine - back_half * sines, back_half * cosine + front_half * sines], axis=2
    )
    return turned.reshape(row_data.shape)


def page_kernel(owner_ref, count_ref, q_ref, k_ref, v_ref, sum_ref, peak_ref, total_ref):
    page = pl.program_id(0)
    steps, cols = q_ref.shape[1], q_ref.shape[2]
    size = k_ref.shape[1]
    padded = peak_ref.shape[2] // steps
    count = count_ref[page]
    wide = q_ref[0].astype(jnp.float32)
    own = lax.broadcasted_iota(jnp.int32, (padded, cols), 1) // HEAD_DIM == lax.broadcasted_iota(
        jnp.int32, (padded, cols), 0
    )
    spread = jnp.concatenate(
        [jnp.where(own, wide[n : n + 1, :], 0.0) for n in range(steps)], axis=0
    ).astype(jnp.bfloat16)
    scores = lax.dot_general(
        k_ref[0], spread, (((1,), (1,)), ((), ())), preferred_element_type=jnp.float32
    ) * (HEAD_DIM ** (-0.5))
    live = lax.broadcasted_iota(jnp.int32, (size, steps * padded), 0) < count
    scores = jnp.where(live, scores, LOWEST)
    peak = jnp.max(scores, axis=0, keepdims=True)
    weights = jnp.where(live, jnp.exp(scores - peak), 0.0)
    peak_ref[0] = peak
    total_ref[0] = jnp.sum(weights, axis=0, keepdims=True)
    mixed = lax.dot_general(
        weights.astype(jnp.bfloat16),
        v_ref[0],
        (((0,), (0,)), ((), ())),
        preferred_element_type=jnp.float32,
    )
    for n in range(steps):
        part = jnp.where(own, mixed[n * padded : (n + 1) * padded, :], 0.0)
        sum_ref[0, n : n + 1, :] = jnp.sum(part, axis=0, keepdims=True)


def page_parts(owner, count, query, keys, values):
    pages, size, cols = keys.shape
    steps = query.shape[1]
    heads = cols // HEAD_DIM
    padded = -(-heads // 8) * 8
    sums, peak, total = pl.pallas_call(
        page_kernel,
        grid_spec=pltpu.PrefetchScalarGridSpec(
            num_scalar_prefetch=2,
            grid=(pages,),
            in_specs=[
                pl.BlockSpec((1, steps, cols), lambda p, o, c: (o[p], 0, 0)),
                pl.BlockSpec((1, size, cols), lambda p, o, c: (p, 0, 0)),
                pl.BlockSpec((1, size, cols), lambda p, o, c: (p, 0, 0)),
            ],
            out_specs=[
                pl.BlockSpec((1, steps, cols), lambda p, o, c: (p, 0, 0)),
                pl.BlockSpec((1, 1, steps * padded), lambda p, o, c: (p, 0, 0)),
                pl.BlockSpec((1, 1, steps * padded), lambda p, o, c: (p, 0, 0)),
            ],
        ),
        out_shape=(
            jax.ShapeDtypeStruct((pages, steps, cols), jnp.float32),
            jax.ShapeDtypeStruct((pages, 1, steps * padded), jnp.float32),
            jax.ShapeDtypeStruct((pages, 1, steps * padded), jnp.float32),
        ),
        cost_estimate=pl.CostEstimate(
            flops=4 * pages * steps * padded * size * cols,
            bytes_accessed=4 * pages * size * cols,
            transcendentals=pages * steps * padded * size,
        ),
    )(owner, count, query, keys, values)
    peak = peak.reshape(pages, steps, padded)[:, :, :heads]
    total = total.reshape(pages, steps, padded)[:, :, :heads]
    return sums, peak, total


def pieces(value, count):
    out = []
    for _ in range(count):
        part = lax.reduce_precision(value, 8, 7)
        out.append(part.astype(jnp.bfloat16))
        value = value - part
    return out


def exchange(blocks):
    return lax.all_to_all(blocks, "seq", split_axis=0, concat_axis=0, tiled=True)


def col_scatter(rows):
    if lax.axis_size("col") == 2:
        half = rows.shape[0] // 2
        me = lax.axis_index("col")
        mine = lax.dynamic_slice_in_dim(rows, me * half, half, 0)
        theirs = lax.dynamic_slice_in_dim(rows, (1 - me) * half, half, 0)
        return mine + lax.ppermute(theirs, "col", [(0, 1), (1, 0)])
    return lax.psum_scatter(rows, "col", scatter_dimension=0, tiled=True)


def col_gather(rows):
    if lax.axis_size("col") == 2:
        me = lax.axis_index("col")
        other = lax.ppermute(rows, "col", [(0, 1), (1, 0)])
        first = jnp.where(me == 0, rows, other)
        second = jnp.where(me == 0, other, rows)
        return jnp.concatenate([first, second], axis=0)
    return lax.all_gather(rows, "col", axis=0, tiled=True)


def local(
    hidden,
    key_cache,
    value_cache,
    page_table,
    cache_len,
    order,
    route_ids,
    w_qkv,
    w_out,
    w_router,
    w_gate_up,
    w_down,
):
    steps, requests, width_loc = hidden.shape
    pages_loc, page_size, cols = key_cache.shape
    heads = cols // HEAD_DIM
    shards = lax.axis_size("seq")
    width_all = width_loc * shards
    experts_loc = w_gate_up.shape[0]
    ff_loc = w_gate_up.shape[3]
    expert_count = w_router.shape[1]
    expert_base = lax.axis_index("col") * experts_loc
    seq_index = lax.axis_index("seq")
    share = -(-requests // shards)
    filler = share * shards - requests
    row_count = steps * requests
    own_rows = share * steps

    placing = (order[:, None] == jnp.arange(requests)[None, :]).astype(jnp.bfloat16)
    inputs = jnp.einsum("nsc,sr->rnc", hidden, placing, preferred_element_type=jnp.float32).astype(
        jnp.bfloat16
    )
    flat_in = inputs.reshape(row_count, width_loc)
    wide_in = flat_in.astype(jnp.float32)
    squares = jnp.sum(wide_in * wide_in, axis=1, keepdims=True)
    partial = jnp.dot(
        flat_in, w_qkv.reshape(width_loc, 3 * cols), preferred_element_type=jnp.float32
    ).astype(jnp.bfloat16)
    tail = jnp.pad(jnp.concatenate(pieces(squares, 3), axis=1), ((0, 0), (0, 125)))
    sent = jnp.pad(jnp.concatenate([partial, tail], axis=1), ((0, filler * steps), (0, 0)))
    sent = sent.reshape(shards, own_rows, 3 * cols + 128)
    got = jnp.sum(exchange(sent).astype(jnp.float32), axis=0)
    inv_one = lax.rsqrt(jnp.sum(got[:, 3 * cols :], axis=1) / width_all + EPSILON)
    proj = got[:, : 3 * cols] * inv_one[:, None]
    own_len = lax.dynamic_slice_in_dim(jnp.pad(cache_len, (0, filler)), seq_index * share, share, 0)
    positions = (own_len[:, None] + jnp.arange(steps)[None, :]).reshape(own_rows)
    query = rotate(proj[:, :cols], positions, HEAD_DIM).astype(jnp.bfloat16)
    fresh_key = rotate(proj[:, cols : 2 * cols], positions, HEAD_DIM).astype(jnp.bfloat16)
    fresh_value = proj[:, 2 * cols :].astype(jnp.bfloat16)
    all_query = lax.all_gather(query, "seq", axis=0, tiled=True)[:row_count]
    all_query, fresh_pair = lax.optimization_barrier(
        (all_query, jnp.concatenate([fresh_key, fresh_value], axis=1))
    )
    all_pair = lax.all_gather(fresh_pair, "seq", axis=0, tiled=True)[:row_count]
    all_pair = all_pair.reshape(requests, steps, 2 * cols).transpose(1, 0, 2)

    needed = (cache_len + steps + page_size - 1) // page_size
    columns = jnp.arange(page_table.shape[1])
    in_use = columns[None, :] < needed[:, None]
    local_pages = page_table - seq_index * pages_loc
    page_hits = in_use[:, :, None] & (
        local_pages[:, :, None] == jnp.arange(pages_loc)[None, None, :]
    )
    owned_by = jnp.any(page_hits, axis=1)
    page_starts = jnp.sum(jnp.where(page_hits, columns[None, :, None] * page_size, 0), axis=(0, 1))
    page_len = jnp.sum(jnp.where(owned_by, cache_len[:, None], 0), axis=0)
    owner = jnp.sum(jnp.where(owned_by, jnp.arange(requests)[:, None], 0), axis=0)
    count = page_len - page_starts
    page_sums, page_peak, page_total = page_parts(
        owner.astype(jnp.int32),
        count.astype(jnp.int32),
        all_query.reshape(requests, steps, cols),
        key_cache,
        value_cache,
    )
    mask = owned_by[:, :, None, None]
    req_peak = jnp.max(jnp.where(mask, page_peak[None], LOWEST), axis=1)
    back_peak = jnp.max(jnp.where(mask, req_peak[:, None], LOWEST), axis=0)
    factor = jnp.exp(page_peak - back_peak)
    factor = jnp.where((count > 0)[:, None, None] & jnp.any(owned_by, axis=0)[:, None, None], factor, 0.0)
    owner_float = owned_by.astype(jnp.float32)
    req_total = jnp.einsum(
        "rp,pnh->rnh", owner_float, page_total * factor, precision=lax.Precision.HIGHEST
    )
    scaled = page_sums * jnp.repeat(factor, HEAD_DIM, axis=2)
    req_sums = jnp.einsum("rp,pnc->rnc", owner_float, scaled, precision=lax.Precision.HIGHEST)
    extra = jnp.concatenate(pieces(req_peak, 3) + pieces(req_total, 3), axis=2)
    spare = -extra.shape[2] % 128
    extra = jnp.pad(extra, ((0, 0), (0, 0), (0, spare)))
    sent = jnp.concatenate([req_sums.astype(jnp.bfloat16), extra], axis=2)
    sent = jnp.pad(sent, ((0, filler), (0, 0), (0, 0)))
    got = exchange(sent.reshape(shards, own_rows, sent.shape[2])).astype(jnp.float32)
    sums = got[:, :, :cols]
    bits = got[:, :, cols : cols + 6 * heads].reshape(shards, own_rows, 6, heads)
    peaks = bits[:, :, 0] + bits[:, :, 1] + bits[:, :, 2]
    totals = bits[:, :, 3] + bits[:, :, 4] + bits[:, :, 5]
    q_own = query.astype(jnp.float32).reshape(share, steps, 1, heads, HEAD_DIM)
    k_own = fresh_key.astype(jnp.float32).reshape(share, 1, steps, heads, HEAD_DIM)
    v_own = fresh_value.astype(jnp.float32).reshape(share, 1, steps, cols)
    fresh_scores = jnp.sum(q_own * k_own, axis=4) * (HEAD_DIM ** (-0.5))
    seen = (jnp.arange(steps)[None, :] <= jnp.arange(steps)[:, None])[None, :, :, None]
    fresh_scores = jnp.where(seen, fresh_scores, LOWEST)
    best = jnp.maximum(
        jnp.max(peaks, axis=0).reshape(share, steps, heads), jnp.max(fresh_scores, axis=2)
    )
    fresh_weights = jnp.where(seen, jnp.exp(fresh_scores - best[:, :, None]), 0.0)
    scale = jnp.exp(peaks - best.reshape(1, own_rows, heads))
    denominator = jnp.sum(totals * scale, axis=0) + jnp.sum(fresh_weights, axis=2).reshape(
        own_rows, heads
    )
    lowered = lax.reduce_precision(fresh_weights, 8, 7)
    numerator = jnp.sum(sums * jnp.repeat(scale, HEAD_DIM, axis=2), axis=0) + jnp.sum(
        jnp.repeat(lowered, HEAD_DIM, axis=3) * v_own, axis=2
    ).reshape(own_rows, cols)
    attended = (numerator / jnp.repeat(denominator, HEAD_DIM, axis=1)).astype(jnp.bfloat16)
    all_attended = lax.all_gather(attended, "seq", axis=0, tiled=True)[:row_count]
    projected = col_scatter(jnp.dot(all_attended, w_out, preferred_element_type=jnp.float32))
    half = projected.shape[0]
    wide_half = lax.dynamic_slice_in_dim(wide_in, lax.axis_index("col") * half, half, 0)
    residual = (wide_half + projected).astype(jnp.bfloat16)
    flat_rows = col_gather(lax.all_gather(residual, "seq", axis=1, tiled=True))

    chosen = route_ids.transpose(1, 0, 2).reshape(row_count, 2)
    expert_ids = jnp.arange(expert_count)
    w_pair = w_gate_up.reshape(experts_loc, width_all, 2 * ff_loc)
    pair_sum = jnp.einsum("rc,ecf->ref", flat_rows, w_pair, preferred_element_type=jnp.float32)
    wide_rows = flat_rows.astype(jnp.float32)
    square_sum = jnp.sum(wide_rows * wide_rows, axis=1)
    router_sum = jnp.dot(flat_rows, w_router, preferred_element_type=jnp.float32)
    inv_two = lax.rsqrt(square_sum / width_all + EPSILON)
    logits = router_sum * inv_two[:, None]
    first_pick = chosen[:, 0:1] == expert_ids[None, :]
    second_pick = chosen[:, 1:2] == expert_ids[None, :]
    first_share = jax.nn.sigmoid(
        jnp.sum(jnp.where(first_pick, logits, 0.0), axis=1)
        - jnp.sum(jnp.where(second_pick, logits, 0.0), axis=1)
    )
    gate_rows = jnp.where(first_pick, first_share[:, None], 0.0) + jnp.where(
        second_pick, 1.0 - first_share[:, None], 0.0
    )
    gate_local = lax.dynamic_slice_in_dim(gate_rows, expert_base, experts_loc, 1)
    pair_sum = pair_sum * inv_two[:, None, None]
    active = (jax.nn.silu(pair_sum[..., :ff_loc]) * pair_sum[..., ff_loc:]).astype(jnp.bfloat16)
    outputs = jnp.einsum("ref,efd->red", active, w_down, preferred_element_type=jnp.float32)
    weighted = jnp.sum(outputs * gate_local[:, :, None], axis=1)
    joined = col_scatter(weighted).astype(jnp.bfloat16)
    blocks = joined.reshape(half, shards, width_loc).transpose(1, 0, 2)
    mixture = jnp.sum(exchange(blocks).astype(jnp.float32), axis=0)
    layer_half = (residual.astype(jnp.float32) + mixture).astype(jnp.bfloat16)
    layer_rows = col_gather(layer_half).reshape(requests, steps, width_loc).transpose(1, 0, 2)
    return (layer_rows, all_pair[:, :, :cols], all_pair[:, :, cols:])


def places():
    s, c = lax.axis_index("seq"), lax.axis_index("col")
    z, y, x = s // 4, (s // 2) % 2, s % 2

    def to(dz, p):
        return ((z + dz) % 4) * 4 + ((y + p // 2) % 2) * 2 + (x + p % 2) % 2

    def source(dz, p):
        return ((z + 4 - dz) % 4) * 4 + ((y + p // 2) % 2) * 2 + (x + p % 2) % 2

    return s, c, to, source


OFFSETS = [(d, p) for p in range(4) for d in range(4)]
PEERS = OFFSETS[1:]


def send(src, dst, sems, slot, seq, col):
    return pltpu.make_async_remote_copy(
        src_ref=src,
        dst_ref=dst,
        send_sem=sems[0].at[slot],
        recv_sem=sems[1].at[slot],
        device_id=(seq, col),
        device_id_type=pl.DeviceIdType.MESH,
    )


NEAR = [(d, p) for d, p in PEERS if d == 0 or p == 0]


def greet(peers=NEAR):
    s, c, to, _ = places()
    barrier = pltpu.get_barrier_semaphore()
    for d, p in peers:
        pl.semaphore_signal(
            barrier, inc=1, device_id=(to(d, p), c), device_id_type=pl.DeviceIdType.MESH
        )
    pl.semaphore_signal(
        barrier, inc=1, device_id=(s, 1 - c), device_id_type=pl.DeviceIdType.MESH
    )
    pl.semaphore_wait(barrier, len(peers) + 1)


def gather_open(block, sems):
    s, c, to, _ = places()
    for d in range(1, 4):
        send(block(s), block(s), sems, d, to(d, 0), c).start()
    for p in range(1, 4):
        send(block(s), block(s), sems, 4 * p, to(0, p), c).start()


def gather_pass(block, sems):
    s, c, to, source = places()
    for d in range(1, 4):
        j = source(d, 0)
        send(block(j), block(j), sems, d, j, c).wait_recv()
        for p in range(1, 4):
            send(block(j), block(j), sems, 4 * p + d, to(0, p), c).start()


def gather_take(block, sems, d, p):
    _, c, _, source = places()
    j = source(d, p)
    send(block(j), block(j), sems, 4 * p + d, j, c).wait_recv()
    return j


def gather_close(block, sems):
    s, c, to, _ = places()
    for d, p in PEERS:
        send(block(s), block(s), sems, 4 * p + d, to(d, p), c).wait_send()


def share_open(block, sems, d, p):
    s, c, _, source = places()
    j = source(d, p)
    send(block(j), block(j), sems, 4 * p + d, s, 1 - c).start()


def share_take(block, other, sems, d, p):
    s, c, _, source = places()
    j = source(d, p)
    send(block(j), other(j), sems, 4 * p + d, s, 1 - c).wait_recv()
    return j


def share_close(block, sems):
    s, c, _, _ = places()
    for d, p in OFFSETS:
        send(block(s), block(s), sems, 4 * p + d, s, 1 - c).wait_send()


def halves(ref):
    c = lax.axis_index("col")
    mine, other = pl.multiple_of(c * 80, 16), pl.multiple_of((1 - c) * 80, 16)
    return (lambda j: ref.at[j, pl.ds(mine, 80), :]), (lambda j: ref.at[j, pl.ds(other, 80), :])


def dot(a, b, dims, precision=None):
    return lax.dot_general(
        a, b, (dims, ((), ())), precision=precision, preferred_element_type=jnp.float32
    )


NN = ((1,), (0,))
NT = ((1,), (1,))
TN = ((0,), (0,))


def iota(shape, axis):
    return lax.broadcasted_iota(jnp.int32, shape, axis)


def list_pages(table, lens, lists, pages, size):
    requests = table.shape[0]
    base = lax.axis_index("seq") * pages
    column = iota((1, table.shape[1]), 1)
    page = iota((pages, table.shape[1]), 0)

    def add(r, codes):
        left = lens[r] - column * size
        code = jnp.where(left > 0, r * 256 + jnp.minimum(left, size), 0)
        return codes + jnp.where(page == table[pl.ds(r, 1), :] - base, code, 0)

    codes = lax.fori_loop(0, requests, add, jnp.zeros(page.shape, jnp.int32))
    code = jnp.sum(codes.astype(jnp.float32), axis=1, keepdims=True)
    taken = jnp.where(code > 0.0, jnp.ones((1, 128), jnp.float32), 0.0)
    below = (iota((pages, pages), 1) < iota((pages, pages), 0)).astype(jnp.float32)
    before = dot(below.astype(jnp.bfloat16), taken.astype(jnp.bfloat16), NN)
    slot = iota((pages, 128), 1).astype(jnp.float32)
    placed = jnp.where(before == slot, taken, 0.0)
    at = jnp.sum(placed * iota((pages, 128), 0).astype(jnp.float32), axis=0, keepdims=True)
    packed = jnp.sum(placed * code, axis=0, keepdims=True).astype(jnp.int32)
    lists[...] = jnp.concatenate(
        [
            at.astype(jnp.int32),
            packed >> 8,
            packed & 255,
            jnp.sum(taken, axis=0, keepdims=True).astype(jnp.int32),
            jnp.zeros((4, 128), jnp.int32),
        ],
        axis=0,
    )


def project_kernel(
    pages, size, hid, order, w3, cos, sin, table, lens, q_all, kv_z, own_in, lists,
    hbuf, wsend, wrecv, stage, far, square, square_far,
    hs, hr, ss, sr, ws, wr, vs, vr, ts, tr, us, ur, ns, nr, qs, qr, ks, kr,
):
    s, c, to, source = places()
    steps, width, requests = hid.shape
    rows = steps * requests
    z, spot = s // 4, s % 4
    greet()
    mine, other = halves(hbuf)
    hsem, ssem, wsem, vsem, tsem, usem, nsem, qsem, ksem = (
        (hs, hr), (ss, sr), (ws, wr), (vs, vr), (ts, tr), (us, ur), (ns, nr), (qs, qr), (ks, kr)
    )
    j_at = iota((rows, requests), 0)
    same = (j_at >> 2) == order[...]
    placed = jnp.zeros((width, rows), jnp.float32)
    for n in range(steps):
        pick = jnp.where(same & ((j_at & 3) == n), 1.0, 0.0).astype(jnp.bfloat16)
        placed = placed + dot(hid[n], pick, NT)
    own = jnp.concatenate([placed, jnp.zeros((160 - width, rows), jnp.float32)], axis=0)
    own_in[...] = own.astype(jnp.bfloat16)
    here = pl.multiple_of(c * 80, 16)
    hbuf[spot, pl.ds(here, 80), :] = own_in[pl.ds(here, 80), :]
    sent = []

    def post(*what):
        copy = send(*what)
        copy.start()
        sent.append(copy)

    for p in range(1, 4):
        post(mine(spot), mine(spot), hsem, p, to(0, p), c)
    post(mine(spot), mine(spot), ssem, 0, s, 1 - c)
    low = iota((width, 128), 1) < HEAD_DIM
    low_v = iota((80, 128), 1) < HEAD_DIM
    for pair in range(8):
        at = slice(128 * pair, 128 * pair + 128)
        wq, wk, wv = [w3[i, :, at].astype(jnp.float32) for i in range(3)]
        va = wv[:80]
        vb = jnp.concatenate([wv[80:], jnp.zeros((160 - width, 128), jnp.float32)], axis=0)
        turn = functools.partial(pltpu.roll, shift=64, axis=1)
        wsend[2 * pair, :width] = jnp.where(low, wq, turn(wk)).astype(jnp.bfloat16)
        wsend[2 * pair + 1, :width] = jnp.where(low, turn(wq), wk).astype(jnp.bfloat16)
        wsend[2 * pair, width:] = jnp.where(low_v, va, turn(vb)).astype(jnp.bfloat16)
        wsend[2 * pair + 1, width:] = jnp.where(low_v, turn(va), vb).astype(jnp.bfloat16)
    upper, lower = pl.ds(0, width), pl.ds(width, 80)
    turns = (1, 2, 3, 0)
    for part, sems in ((upper, wsem), (lower, vsem)):
        for d in turns:
            for p in range(1, 4):
                j = to(d, p)
                post(wsend.at[j, part], wrecv.at[p, d, part], sems, 4 * p + d, to(0, p), c)
    list_pages(table, lens, lists, pages, size)
    for p in range(1, 4):
        k = to(0, p) % 4
        send(mine(k), mine(k), hsem, p, to(0, p), c).wait_recv()
        post(mine(k), mine(k), ssem, p, s, 1 - c)
    squares = jnp.zeros((1, rows), jnp.float32)
    for p in range(4):
        k = to(0, p) % 4
        send(mine(k), other(k), ssem, p, s, 1 - c).wait_recv()
        wide = hbuf[k].astype(jnp.float32)
        squares = squares + jnp.sum(wide * wide, axis=0, keepdims=True)
    for t in range(3):
        square[t : t + 1, :] = squares[:, 128 * t : 128 * t + 128]
    square[3:8, :] = jnp.zeros((5, 128), jnp.float32)
    for d in range(1, 4):
        post(square, square_far.at[d], nsem, d, to(d, 0), c)

    def weights(p, d, part, sems):
        if p == 0:
            return wsend[to(d, 0), part]
        send(wsend.at[s, part], wrecv.at[p, d, part], sems, 4 * p + d, to(0, p), c).wait_recv()
        return wrecv[p, d, part]

    head = pl.ds(0, HEAD_DIM)
    tail = pl.ds(HEAD_DIM, 2 * HEAD_DIM)
    for d in turns:
        qk = jnp.zeros((128, rows), jnp.float32)
        for p in range(4):
            qk = qk + dot(weights(p, d, upper, wsem), hbuf[to(0, p) % 4, :width], TN)
        if d:
            stage[d, :128] = qk.astype(jnp.bfloat16)
            post(stage.at[d, head], far.at[d, head], tsem, d, to(d, 0), c)
    for d in turns:
        v0 = jnp.zeros((128, rows), jnp.float32)
        v1 = jnp.zeros((128, rows), jnp.float32)
        for p in range(4):
            w = weights(p, d, lower, vsem)
            k = to(0, p) % 4
            v0 = v0 + dot(w, hbuf[k, :80], TN)
            v1 = v1 + dot(w[: width - 80], hbuf[k, 80:width], TN)
        v = v0[:HEAD_DIM] + v1[HEAD_DIM:]
        if d:
            stage[d, 128:] = v.astype(jnp.bfloat16)
            post(stage.at[d, tail], far.at[d, tail], usem, d, to(d, 0), c)
    for d in range(1, 4):
        send(square, square_far.at[d], nsem, d, source(d, 0), c).wait_recv()
        squares = squares + jnp.concatenate(
            [square_far[d, t : t + 1, :] for t in range(3)], axis=1
        )
    inv = lax.rsqrt(squares / (width * 16) + EPSILON)
    half = HEAD_DIM // 2

    def turned(part):
        a, b = part[:half], part[half:]
        return jnp.concatenate([a * cos[...] - b * sin[...], b * cos[...] + a * sin[...]], axis=0)

    query, key = qk[:HEAD_DIM], qk[HEAD_DIM:]
    for d in range(1, 4):
        send(stage.at[d, head], far.at[d, head], tsem, d, source(d, 0), c).wait_recv()
        query = query + far[d, :HEAD_DIM].astype(jnp.float32)
    q_all[s] = turned(query * inv).astype(jnp.bfloat16)
    gather_open(lambda j: q_all.at[j], qsem)
    for d in range(1, 4):
        send(stage.at[d, tail], far.at[d, tail], usem, d, source(d, 0), c).wait_recv()
        key = key + far[d, HEAD_DIM:128].astype(jnp.float32)
        v = v + far[d, 128:].astype(jnp.float32)
    kv_z[z, :HEAD_DIM] = turned(key * inv).astype(jnp.bfloat16)
    kv_z[z, HEAD_DIM:] = (v * inv).astype(jnp.bfloat16)
    gather_pass(lambda j: q_all.at[j], qsem)
    for d in range(1, 4):
        post(kv_z.at[z], kv_z.at[z], ksem, d, to(d, 0), c)
    for p in range(1, 4):
        for d in range(4):
            gather_take(lambda j: q_all.at[j], qsem, d, p)
    for d in range(1, 4):
        block = kv_z.at[(z + 4 - d) % 4]
        send(block, block, ksem, d, source(d, 0), c).wait_recv()
    for copy in sent:
        copy.wait_send()
    gather_close(lambda j: q_all.at[j], qsem)


def vmem():
    return pl.BlockSpec(memory_space=pltpu.VMEM)


def pair_sems(*counts):
    counts = counts or (16,)
    return [pltpu.SemaphoreType.DMA(counts), pltpu.SemaphoreType.DMA(counts)]


def project(hid, order, w3, cos, sin, table, lens, pages, size):
    steps, width, requests = hid.shape
    rows = steps * requests
    bf16 = jnp.bfloat16
    return pl.pallas_call(
        functools.partial(project_kernel, pages, size),
        out_shape=(
            jax.ShapeDtypeStruct((16, HEAD_DIM, rows), bf16),
            jax.ShapeDtypeStruct((4, 2 * HEAD_DIM, rows), bf16),
            jax.ShapeDtypeStruct((160, rows), bf16),
            jax.ShapeDtypeStruct((8, 128), jnp.int32),
        ),
        in_specs=[vmem()] * 6 + [pl.BlockSpec(memory_space=pltpu.SMEM)],
        out_specs=[vmem()] * 4,
        scratch_shapes=[
            pltpu.VMEM((4, 160, rows), bf16),
            pltpu.VMEM((16, width + 80, 128), bf16),
            pltpu.VMEM((4, 4, width + 80, 128), bf16),
            pltpu.VMEM((4, 3 * HEAD_DIM, rows), bf16),
            pltpu.VMEM((4, 3 * HEAD_DIM, rows), bf16),
            pltpu.VMEM((8, 128), jnp.float32),
            pltpu.VMEM((4, 8, 128), jnp.float32),
            *pair_sems(4), *pair_sems(4), *pair_sems(), *pair_sems(),
            *pair_sems(4), *pair_sems(4), *pair_sems(4), *pair_sems(), *pair_sems(4),
        ],
        compiler_params=pltpu.CompilerParams(
            collective_id=0, has_side_effects=True, vmem_limit_bytes=58 * MIB
        ),
        name="project",
    )(hid, order, w3, cos, sin, table, lens)


def attend_kernel(lists, q_all, *refs):
    keys, values = refs[:GROUP], refs[GROUP : 2 * GROUP]
    out, tops, flat, acc, peaks, totals, rowed = refs[2 * GROUP :]
    step = pl.program_id(0)
    rows = flat.shape[0]
    requests = rows // 4
    own = ((iota((16, 1024), 1) >> 6) & 3) == (iota((16, 1024), 0) >> 2)

    @pl.when(step == 0)
    def _():
        turned = q_all[...].reshape(16 * HEAD_DIM, rows).astype(jnp.float32)
        flat[...] = jnp.transpose(turned)

        @pl.loop(0, requests, unroll=4)
        def _(r):
            acc[r] = jnp.zeros((64, 256), jnp.float32)
            peaks[r] = jnp.full((64, 128), LOWEST, jnp.float32)
            totals[r] = jnp.zeros((64, 128), jnp.float32)

    @pl.when(step * GROUP < lists[3, 0])
    def _():
        token = iota((64, 128), 1)
        found = []
        for g in range(GROUP):
            at = step * GROUP + g
            r = lists[1, at]
            live = token < lists[2, at]
            lines = [flat[pl.ds(4 * r + n, 1), :] for n in range(4)]
            spread = jnp.where(own, jnp.concatenate(lines * 4, axis=0), 0.0).astype(jnp.bfloat16)
            scores = jnp.concatenate(
                [
                    dot(spread[:, 256 * i : 256 * i + 256], keys[g][0, :, 256 * i : 256 * i + 256], NT)
                    for i in range(4)
                ],
                axis=0,
            )
            scores = jnp.where(live, scores * (HEAD_DIM**-0.5), LOWEST)
            top = jnp.max(scores, axis=1, keepdims=True)
            weights = jnp.where(live, jnp.exp(scores - top), 0.0)
            total = jnp.sum(weights, axis=1, keepdims=True)
            lowered = weights.astype(jnp.bfloat16)
            mixed = jnp.concatenate(
                [
                    dot(lowered[16 * i : 16 * i + 16], values[g][0, :, 256 * i : 256 * i + 256], NN)
                    for i in range(4)
                ],
                axis=0,
            )
            found.append((r, top, total, mixed))
        for r, top, total, mixed in found:
            old = peaks[r]
            new = jnp.maximum(old, top)
            keep = jnp.exp(old - new)
            add = jnp.exp(top - new)
            peaks[r] = new
            totals[r] = totals[r] * keep + total * add
            acc[r] = acc[r] * jnp.concatenate([keep, keep], axis=1) + mixed * jnp.concatenate(
                [add, add], axis=1
            )

    @pl.when(step == pl.num_programs(0) - 1)
    def _():
        diagonal = iota((64, 128), 0) == iota((64, 128), 1)
        rowed[...] = jnp.zeros_like(rowed)

        @pl.loop(0, requests // 2, unroll=4)
        def _(pair):
            parts = []
            for e in range(2):
                r = 2 * pair + e
                whole = acc[r]
                lines = []
                for i in range(4):
                    x = jnp.where(own[:, :256], whole[16 * i : 16 * i + 16], 0.0)
                    y = x[:8] + x[8:]
                    lines.append(y[:4] + y[4:])
                parts.append(jnp.concatenate(lines, axis=1))
                rowed[0, pl.ds(r, 1), :] = jnp.sum(
                    jnp.where(diagonal, peaks[r], 0.0), axis=0, keepdims=True
                )
                rowed[1, pl.ds(r, 1), :] = jnp.sum(
                    jnp.where(diagonal, totals[r], 0.0), axis=0, keepdims=True
                )
            flat[pl.ds(pl.multiple_of(8 * pair, 8), 8), :] = jnp.concatenate(parts, axis=0)

        out[...] = (
            jnp.transpose(flat[...]).astype(jnp.bfloat16).reshape(16, HEAD_DIM, rows)
        )
        place = ((iota((128, rows), 1) >> 2) == iota((128, rows), 0)).astype(jnp.float32)
        match = (iota((64, rows), 0) & 3) == (iota((64, rows), 1) & 3)
        fold = ((iota((16, 64), 1) >> 2) == iota((16, 64), 0)).astype(jnp.float32)
        for k in range(2):
            spread = dot(jnp.transpose(rowed[k])[:64], place, NN, lax.Precision.HIGHEST)
            by_head = dot(fold, jnp.where(match, spread, 0.0), NN, lax.Precision.HIGHEST)
            for h in range(16):
                for t in range(3):
                    tops[h, 3 * k + t : 3 * k + t + 1, :] = by_head[
                        h : h + 1, 128 * t : 128 * t + 128
                    ]
        tops[:, 6:8, :] = jnp.zeros((16, 2, 128), jnp.float32)


def attend(lists, q_all, keys, values):
    pages, size, cols = keys.shape
    rows = q_all.shape[2]
    requests = rows // 4

    def page_spec(g):
        def index(i, lists):
            at = jnp.minimum(i * GROUP + g, jnp.maximum(lists[3, 0] - 1, 0))
            return (lists[0, at], 0, 0)

        return pl.BlockSpec((1, size, cols), index)

    specs = [page_spec(g) for g in range(GROUP)]
    return pl.pallas_call(
        attend_kernel,
        grid_spec=pltpu.PrefetchScalarGridSpec(
            num_scalar_prefetch=1,
            grid=(pages // GROUP,),
            in_specs=[pl.BlockSpec((16, HEAD_DIM, rows), lambda *_: (0, 0, 0))] + specs + specs,
            out_specs=[
                pl.BlockSpec((16, HEAD_DIM, rows), lambda *_: (0, 0, 0)),
                pl.BlockSpec((16, 8, 128), lambda *_: (0, 0, 0)),
            ],
            scratch_shapes=[
                pltpu.VMEM((rows, cols), jnp.float32),
                pltpu.VMEM((requests, 64, 256), jnp.float32),
                pltpu.VMEM((requests, 64, 128), jnp.float32),
                pltpu.VMEM((requests, 64, 128), jnp.float32),
                pltpu.VMEM((2, 128, 128), jnp.float32),
            ],
        ),
        out_shape=(
            jax.ShapeDtypeStruct((16, HEAD_DIM, rows), jnp.bfloat16),
            jax.ShapeDtypeStruct((16, 8, 128), jnp.float32),
        ),
        compiler_params=pltpu.CompilerParams(vmem_limit_bytes=48 * MIB),
        cost_estimate=pl.CostEstimate(
            flops=4 * pages * 64 * size * cols,
            bytes_accessed=4 * pages * size * cols,
            transcendentals=pages * 64 * size,
        ),
        name="attend",
    )(lists, q_all, *([keys] * GROUP), *([values] * GROUP))


def finish_kernel(
    parts, tops, q_all, kv_z, own_in, w_out, pair_hbm, down_hbm, router, routes, final,
    got, got_tops, far, far_tops, stage, stage_tops, attended, partial, theirs, mbuf,
    mid_all, pair, down, gates, active, mixed, swapped, summed, near_sums, sums, far_sums, kept,
    gs, gr, ts, tr, fs, fr, us, ur, as_, ar, ps, pr, ms, mr, ss, sr,
    cs, cr, hs, hr, ds, dr, ls, lr, pair_sem, down_sem,
):
    s, c, to, source = places()
    rows = kv_z.shape[2]
    fetches = [
        pltpu.make_async_copy(pair_hbm.at[e], pair.at[e], pair_sem.at[e])
        for e in range(pair.shape[0])
    ] + [pltpu.make_async_copy(down_hbm, down, down_sem)]
    greet()
    tsem, usem = (ts, tr), (us, ur)
    gsem, fsem, asem, psem, msem, ssem = [
        [(pair[0].at[t], pair[1].at[t]) for t in range(CHUNKS)]
        for pair in ((gs, gr), (fs, fr), (as_, ar), (ps, pr), (ms, mr), (ss, sr))
    ]
    order = (1, 2, 3, 0)
    lanes = [pl.ds(128 * t, 128) for t in range(CHUNKS)]
    spans = [slice(128 * t, 128 * t + 128) for t in range(CHUNKS)]
    every = slice(None)
    sent = []

    def post(*what):
        copy = send(*what)
        copy.start()
        sent.append(copy)

    for d in order:
        for p in range(1, 4):
            post(tops.at[to(d, p)], got_tops.at[p, d], tsem, 4 * p + d, to(0, p), c)
    for t in range(CHUNKS):
        for d in order:
            for p in range(1, 4):
                post(
                    parts.at[to(d, p), every, lanes[t]], got.at[p, d, every, lanes[t]],
                    gsem[t], 4 * p + d, to(0, p), c,
                )
    for fetch in fetches:
        fetch.start()
    q = q_all[s].astype(jnp.float32)
    k = kv_z[s // 4, :HEAD_DIM].astype(jnp.float32)
    v = kv_z[s // 4, HEAD_DIM:].astype(jnp.float32)
    moment = iota((1, rows), 1) & 3
    at = (routes.shape[2], rows)
    step_of = iota(at, 1) - 4 * iota(at, 0)
    picked = jnp.zeros((2, rows), jnp.float32)
    for n in range(routes.shape[0]):
        place = jnp.where(step_of == n, 1.0, 0.0).astype(jnp.bfloat16)
        named = routes[n].astype(jnp.float32).astype(jnp.bfloat16)
        picked = picked + dot(named, place, NN)
    fresh = []
    for back in range(4):
        moved = k if back == 0 else pltpu.roll(k, shift=back, axis=1)
        score = jnp.sum(q * moved, axis=0, keepdims=True) * (HEAD_DIM**-0.5)
        fresh.append(jnp.where(moment >= back, score, LOWEST))

    def lines(block):
        return [
            jnp.concatenate([block[3 * k + t : 3 * k + t + 1] for t in range(3)], axis=1)
            for k in range(2)
        ]

    def level(pairs, extra):
        best = functools.reduce(jnp.maximum, extra + [pair[0] for pair in pairs])
        scales = [jnp.exp(pair[0] - best) for pair in pairs]
        return best, sum(pair[1] * scale for pair, scale in zip(pairs, scales)), scales

    scales = {}
    for d in order:
        pairs = [lines(tops[to(d, 0)])]
        for p in range(1, 4):
            send(tops.at[s], got_tops.at[p, d], tsem, 4 * p + d, to(0, p), c).wait_recv()
            pairs.append(lines(got_tops[p, d]))
        best, bottom, scales[d] = level(pairs, [])
        if d:
            for k, row in enumerate((best, bottom)):
                for t in range(3):
                    stage_tops[d, 3 * k + t : 3 * k + t + 1, :] = row[:, 128 * t : 128 * t + 128]
            stage_tops[d, 6:8, :] = jnp.zeros((2, 128), jnp.float32)
            post(stage_tops.at[d], far_tops.at[d], usem, d, to(d, 0), c)
    near_pair = (best, bottom)

    def reduce_plane(t):
        for d in order:
            top = parts[to(d, 0), :, spans[t]].astype(jnp.float32) * scales[d][0][:, spans[t]]
            for p in range(1, 4):
                block = got.at[p, d, every, lanes[t]]
                send(block, block, gsem[t], 4 * p + d, to(0, p), c).wait_recv()
                top = top + got[p, d, :, spans[t]].astype(jnp.float32) * scales[d][p][:, spans[t]]
            if d:
                stage[d, :, spans[t]] = top.astype(jnp.bfloat16)
                post(
                    stage.at[d, every, lanes[t]], far.at[d, every, lanes[t]],
                    fsem[t], d, to(d, 0), c,
                )
        return top

    def attend_block(t):
        return lambda j: attended.at[j, every, lanes[t]]

    def reduce_far(t, top):
        top = top * far_scales[0][:, spans[t]] + added[:, spans[t]]
        for d in range(1, 4):
            block = far.at[d, every, lanes[t]]
            send(block, block, fsem[t], d, source(d, 0), c).wait_recv()
            top = top + far[d, :, spans[t]].astype(jnp.float32) * far_scales[d][:, spans[t]]
        attended[s, :, spans[t]] = (top / bottom[:, spans[t]]).astype(jnp.bfloat16)
        gather_open(attend_block(t), asem[t])

    held = [reduce_plane(0)]
    pairs = [near_pair]
    for d in range(1, 4):
        send(stage_tops.at[d], far_tops.at[d], usem, d, source(d, 0), c).wait_recv()
        pairs.append(lines(far_tops[d]))
    best, bottom, far_scales = level(pairs, fresh)
    added = jnp.zeros((HEAD_DIM, rows), jnp.float32)
    for back in range(4):
        weight = jnp.where(moment >= back, jnp.exp(fresh[back] - best), 0.0)
        bottom = bottom + weight
        moved = v if back == 0 else pltpu.roll(v, shift=back, axis=1)
        added = added + weight.astype(jnp.bfloat16).astype(jnp.float32) * moved

    width = w_out.shape[0]
    here, there = pl.multiple_of(c * 80, 16), pl.multiple_of((1 - c) * 80, 16)
    partial[width:] = jnp.zeros((160 - width, rows), jnp.float32)

    def half_block(t, start):
        return lambda j: mbuf.at[j, pl.ds(start, 80), lanes[t]]

    def swap_copy(t):
        return send(
            partial.at[pl.ds(there, 80), lanes[t]], theirs.at[every, lanes[t]],
            psem[t], 0, s, 1 - c,
        )

    def output(t):
        for p in range(1, 4):
            for d in range(4):
                gather_take(attend_block(t), asem[t], d, p)
        block = attended[:, :, spans[t]].reshape(16 * HEAD_DIM, 128)
        partial[:width, spans[t]] = dot(w_out[...], block, NN)
        swap_copy(t).start()

    def middle(t):
        swap_copy(t).wait_recv()
        mid = own_in[pl.ds(here, 80), spans[t]].astype(jnp.float32)
        mid = mid + partial[pl.ds(here, 80), spans[t]] + theirs[:, spans[t]]
        mbuf[s, pl.ds(here, 80), spans[t]] = mid.astype(jnp.bfloat16)
        gather_open(half_block(t, here), msem[t])
        share_open(half_block(t, here), ssem[t], 0, 0)

    def middle_pass(t):
        gather_pass(half_block(t, here), msem[t])
        for d in range(1, 4):
            share_open(half_block(t, here), ssem[t], d, 0)

    held.append(reduce_plane(1))
    reduce_far(0, held[0])
    held.append(reduce_plane(2))
    reduce_far(1, held[1])
    gather_pass(attend_block(0), asem[0])
    reduce_far(2, held[2])
    gather_pass(attend_block(1), asem[1])
    gather_pass(attend_block(2), asem[2])
    output(0)
    output(1)
    middle(0)
    output(2)
    middle(1)
    middle_pass(0)
    middle(2)
    middle_pass(1)
    middle_pass(2)
    for t in range(CHUNKS):
        for p in range(1, 4):
            for d in range(4):
                gather_take(half_block(t, here), msem[t], d, p)
                share_open(half_block(t, here), ssem[t], d, p)
    for t in range(CHUNKS):
        for d, p in OFFSETS:
            share_take(half_block(t, here), half_block(t, there), ssem[t], d, p)
    squares = jnp.zeros((1, rows), jnp.float32)
    for j in range(16):
        block = mbuf[j, :width]
        mid_all[width * j : width * j + width] = block
        wide = block.astype(jnp.float32)
        squares = squares + jnp.sum(wide * wide, axis=0, keepdims=True)

    inv = lax.rsqrt(squares / (width * 16) + EPSILON)
    logits = dot(router[...], mid_all[...], NN) * inv
    which = iota(logits.shape, 0).astype(jnp.float32)
    first, second = which == picked[0:1], which == picked[1:2]
    share = jax.nn.sigmoid(
        jnp.sum(jnp.where(first, logits, 0.0), axis=0, keepdims=True)
        - jnp.sum(jnp.where(second, logits, 0.0), axis=0, keepdims=True)
    )
    gates[...] = jnp.where(first, share, 0.0) + jnp.where(second, 1.0 - share, 0.0)
    count = pair.shape[0]

    def expert(e):
        pltpu.make_async_copy(pair_hbm.at[e], pair.at[e], pair_sem.at[e]).wait()
        mask = iota(gates.shape, 0) == c * count + e
        gate = jnp.sum(jnp.where(mask, gates[...], 0.0), axis=0, keepdims=True)
        front = dot(pair[e, 0], mid_all[...], NN) * inv
        back = dot(pair[e, 1], mid_all[...], NN) * inv
        value = (front / (1.0 + jnp.exp(-front))) * back
        active[e] = jnp.transpose(value * gate).astype(jnp.bfloat16)

    @pl.loop(0, count)
    def _(e):
        expert(e)

    fetches[-1].wait()
    csem, hsem, lsem = (cs, cr), (hs, hr), (ls, lr)
    step = 384
    z = s // 4
    here_seq = s % 4

    def mix(i):
        at = slice(step * i, step * i + step)
        part = dot(active[0], down[0, :, at], NN)
        for k in range(1, count):
            part = part + dot(active[k], down[k, :, at], NN)
        mixed[at] = jnp.transpose(part).astype(jnp.bfloat16)

    def trade(half):
        for j in range(8 * half, 8 * half + 8):
            at = width * j

            @pl.when(c == 0)
            def _(j=j, at=at):
                swapped[0, j, : width - 80] = mixed[at + 80 : at + width]

            @pl.when(c == 1)
            def _(j=j, at=at):
                swapped[0, j] = mixed[at : at + 80]

            send(swapped.at[0, j], swapped.at[1, j], csem, j, s, 1 - c).start()

    def spread(zt):
        for k in range(4):
            j = 4 * zt + k
            send(swapped.at[0, j], swapped.at[1, j], csem, j, s, 1 - c).wait_recv()
            at = width * j

            @pl.when(c == 0)
            def _(j=j, at=at):
                mine_part = mixed[at : at + 80].astype(jnp.float32)
                summed[j] = (mine_part + swapped[1, j].astype(jnp.float32)).astype(jnp.bfloat16)

            @pl.when(c == 1)
            def _(j=j, at=at):
                mine_part = mixed[at + 80 : at + width].astype(jnp.float32)
                rest = width - 80
                summed[j, :rest] = (mine_part + swapped[1, j, :rest].astype(jnp.float32)).astype(
                    jnp.bfloat16
                )

        for p in (3, 1, 2):
            near = to(0, p)
            send(
                summed.at[4 * zt + near % 4], near_sums.at[p, zt], hsem, 4 * p + zt, near, c
            ).start()

    for i in range(3):
        mix(i)
    trade(0)
    mix(3)
    spread(0)
    mix(4)
    spread(1)
    mix(5)
    trade(1)
    spread(2)
    spread(3)

    def far_copy(zt, zs):
        return pltpu.make_async_remote_copy(
            src_ref=sums.at[zt],
            dst_ref=far_sums.at[zs],
            send_sem=ds.at[zt],
            recv_sem=dr.at[zs],
            device_id=(4 * zt + here_seq, c),
            device_id_type=pl.DeviceIdType.MESH,
        )

    for zt in range(4):
        total = summed[4 * zt + here_seq].astype(jnp.float32)
        for p in range(1, 4):
            send(summed.at[0], near_sums.at[p, zt], hsem, 4 * p + zt, to(0, p), c).wait_recv()
            total = total + near_sums[p, zt].astype(jnp.float32)

        @pl.when(zt == z)
        def _(total=total):
            kept[...] = total

        @pl.when(zt != z)
        def _(total=total, zt=zt):
            sums[zt] = total.astype(jnp.bfloat16)
            far_copy(zt, z).start()

    total = kept[...] + mbuf[s, pl.ds(here, 80), :].astype(jnp.float32)
    for d in range(1, 4):
        zs = (z + d) % 4
        far_copy(zs, zs).wait_recv()
        total = total + far_sums[zs].astype(jnp.float32)
    final[pl.ds(here, 80), :] = total.astype(jnp.bfloat16)
    half, rest = final.at[pl.ds(here, 80), :], final.at[pl.ds(there, 80), :]
    last = send(half, half, lsem, 0, s, 1 - c)
    last.start()
    send(half, rest, lsem, 0, s, 1 - c).wait_recv()
    last.wait_send()
    for copy in sent:
        copy.wait_send()
    for t in range(CHUNKS):
        swap_copy(t).wait_send()
        gather_close(attend_block(t), asem[t])
        gather_close(half_block(t, here), msem[t])
        share_close(half_block(t, here), ssem[t])
    for j in range(16):
        send(swapped.at[0, j], swapped.at[1, j], csem, j, s, 1 - c).wait_send()
    for p in range(1, 4):
        for zt in range(4):
            send(summed.at[0], near_sums.at[p, zt], hsem, 4 * p + zt, to(0, p), c).wait_send()
    for d in range(1, 4):
        far_copy((z + d) % 4, z).wait_send()


def finish(parts, tops, q_all, kv_z, own_in, w_out, pair, down, router, routes):
    rows = kv_z.shape[2]
    width = w_out.shape[0]
    bf16, f32 = jnp.bfloat16, jnp.float32
    anywhere = pl.BlockSpec(memory_space=pl.ANY)
    return pl.pallas_call(
        finish_kernel,
        out_shape=jax.ShapeDtypeStruct((160, rows), bf16),
        in_specs=[vmem()] * 6 + [anywhere] * 2 + [vmem()] * 2,
        out_specs=vmem(),
        scratch_shapes=[
            pltpu.VMEM((4, 4, HEAD_DIM, rows), bf16),
            pltpu.VMEM((4, 4, 8, 128), f32),
            pltpu.VMEM((4, HEAD_DIM, rows), bf16),
            pltpu.VMEM((4, 8, 128), f32),
            pltpu.VMEM((4, HEAD_DIM, rows), bf16),
            pltpu.VMEM((4, 8, 128), f32),
            pltpu.VMEM((16, HEAD_DIM, rows), bf16),
            pltpu.VMEM((160, rows), f32),
            pltpu.VMEM((80, rows), f32),
            pltpu.VMEM((16, 160, rows), bf16),
            pltpu.VMEM((16 * width, rows), bf16),
            pltpu.VMEM(pair.shape, bf16),
            pltpu.VMEM(down.shape, bf16),
            pltpu.VMEM((router.shape[0], rows), f32),
            pltpu.VMEM((pair.shape[0], rows, pair.shape[2]), bf16),
            pltpu.VMEM((16 * width, rows), bf16),
            pltpu.VMEM((2, 16, 80, rows), bf16),
            pltpu.VMEM((16, 80, rows), bf16),
            pltpu.VMEM((4, 4, 80, rows), bf16),
            pltpu.VMEM((4, 80, rows), bf16),
            pltpu.VMEM((4, 80, rows), bf16),
            pltpu.VMEM((80, rows), f32),
            *pair_sems(CHUNKS, 16), *pair_sems(), *pair_sems(CHUNKS, 4), *pair_sems(4),
            *pair_sems(CHUNKS, 16), *pair_sems(CHUNKS, 1),
            *pair_sems(CHUNKS, 16), *pair_sems(CHUNKS, 16),
            *pair_sems(), *pair_sems(), *pair_sems(4), *pair_sems(1),
            pltpu.SemaphoreType.DMA((pair.shape[0],)), pltpu.SemaphoreType.DMA,
        ],
        compiler_params=pltpu.CompilerParams(
            collective_id=1, has_side_effects=True, vmem_limit_bytes=58 * MIB
        ),
        name="finish",
    )(parts, tops, q_all, kv_z, own_in, w_out, pair, down, router, routes)


def unpack_kernel(*refs):
    planes, (final, layer, keys, values, pick) = refs[:4], refs[4:]
    steps, requests, _ = keys.shape
    rows = planes[0].shape[2]

    @pl.when(pl.program_id(0) == 0)
    def _():
        width = layer.shape[1]
        at = (requests, rows)
        far = iota(at, 1) - 4 * iota(at, 0)
        for n in range(steps):
            pick[n * requests : n * requests + requests] = jnp.where(far == n, 1.0, 0.0).astype(
                jnp.bfloat16
            )
        done = dot(final[...], pick[...], NT).astype(jnp.bfloat16)
        for n in range(steps):
            layer[n] = done[:width, n * requests : n * requests + requests]

    mine = lax.axis_index("seq") % 4
    heads = []
    for k in range(4):
        offset = ((k // 2 + 2 - mine // 2) % 2) * 2 + (k + 2 - mine) % 2
        block = planes[0][0]
        for p in range(1, 4):
            block = jnp.where(offset == p, planes[p][0], block)
        heads.append(block)
    for first, result in ((0, keys), (HEAD_DIM, values)):
        four = jnp.concatenate([head[first : first + HEAD_DIM] for head in heads], axis=0)
        done = dot(pick[...], four, NT).astype(jnp.bfloat16)
        for n in range(steps):
            result[n] = done[n * requests : n * requests + requests]


def unpack(planes, final, steps, width):
    _, both, rows = planes[0].shape
    shape = (steps, rows // steps, 16 * HEAD_DIM)
    first = (steps, width, rows // steps)
    spec = pl.BlockSpec((*shape[:2], 4 * HEAD_DIM), lambda z: (0, 0, z))
    return pl.pallas_call(
        unpack_kernel,
        grid=(4,),
        in_specs=[pl.BlockSpec((1, both, rows), lambda z: (z, 0, 0))] * 4
        + [pl.BlockSpec(final.shape, lambda z: (0, 0))],
        out_specs=[pl.BlockSpec(first, lambda z: (0, 0, 0)), spec, spec],
        out_shape=(
            jax.ShapeDtypeStruct(first, jnp.bfloat16),
            jax.ShapeDtypeStruct(shape, jnp.bfloat16),
            jax.ShapeDtypeStruct(shape, jnp.bfloat16),
        ),
        cost_estimate=pl.CostEstimate(
            flops=4 * rows * rows * shape[2], bytes_accessed=8 * rows * shape[2], transcendentals=0
        ),
        scratch_shapes=[pltpu.VMEM((rows, rows), jnp.bfloat16)],
        name="unpack",
    )(*planes, final)


def plane_shift(block, p):
    pairs = [(i, i // 4 * 4 + (i % 4 ^ p)) for i in range(16)]
    return lax.ppermute(block, "seq", pairs)


def fast(
    hidden,
    key_cache,
    value_cache,
    page_table,
    cache_len,
    order,
    route_ids,
    w_qkv,
    w_out,
    w_router,
    w_gate_up,
    w_down,
):
    steps, requests, width = hidden.shape
    pages, size, cols = key_cache.shape
    rows = steps * requests
    half = HEAD_DIM // 2
    frequency = jnp.exp(
        -jnp.log(10000.0) * 2.0 * jnp.arange(half, dtype=jnp.float32) / HEAD_DIM
    )
    positions = (cache_len[:, None] + jnp.arange(steps)[None, :]).reshape(rows)
    angles = frequency[:, None] * positions.astype(jnp.float32)[None, :]
    q_all, kv_z, own_in, lists = project(
        hidden.transpose(0, 2, 1),
        order[None, :],
        w_qkv.transpose(1, 0, 2),
        jnp.cos(angles),
        jnp.sin(angles),
        page_table,
        cache_len,
        pages,
        size,
    )
    planes = [kv_z] + [plane_shift(kv_z, p) for p in range(1, 4)]
    parts, tops = attend(lists, q_all, key_cache, value_cache)
    final = finish(
        parts, tops, q_all, kv_z, own_in, w_out.T,
        w_gate_up.transpose(0, 2, 3, 1), w_down, w_router.T, route_ids.transpose(0, 2, 1),
    )
    layer, keys, values = unpack(planes, final, steps, width)
    return layer.transpose(0, 2, 1), keys, values


def solution(mesh):
    placed = (
        P(None, None, "seq"),
        P("seq", None, "col"),
        P("seq", None, "col"),
        P(),
        P(),
        P(),
        P(),
        P("seq", None, "col"),
        P("col", "seq"),
        P(),
        P("col", None, None, "seq"),
        P("col", "seq", None),
    )
    small = mesh.shape["seq"] == 16 and mesh.shape["col"] == 2
    return jax.shard_map(
        fast if small else local,
        mesh=mesh,
        in_specs=placed,
        out_specs=(P(None, None, "seq"), P(None, None, "col"), P(None, None, "col")),
        check_vma=False,
    )
```
